32 devices in a mesh: cols: 32 (over z, y, x, core).
Axes of the slice: x: 2, y: 2, z: 4, core: 2. Of those that a mesh axis runs over, the one named last changes fastest.
Arguments:
- mortality: bfloat16 [1024, 16384], P('cols'), may hold values from -18 to 18
Outputs:
- projected: bfloat16 [1024, 16384], P('cols')
The draws below stay inside these ranges and needn't reach their ends.
All inputs are finite; a program needn't handle non-finite values.
Results may differ from the reference program's by a relative error of at most 0.02.
Values may be sent and summed in bfloat16 or wider, within the bound.
No kernel may reach another device: no remote copies, remote signals or barrier semaphores. Data moves between devices by JAX's collectives and lax.ppermute only.
A program may use at most 64 MiB of HBM per device.

```python
import math
import jax
import jax.numpy as jnp
from jax import lax

M = 16384
RANK = 128
COLS_DEV = 32
LEVELS = 5
SWEEPS = 3
COLUMNS = 1024
TREES = 1


def draw_mortality(key, part):
    subkeys = jax.random.split(key, 5)
    classes_all = 4 * RANK
    row_scale = jnp.exp(jax.random.uniform(subkeys[0], (M,), jnp.float32, math.log(0.5), math.log(2.0)))
    block_scale = jnp.exp(jax.random.uniform(subkeys[1], (COLUMNS // COLS_DEV, M), jnp.float32, math.log(0.7), math.log(1.4)))
    class_scale = jnp.exp(jax.random.uniform(subkeys[2], (classes_all,), jnp.float32, math.log(0.5), math.log(1.5)))
    loading = jnp.clip(jax.random.normal(subkeys[3], (COLUMNS, classes_all), jnp.float32), -4.0, 4.0)
    jitter_part = 0.3 * jnp.clip(jax.random.normal(subkeys[4], (COLUMNS, M), jnp.float32), -4.0, 4.0)
    strong = jnp.tile(loading * class_scale, (1, M // classes_all))
    scales = jnp.repeat(block_scale, COLS_DEV, axis=0) * row_scale
    return (strong * scales + jitter_part).astype(jnp.bfloat16)


def setup_inputs(seed: int = 0) -> dict:
    key_list = jax.random.split(jax.random.key(seed), 2)
    return {
        "mortality": draw_mortality(jax.random.fold_in(key_list[1], 71), 0),
    }


precise = lax.Precision.HIGHEST

def leading_space(gram_full):
    frame_now = jnp.eye(gram_full.shape[0], RANK, dtype=jnp.float32)
    for sweep_index in range(SWEEPS):
        imaged = jnp.dot(gram_full, frame_now, precision=precise)
        inner_gram = jnp.dot(imaged.T, imaged, precision=precise)
        factor = jnp.linalg.cholesky(inner_gram)
        frame_now = jax.scipy.linalg.solve_triangular(factor, imaged.T, lower=True).T
    return frame_now

def merge_step(stacked):
    gram_full = jnp.dot(stacked.astype(jnp.float32), stacked.T.astype(jnp.float32), preferred_element_type=jnp.float32)
    frame_low = leading_space(gram_full).astype(jnp.bfloat16)
    joined = jnp.dot(frame_low.T.astype(jnp.float32), stacked.astype(jnp.float32), preferred_element_type=jnp.float32).astype(jnp.bfloat16)
    return (joined, gram_full, frame_low)

def tree_project(blocks):
    node_rows = blocks.reshape(2 ** LEVELS, COLS_DEV, M)
    gram_full = None
    frame_low = None
    for level_index in range(LEVELS):
        paired = node_rows.reshape(node_rows.shape[0] // 2, 2 * node_rows.shape[1], M)
        if paired.shape[1] > RANK:
            node_rows, gram_full, frame_low = jax.vmap(merge_step)(paired)
        else:
            node_rows = paired
    top_node = node_rows[0]
    widened = frame_low[0].astype(jnp.float32)
    inner_gram = jnp.dot(widened.T, jnp.dot(gram_full[0], widened, precision=precise), precision=precise)
    factor = jnp.linalg.cholesky(inner_gram)
    coeffs = jnp.dot(top_node.astype(jnp.float32), blocks.T.astype(jnp.float32), preferred_element_type=jnp.float32)
    solved = jax.scipy.linalg.cho_solve((factor, True), coeffs).astype(jnp.bfloat16)
    return jnp.dot(solved.T.astype(jnp.float32), top_node.astype(jnp.float32), preferred_element_type=jnp.float32).astype(jnp.bfloat16)

def reference(mortality):
    span_cols = 2 ** LEVELS * COLS_DEV

    def one_tree(tree_index, result_all):
        start_row = (tree_index * span_cols).astype(jnp.int32)
        blocks = lax.dynamic_slice_in_dim(mortality, start_row, span_cols, 0)
        return lax.dynamic_update_slice_in_dim(result_all, tree_project(blocks), start_row, 0)
    return lax.fori_loop(0, TREES, one_tree, jnp.zeros_like(mortality))
```

```python
import jax
import jax.numpy as jnp
from jax import lax
from jax.experimental import pallas as pl
from jax.experimental.pallas import tpu as pltpu
from jax.sharding import PartitionSpec as P

RANK = 128
LEVELS = 5
SWEEPS = 3
PLANE = 8
PLANES = 2**LEVELS // PLANE
TILE = 8
PANEL = 64
PIVOT_SHARE = 2e-5

precise = lax.Precision.HIGHEST
f32 = jnp.float32
bf16 = jnp.bfloat16


def iota2(shape, dim):
    return lax.broadcasted_iota(jnp.int32, shape, dim)


def dot(a, b, ca, cb, precision=precise):
    return lax.dot_general(a, b, (((ca,), (cb,)), ((), ())), precision=precision, preferred_element_type=f32)


def dot_low(a, b, ca, cb):
    return dot(a, b, ca, cb, None)


def lanes_of(x, k):
    return jnp.broadcast_to(x[:, k : k + 1], x.shape)


def rows_of(x, s):
    return jnp.broadcast_to(x[s : s + 1, :], x.shape)


def eliminate(tiles, first):
    lane = iota2((TILE, RANK), 1)
    sub = iota2((TILE, RANK), 0)
    count = len(tiles)
    for t in range(count):
        g = TILE * (first + t)
        cols = {i: [lanes_of(tiles[i], g + j) for j in range(TILE)] for i in range(t, count)}
        for k in range(TILE):
            here = lane == g + k
            pivot_row = [rows_of(cols[t][j], k) if j >= k else None for j in range(TILE)]
            inv = 1.0 / pivot_row[k]
            row = jnp.where(here, 1.0, rows_of(tiles[t], k)) * inv
            scaled = [pivot_row[j] * inv if j > k else None for j in range(TILE)]
            for i in range(t, count):
                col = cols[i][k]
                if i == t:
                    col = jnp.where(sub > k, col, 0.0)
                    kept = jnp.where(here & (sub > k), 0.0, tiles[i])
                else:
                    kept = jnp.where(here, 0.0, tiles[i])
                tiles[i] = kept - col * row
                for j in range(k + 1, TILE):
                    cols[i][j] = cols[i][j] - col * scaled[j]
    return tiles


def inverse_factor(s):
    rest = s
    done = []
    for p in range(RANK // PANEL):
        lo, hi = p * PANEL, (p + 1) * PANEL
        head = rest[:PANEL, :]
        tiles = [head[TILE * t : TILE * t + TILE, :] for t in range(PANEL // TILE)]
        panel = jnp.concatenate(eliminate(tiles, lo // TILE), 0)
        done.append(panel)
        if hi == RANK:
            break
        r = iota2((PANEL, RANK), 0) + lo
        c = iota2((PANEL, RANK), 1)
        pivots = jnp.sum(jnp.where(r == c, panel, 0.0), 1, keepdims=True)
        rows = jnp.where(r == c, 1.0, jnp.where((c > r) & (c < hi), 0.0, panel))
        tail = rest[PANEL:, :]
        c = iota2(tail.shape, 1)
        tail = jnp.where((c >= lo) & (c < hi), 0.0, tail)
        rest = tail - dot(panel * (1.0 / pivots), rows, 0, 0)[hi:, :]
    x = jnp.concatenate(done, 0)
    r = iota2((RANK, RANK), 0)
    c = iota2((RANK, RANK), 1)
    pivots = jnp.sum(jnp.where(r == c, x, 0.0), 1, keepdims=True)
    unit = jnp.where(r > c, x, jnp.where(r == c, 1.0, 0.0))
    return unit * lax.rsqrt(pivots), pivots


def on_diagonal(x):
    return jnp.where(iota2(x.shape, 0) == iota2(x.shape, 1), x, 0.0)


def leading_space(gram, frame_ref):
    gram = gram * (1.0 / jnp.max(on_diagonal(gram), keepdims=True))
    imaged = gram[:, :RANK]
    for step in range(SWEEPS - 1):
        imaged = dot(gram, imaged, 1, 0)
    inner = dot(imaged, imaged, 0, 0)
    factor, pivots = inverse_factor(inner)
    frame_ref[...] = dot(imaged, factor, 1, 1)
    share = jnp.min(pivots / jnp.sum(on_diagonal(inner), 1, keepdims=True))

    @pl.when(jnp.logical_not(share > PIVOT_SHARE))
    def _():
        frame_ref[...] = jnp.where(iota2(imaged.shape, 0) == iota2(imaged.shape, 1), 1.0, 0.0)

        def sweep(step, carry):
            again = dot(gram, frame_ref[...], 1, 0)
            again_factor, _ = inverse_factor(dot(again, again, 0, 0))
            frame_ref[...] = dot(again, again_factor, 1, 1)
            return carry

        lax.fori_loop(0, SWEEPS, sweep, 0)

    return frame_ref[...].astype(bf16)


def place(pos_ref):
    pos = pos_ref[0]
    return pos % 2, pos // PLANE % PLANES


def split(blocks, core, mine_ref, theirs_ref):
    half = mine_ref.shape[1]
    for b, block in enumerate(blocks):
        low, high = block[:half, :], block[half:, :]
        mine_ref[b] = jnp.where(core == 1, high, low)
        theirs_ref[b] = jnp.where(core == 1, low, high)


def joined(mine_ref, other_ref, core, b):
    mine, other = mine_ref[b], other_ref[b]
    low = jnp.where(core == 1, other, mine)
    high = jnp.where(core == 1, mine, other)
    return jnp.concatenate([low, high], 0)


def chunk(z, m, width):
    return pl.ds(pl.multiple_of((z ^ m) * width, width), width)


def gram_kernel(pos_ref, rows_ref, mine_ref, theirs_ref):
    core, _ = place(pos_ref)
    rows = rows_ref[...]
    gram = dot_low(rows, rows, 1, 1)
    split([gram[:RANK, :RANK], gram[RANK:, :RANK], gram[RANK:, RANK:]], core, mine_ref, theirs_ref)


def square(a, b, d):
    return jnp.concatenate([jnp.concatenate([a, b.T], 1), jnp.concatenate([b, d], 1)], 0)


def node_kernel(pos_ref, mine_ref, other_ref, rows_ref, *refs):
    nodes, diag_ref, frame_ref = refs[:PLANES], refs[PLANES], refs[PLANES + 1]
    core, z = place(pos_ref)
    gram = square(*[joined(mine_ref, other_ref, core, b) for b in range(3)])
    frame_low = leading_space(gram, frame_ref)
    width = nodes[0].shape[1]
    for m in range(PLANES):
        nodes[m][...] = dot_low(frame_low, rows_ref[:, chunk(z, m, width)], 0, 0).astype(bf16)
    wide = frame_low.astype(f32)
    diag_ref[...] = dot(wide, dot(gram, wide, 1, 0), 0, 0).astype(diag_ref.dtype)


PAIRS = [(i, j) for i in range(PLANES) for j in range(i + 1, PLANES)]


def cross_kernel(pos_ref, *refs):
    nodes, (mine_ref, theirs_ref, all_ref) = refs[:PLANES], refs[PLANES:]
    core, z = place(pos_ref)
    for m in range(PLANES):
        all_ref[z ^ m] = nodes[m][...]
    split([dot_low(all_ref[j], all_ref[i], 1, 1) for i, j in PAIRS], core, mine_ref, theirs_ref)


def top_kernel(pos_ref, mine_ref, other_ref, *refs):
    nodes, diags = refs[:PLANES], refs[PLANES : 2 * PLANES]
    top_ref, inner_ref, frame_a, frame_b, all_ref, diag_ref = refs[2 * PLANES :]
    core, z = place(pos_ref)
    for m in range(PLANES):
        all_ref[z ^ m] = nodes[m][...]
        diag_ref[z ^ m] = diags[m][...].astype(f32)
    cross = {pair: joined(mine_ref, other_ref, core, b) for b, pair in enumerate(PAIRS)}
    gram_a = square(diag_ref[0], cross[0, 1], diag_ref[1])
    gram_b = square(diag_ref[2], cross[2, 3], diag_ref[3])
    low_a = leading_space(gram_a, frame_a)
    low_b = leading_space(gram_b, frame_b)
    wide_a, wide_b = low_a.astype(f32), low_b.astype(f32)
    between = jnp.concatenate(
        [
            jnp.concatenate([cross[0, 2], cross[1, 2]], 1),
            jnp.concatenate([cross[0, 3], cross[1, 3]], 1),
        ],
        0,
    )
    gram = square(
        dot(wide_a, dot(gram_a, wide_a, 1, 0), 0, 0),
        dot(wide_b, dot(between, wide_a, 1, 0), 0, 0),
        dot(wide_b, dot(gram_b, wide_b, 1, 0), 0, 0),
    )
    low = leading_space(gram, frame_a)
    node_a = dot_low(low_a, jnp.concatenate([all_ref[0], all_ref[1]], 0), 0, 0).astype(bf16)
    node_b = dot_low(low_b, jnp.concatenate([all_ref[2], all_ref[3]], 0), 0, 0).astype(bf16)
    top_ref[...] = dot_low(low, jnp.concatenate([node_a, node_b], 0), 0, 0).astype(bf16)
    wide = low.astype(f32)
    inner_ref[...] = dot(wide, dot(gram, wide, 1, 0), 0, 0)


def factor_kernel(inner_ref, factor_ref):
    factor_ref[...] = inverse_factor(inner_ref[...])[0]


def coeffs_kernel(pos_ref, rows_ref, *refs):
    tops, (mine_ref, theirs_ref) = refs[:PLANES], refs[PLANES:]
    core, z = place(pos_ref)
    width = tops[0].shape[1]
    total = None
    for m in range(PLANES):
        part = dot_low(rows_ref[:, chunk(z, m, width)], tops[m][...], 1, 1)
        total = part if total is None else total + part
    split([total], core, mine_ref, theirs_ref)


def project_kernel(pos_ref, mine_ref, other_ref, factor_ref, *refs):
    tops, out_ref = refs[:PLANES], refs[PLANES]
    core, z = place(pos_ref)
    coeffs = joined(mine_ref, other_ref, core, 0)
    factor = factor_ref[...]
    solved = dot(dot(coeffs, factor, 1, 1), factor, 1, 0).astype(bf16)
    width = tops[0].shape[1]
    for m in range(PLANES):
        out_ref[:, chunk(z, m, width)] = dot_low(solved, tops[m][...], 1, 0).astype(bf16)


smem = pl.BlockSpec(memory_space=pltpu.SMEM)
vmem = pl.BlockSpec(memory_space=pltpu.VMEM)


def kernel(fn, outs, *args, scratch=(), scalar=True):
    single = not isinstance(outs, (list, tuple))
    shapes = [outs] if single else list(outs)
    res = pl.pallas_call(
        fn,
        out_shape=[jax.ShapeDtypeStruct(s, d) for s, d in shapes] if not single else None,
        in_specs=[smem if scalar and i == 0 else vmem for i in range(len(args))],
        out_specs=[vmem for _ in shapes],
        scratch_shapes=list(scratch),
        compiler_params=pltpu.CompilerParams(vmem_limit_bytes=40 * 2**20),
        name=fn.__name__,
    )(*args)
    return res


def body(mortality):
    count = lax.axis_size("cols")
    pos = lax.axis_index("cols").astype(jnp.int32).reshape(1)
    plane_groups = [list(range(s, s + PLANE)) for s in range(0, count, PLANE)]

    def swap(x, apart):
        return lax.ppermute(x, "cols", [(i, i ^ apart) for i in range(count)])

    def plane_sum(mine, theirs):
        half = mine + swap(theirs, 1)
        return (half + swap(half, 2)) + (swap(half, 4) + swap(half, 6))

    def low_sum(x, unit):
        x = x.astype(bf16)
        parts = [x] + [swap(x, unit * m) for m in range(1, 4)]
        parts = [p.astype(f32) for p in parts]
        return (parts[0] + parts[1]) + (parts[2] + parts[3])

    rows = lax.all_to_all(mortality, "cols", 1, 0, tiled=True, axis_index_groups=plane_groups)
    height, width = rows.shape
    part = width // PLANES
    half = RANK // 2

    mine, theirs = kernel(gram_kernel, [((3, half, RANK), f32)] * 2, pos, rows)
    mine = plane_sum(mine, theirs)
    other = swap(mine, 1)
    *nodes, diag = kernel(
        node_kernel,
        [((RANK, part), bf16)] * PLANES + [((RANK, RANK), bf16)],
        pos, mine, other, rows,
        scratch=[pltpu.VMEM((2 * RANK, RANK), f32)],
    )
    nodes = [nodes[0]] + [swap(nodes[m], PLANE * m) for m in range(1, PLANES)]
    diags = [diag] + [swap(diag, PLANE * m) for m in range(1, PLANES)]

    mine, theirs = kernel(
        cross_kernel,
        [((len(PAIRS), half, RANK), f32)] * 2,
        pos, *nodes,
        scratch=[pltpu.VMEM((PLANES, RANK, part), bf16)],
    )
    mine = low_sum(low_sum(mine + swap(theirs, 1), 2), PLANE)
    other = swap(mine, 1)
    top, inner = kernel(
        top_kernel,
        [((RANK, part), bf16), ((RANK, RANK), f32)],
        pos, mine, other, *nodes, *diags,
        scratch=[pltpu.VMEM((2 * RANK, RANK), f32)] * 2
        + [pltpu.VMEM((PLANES, RANK, part), bf16), pltpu.VMEM((PLANES, RANK, RANK), f32)],
    )
    tops = [top] + [swap(top, PLANE * m) for m in range(1, PLANES)]
    (factor,) = kernel(factor_kernel, [((RANK, RANK), f32)], inner, scalar=False)

    mine, theirs = kernel(coeffs_kernel, [((1, height // 2, RANK), f32)] * 2, pos, rows, *tops)
    mine = plane_sum(mine, theirs)
    other = swap(mine, 1)
    (out,) = kernel(project_kernel, [((height, width), bf16)], pos, mine, other, factor, *tops)
    return lax.all_to_all(out, "cols", 0, 1, tiled=True, axis_index_groups=plane_groups)


def solution(mesh):
    in_specs = (P("cols", None),)
    out_specs = P("cols", None)
    return jax.shard_map(body, mesh=mesh, in_specs=in_specs, out_specs=out_specs, check_vma=False)
```

```python
import jax
import jax.numpy as jnp
from jax import lax
from jax.experimental import pallas as pl
from jax.experimental.pallas import tpu as pltpu
from jax.sharding import PartitionSpec as P

RANK = 128
LEVELS = 5
SWEEPS = 3
PLANE = 8
PLANES = 2**LEVELS // PLANE
TILE = 8
PANEL = 64
PIVOT_SHARE = 2e-5

precise = lax.Precision.HIGHEST
f32 = jnp.float32
bf16 = jnp.bfloat16


def iota2(shape, dim):
    return lax.broadcasted_iota(jnp.int32, shape, dim)


def dot(a, b, ca, cb, precision=precise):
    return lax.dot_general(a, b, (((ca,), (cb,)), ((), ())), precision=precision, preferred_element_type=f32)


def dot_low(a, b, ca, cb):
    return dot(a, b, ca, cb, None)


def lanes_of(x, k):
    return jnp.broadcast_to(x[:, k : k + 1], x.shape)


def rows_of(x, s):
    return jnp.broadcast_to(x[s : s + 1, :], x.shape)


def eliminate(tiles, first):
    lane = iota2((TILE, RANK), 1)
    sub = iota2((TILE, RANK), 0)
    count = len(tiles)
    for t in range(count):
        g = TILE * (first + t)
        cols = {i: [lanes_of(tiles[i], g + j) for j in range(TILE)] for i in range(t, count)}
        for k in range(TILE):
            here = lane == g + k
            pivot_row = [rows_of(cols[t][j], k) if j >= k else None for j in range(TILE)]
            inv = 1.0 / pivot_row[k]
            row = jnp.where(here, 1.0, rows_of(tiles[t], k)) * inv
            scaled = [pivot_row[j] * inv if j > k else None for j in range(TILE)]
            for i in range(t, count):
                col = cols[i][k]
                if i == t:
                    col = jnp.where(sub > k, col, 0.0)
                    kept = jnp.where(here & (sub > k), 0.0, tiles[i])
                else:
                    kept = jnp.where(here, 0.0, tiles[i])
                tiles[i] = kept - col * row
                for j in range(k + 1, TILE):
                    cols[i][j] = cols[i][j] - col * scaled[j]
    return tiles


def inverse_factor(s):
    rest = s
    done = []
    for p in range(RANK // PANEL):
        lo, hi = p * PANEL, (p + 1) * PANEL
        head = rest[:PANEL, :]
        tiles = [head[TILE * t : TILE * t + TILE, :] for t in range(PANEL // TILE)]
        panel = jnp.concatenate(eliminate(tiles, lo // TILE), 0)
        done.append(panel)
        if hi == RANK:
            break
        r = iota2((PANEL, RANK), 0) + lo
        c = iota2((PANEL, RANK), 1)
        pivots = jnp.sum(jnp.where(r == c, panel, 0.0), 1, keepdims=True)
        rows = jnp.where(r == c, 1.0, jnp.where((c > r) & (c < hi), 0.0, panel))
        tail = rest[PANEL:, :]
        c = iota2(tail.shape, 1)
        tail = jnp.where((c >= lo) & (c < hi), 0.0, tail)
        rest = tail - dot(panel * (1.0 / pivots), rows, 0, 0)[hi:, :]
    x = jnp.concatenate(done, 0)
    r = iota2((RANK, RANK), 0)
    c = iota2((RANK, RANK), 1)
    pivots = jnp.sum(jnp.where(r == c, x, 0.0), 1, keepdims=True)
    unit = jnp.where(r > c, x, jnp.where(r == c, 1.0, 0.0))
    return unit * lax.rsqrt(pivots), pivots


def on_diagonal(x):
    return jnp.where(iota2(x.shape, 0) == iota2(x.shape, 1), x, 0.0)


def leading_space(gram, frame_ref):
    gram = gram * (1.0 / jnp.max(on_diagonal(gram), keepdims=True))
    imaged = gram[:, :RANK]
    for step in range(SWEEPS - 1):
        imaged = dot(gram, imaged, 1, 0)
    inner = dot(imaged, imaged, 0, 0)
    factor, pivots = inverse_factor(inner)
    frame_ref[...] = dot(imaged, factor, 1, 1)
    share = jnp.min(pivots / jnp.sum(on_diagonal(inner), 1, keepdims=True))

    @pl.when(jnp.logical_not(share > PIVOT_SHARE))
    def _():
        frame_ref[...] = jnp.where(iota2(imaged.shape, 0) == iota2(imaged.shape, 1), 1.0, 0.0)

        def sweep(step, carry):
            again = dot(gram, frame_ref[...], 1, 0)
            again_factor, _ = inverse_factor(dot(again, again, 0, 0))
            frame_ref[...] = dot(again, again_factor, 1, 1)
            return carry

        lax.fori_loop(0, SWEEPS, sweep, 0)

    return frame_ref[...].astype(bf16)


def place(pos_ref):
    pos = pos_ref[0]
    return pos % 2, pos // PLANE % PLANES


def split(blocks, core, mine_ref, theirs_ref):
    half = mine_ref.shape[1]
    for b, block in enumerate(blocks):
        low, high = block[:half, :], block[half:, :]
        mine_ref[b] = jnp.where(core == 1, high, low)
        theirs_ref[b] = jnp.where(core == 1, low, high)


def joined(mine_ref, other_ref, core, b):
    mine, other = mine_ref[b], other_ref[b]
    low = jnp.where(core == 1, other, mine)
    high = jnp.where(core == 1, mine, other)
    return jnp.concatenate([low, high], 0)


def chunk(z, m, width):
    return pl.ds(pl.multiple_of((z ^ m) * width, width), width)


def member(pos_ref):
    return pos_ref[0] % PLANE


def parts_kernel(pos_ref, x_ref, *refs):
    width = refs[0].shape[1]
    for m in range(PLANE):
        refs[m][...] = x_ref[:, chunk(member(pos_ref), m, width)]


def gram_kernel(pos_ref, *refs):
    parts, (rows_ref, mine_ref, theirs_ref) = refs[:PLANE], refs[PLANE:]
    core, _ = place(pos_ref)
    height = parts[0].shape[0]
    for m in range(PLANE):
        rows_ref[chunk(member(pos_ref), m, height), :] = parts[m][...]
    rows = rows_ref[...]
    gram = dot_low(rows, rows, 1, 1)
    split([gram[:RANK, :RANK], gram[RANK:, :RANK], gram[RANK:, RANK:]], core, mine_ref, theirs_ref)


def square(a, b, d):
    return jnp.concatenate([jnp.concatenate([a, b.T], 1), jnp.concatenate([b, d], 1)], 0)


def node_kernel(pos_ref, mine_ref, other_ref, rows_ref, *refs):
    nodes, diag_ref, frame_ref = refs[:PLANES], refs[PLANES], refs[PLANES + 1]
    core, z = place(pos_ref)
    gram = square(*[joined(mine_ref, other_ref, core, b) for b in range(3)])
    frame_low = leading_space(gram, frame_ref)
    width = nodes[0].shape[1]
    for m in range(PLANES):
        nodes[m][...] = dot_low(frame_low, rows_ref[:, chunk(z, m, width)], 0, 0).astype(bf16)
    wide = frame_low.astype(f32)
    diag = dot(wide, dot(gram, wide, 1, 0), 0, 0)
    half = diag_ref.shape[1]
    diag_ref[0] = jnp.where(core == 1, diag[half:, :], diag[:half, :]).astype(diag_ref.dtype)


PAIRS = [(i, j) for i in range(PLANES) for j in range(i + 1, PLANES)]


def cross_kernel(pos_ref, *refs):
    nodes, (mine_ref, theirs_ref, all_ref) = refs[:PLANES], refs[PLANES:]
    core, z = place(pos_ref)
    for m in range(PLANES):
        all_ref[z ^ m] = nodes[m][...]
    split([dot_low(all_ref[j], all_ref[i], 1, 1) for i, j in PAIRS], core, mine_ref, theirs_ref)


def top_kernel(pos_ref, mine_ref, other_ref, *refs):
    nodes, (top_ref, inner_ref, frame_a, frame_b, all_ref, diag_ref) = refs[:PLANES], refs[PLANES:]
    core, z = place(pos_ref)
    for m in range(PLANES):
        all_ref[z ^ m] = nodes[m][...]
        diag_ref[z ^ m] = joined(mine_ref, other_ref, core, len(PAIRS) + m)
    cross = {pair: joined(mine_ref, other_ref, core, b) for b, pair in enumerate(PAIRS)}
    gram_a = square(diag_ref[0], cross[0, 1], diag_ref[1])
    gram_b = square(diag_ref[2], cross[2, 3], diag_ref[3])
    low_a = leading_space(gram_a, frame_a)
    low_b = leading_space(gram_b, frame_b)
    wide_a, wide_b = low_a.astype(f32), low_b.astype(f32)
    between = jnp.concatenate(
        [
            jnp.concatenate([cross[0, 2], cross[1, 2]], 1),
            jnp.concatenate([cross[0, 3], cross[1, 3]], 1),
        ],
        0,
    )
    gram = square(
        dot(wide_a, dot(gram_a, wide_a, 1, 0), 0, 0),
        dot(wide_b, dot(between, wide_a, 1, 0), 0, 0),
        dot(wide_b, dot(gram_b, wide_b, 1, 0), 0, 0),
    )
    low = leading_space(gram, frame_a)
    node_a = dot_low(low_a, jnp.concatenate([all_ref[0], all_ref[1]], 0), 0, 0).astype(bf16)
    node_b = dot_low(low_b, jnp.concatenate([all_ref[2], all_ref[3]], 0), 0, 0).astype(bf16)
    top_ref[...] = dot_low(low, jnp.concatenate([node_a, node_b], 0), 0, 0).astype(bf16)
    wide = low.astype(f32)
    inner_ref[...] = dot(wide, dot(gram, wide, 1, 0), 0, 0)


def factor_kernel(inner_ref, factor_ref):
    factor_ref[...] = inverse_factor(inner_ref[...])[0]


def coeffs_kernel(pos_ref, rows_ref, factor_ref, *refs):
    tops, (mine_ref, theirs_ref) = refs[:PLANES], refs[PLANES:]
    core, z = place(pos_ref)
    width = tops[0].shape[1]
    total = None
    for m in range(PLANES):
        part = dot_low(rows_ref[:, chunk(z, m, width)], tops[m][...], 1, 1)
        total = part if total is None else total + part
    split([dot(total, factor_ref[...], 1, 1)], core, mine_ref, theirs_ref)


def project_kernel(pos_ref, mine_ref, other_ref, factor_ref, *refs):
    tops, outs, solved_ref = refs[:PLANES], refs[PLANES:-1], refs[-1]
    core, z = place(pos_ref)
    height, width = outs[0].shape[0], tops[0].shape[1]
    solved_ref[...] = dot(joined(mine_ref, other_ref, core, 0), factor_ref[...], 1, 0)
    solved = [solved_ref[chunk(member(pos_ref), m, height), :] for m in range(PLANE)]
    solved = jnp.concatenate(solved, 0).astype(bf16)
    for c in range(PLANES):
        made = dot_low(solved, tops[c][...], 1, 0).astype(bf16)
        for m in range(PLANE):
            outs[m][:, chunk(z, c, width)] = made[m * height : (m + 1) * height, :]


smem = pl.BlockSpec(memory_space=pltpu.SMEM)
vmem = pl.BlockSpec(memory_space=pltpu.VMEM)


def kernel(fn, outs, *args, scratch=(), scalar=True):
    single = not isinstance(outs, (list, tuple))
    shapes = [outs] if single else list(outs)
    res = pl.pallas_call(
        fn,
        out_shape=[jax.ShapeDtypeStruct(s, d) for s, d in shapes] if not single else None,
        in_specs=[smem if scalar and i == 0 else vmem for i in range(len(args))],
        out_specs=[vmem for _ in shapes],
        scratch_shapes=list(scratch),
        compiler_params=pltpu.CompilerParams(vmem_limit_bytes=40 * 2**20),
        name=fn.__name__,
    )(*args)
    return res


def body(mortality):
    count = lax.axis_size("cols")
    pos = lax.axis_index("cols").astype(jnp.int32).reshape(1)

    def swap(x, apart):
        return lax.ppermute(x, "cols", [(i, i ^ apart) for i in range(count)])

    def swap_all(parts, unit):
        return [parts[0]] + [swap(parts[m], unit * m) for m in range(1, len(parts))]

    def sum4(parts):
        parts = [p.astype(f32) for p in parts]
        return (parts[0] + parts[1]) + (parts[2] + parts[3])

    block, total = mortality.shape
    height, width = block * PLANE, total // PLANE
    part = width // PLANES
    half = RANK // 2

    parts = kernel(parts_kernel, [((block, width), bf16)] * PLANE, pos, mortality)
    parts = swap_all(parts, 1)
    rows, mine, theirs = kernel(
        gram_kernel, [((height, width), bf16)] + [((3, half, RANK), f32)] * 2, pos, *parts
    )
    mine = sum4(swap_all([mine + swap(theirs, 1)] * 4, 2))
    *nodes, diag = kernel(
        node_kernel,
        [((RANK, part), bf16)] * PLANES + [((1, half, RANK), bf16)],
        pos, mine, swap(mine, 1), rows,
        scratch=[pltpu.VMEM((2 * RANK, RANK), f32)],
    )
    nodes = swap_all(nodes, PLANE)

    mine, theirs = kernel(
        cross_kernel,
        [((len(PAIRS), half, RANK), f32)] * 2,
        pos, *nodes,
        scratch=[pltpu.VMEM((PLANES, RANK, part), bf16)],
    )
    mine = sum4(swap_all([(mine + swap(theirs, 1)).astype(bf16)] * 4, 2))
    both = swap_all([jnp.concatenate([mine.astype(bf16), diag], 0)] * PLANES, PLANE)
    mine = jnp.concatenate([sum4([x[: len(PAIRS)] for x in both])] + [x[len(PAIRS) :].astype(f32) for x in both], 0)
    top, inner = kernel(
        top_kernel,
        [((RANK, part), bf16), ((RANK, RANK), f32)],
        pos, mine, swap(mine, 1), *nodes,
        scratch=[pltpu.VMEM((2 * RANK, RANK), f32)] * 2
        + [pltpu.VMEM((PLANES, RANK, part), bf16), pltpu.VMEM((PLANES, RANK, RANK), f32)],
    )
    tops = swap_all([top] * PLANES, PLANE)
    (factor,) = kernel(factor_kernel, [((RANK, RANK), f32)], inner, scalar=False)

    mine, theirs = kernel(coeffs_kernel, [((1, height // 2, RANK), f32)] * 2, pos, rows, factor, *tops)
    mine = sum4(swap_all([mine + swap(theirs, 1)] * 4, 2))
    outs = kernel(
        project_kernel,
        [((block, width), bf16)] * PLANE,
        pos, mine, swap(mine, 1), factor, *tops,
        scratch=[pltpu.VMEM((height, RANK), f32)],
    )
    result = jnp.zeros_like(mortality)
    for m, x in enumerate(swap_all(outs, 1)):
        result = lax.dynamic_update_slice(result, x, (0, (pos[0] % PLANE ^ m) * width))
    return result


def solution(mesh):
    in_specs = (P("cols", None),)
    out_specs = P("cols", None)
    return jax.shard_map(body, mesh=mesh, in_specs=in_specs, out_specs=out_specs, check_vma=False)
```

```python
import jax
import jax.numpy as jnp
from jax import lax
from jax.experimental import pallas as pl
from jax.experimental.pallas import tpu as pltpu
from jax.sharding import PartitionSpec as P

RANK = 128
LEVELS = 5
SWEEPS = 3
PLANE = 8
PLANES = 2**LEVELS // PLANE
TILE = 8
PANEL = 64
PIVOT_SHARE = 2e-5

precise = lax.Precision.HIGHEST
f32 = jnp.float32
bf16 = jnp.bfloat16


def iota2(shape, dim):
    return lax.broadcasted_iota(jnp.int32, shape, dim)


def dot(a, b, ca, cb, precision=precise):
    return lax.dot_general(a, b, (((ca,), (cb,)), ((), ())), precision=precision, preferred_element_type=f32)


def dot_low(a, b, ca, cb):
    return dot(a, b, ca, cb, None)


def lanes_of(x, k):
    return jnp.broadcast_to(x[:, k : k + 1], x.shape)


def rows_of(x, s):
    return jnp.broadcast_to(x[s : s + 1, :], x.shape)


def eliminate(sets, first, ahead):
    lane = iota2((TILE, RANK), 1)
    sub = iota2((TILE, RANK), 0)
    count = len(sets[0])
    early = [None] * len(sets)
    for t in range(count):
        g = TILE * (first + t)
        spread, coming = [], []
        for n, tiles in enumerate(sets):
            cols = {} if early[n] is None else {t: early[n]}
            for i in range(t + len(cols), count):
                cols[i] = [lanes_of(tiles[i], g + j) for j in range(TILE)]
            spread.append(cols)
            near = (t, t + 1) if ahead and t + 1 < count else ()
            coming.append({i: [lanes_of(tiles[i], g + TILE + j) for j in range(TILE)] for i in near})
        for k in range(TILE):
            here = lane == g + k
            for tiles, cols, look in zip(sets, spread, coming):
                pivot_row = [rows_of(cols[t][j], k) if j >= k else None for j in range(TILE)]
                inv = 1.0 / pivot_row[k]
                scaled = [pivot_row[j] * inv if j > k else None for j in range(TILE)]
                row = jnp.where(here, 1.0, rows_of(tiles[t], k)) * inv
                look_row = [rows_of(x, k) * inv for x in look[t]] if look else None
                for i in range(t, count):
                    col = cols[i][k]
                    if i == t:
                        col = jnp.where(sub > k, col, 0.0)
                        kept = jnp.where(here & (sub > k), 0.0, tiles[i])
                    else:
                        kept = jnp.where(here, 0.0, tiles[i])
                    for j in range(k + 1, TILE):
                        cols[i][j] = cols[i][j] - col * scaled[j]
                    tiles[i] = kept - col * row
                    if i in look:
                        look[i] = [x - col * y for x, y in zip(look[i], look_row)]
        early = [look.get(t + 1) for look in coming]
    return sets


def inverse_factors(matrices):
    alone = len(matrices) == 1
    size = PANEL if alone else PANEL // 2
    rests = list(matrices)
    done = [[] for _ in rests]
    for lo in range(0, RANK, size):
        hi = lo + size
        sets = [[rest[TILE * t : TILE * t + TILE, :] for t in range(size // TILE)] for rest in rests]
        for n, tiles in enumerate(eliminate(sets, lo // TILE, alone)):
            panel = jnp.concatenate(tiles, 0)
            done[n].append(panel)
            if hi == RANK:
                continue
            r = iota2((size, RANK), 0) + lo
            c = iota2((size, RANK), 1)
            pivots = jnp.sum(jnp.where(r == c, panel, 0.0), 1, keepdims=True)
            rows = jnp.where(r == c, 1.0, jnp.where((c > r) & (c < hi), 0.0, panel))
            tail = rests[n][size:, :]
            c = iota2(tail.shape, 1)
            tail = jnp.where((c >= lo) & (c < hi), 0.0, tail)
            rests[n] = tail - dot(panel * (1.0 / pivots), rows, 0, 0)[hi:, :]
    results = []
    for panels in done:
        x = jnp.concatenate(panels, 0)
        r = iota2((RANK, RANK), 0)
        c = iota2((RANK, RANK), 1)
        pivots = jnp.sum(jnp.where(r == c, x, 0.0), 1, keepdims=True)
        unit = jnp.where(r > c, x, jnp.where(r == c, 1.0, 0.0))
        results.append((unit * lax.rsqrt(pivots), pivots))
    return results


def diagonal_of(x):
    return jnp.sum(jnp.where(iota2(x.shape, 0) == iota2(x.shape, 1), x, 0.0), 1, keepdims=True)


def leading_spaces(grams, work):
    for gram, (gram_ref, imaged_ref, _) in zip(grams, work):
        largest = jnp.maximum(diagonal_of(gram[:RANK, :RANK]), diagonal_of(gram[RANK:, RANK:]))
        gram = gram * (1.0 / jnp.max(largest, keepdims=True))
        gram_ref[...] = gram
        imaged = gram[:, :RANK]
        for step in range(SWEEPS - 1):
            imaged = dot(gram, imaged, 1, 0)
        imaged_ref[...] = imaged

    def attempt(step):
        inners = [dot(imaged_ref[...], imaged_ref[...], 0, 0) for _, imaged_ref, _ in work]
        share = None
        for inner, (factor, pivots), (_, imaged_ref, frame_ref) in zip(inners, inverse_factors(inners), work):
            frame_ref[...] = dot(imaged_ref[...], factor, 1, 1)
            ratio = pivots / diagonal_of(inner)
            share = ratio if share is None else jnp.where(ratio < share, ratio, share)
        good = jnp.logical_and(step == 0, jnp.min(share) > PIVOT_SHARE)
        last = jnp.logical_or(good, step == SWEEPS)

        @pl.when(jnp.logical_not(last))
        def _():
            for gram_ref, imaged_ref, frame_ref in work:
                first = gram_ref[:, :RANK]
                imaged_ref[...] = jnp.where(step == 0, first, dot(gram_ref[...], frame_ref[...], 1, 0))

        return jnp.where(last, SWEEPS + 1, step + 1)

    lax.while_loop(lambda step: step <= SWEEPS, attempt, jnp.int32(0))
    return [frame_ref[...].astype(bf16) for _, _, frame_ref in work]


work_shapes = [pltpu.VMEM((2 * RANK, 2 * RANK), f32)] + [pltpu.VMEM((2 * RANK, RANK), f32)] * 2


def place(pos_ref):
    pos = pos_ref[0]
    return pos % 2, pos // PLANE % PLANES


def split(blocks, core, mine_ref, theirs_ref):
    half = mine_ref.shape[1]
    for b, block in enumerate(blocks):
        low, high = block[:half, :], block[half:, :]
        mine_ref[b] = jnp.where(core == 1, high, low)
        theirs_ref[b] = jnp.where(core == 1, low, high)


def joined(mine_ref, other_ref, core, b):
    mine, other = mine_ref[b], other_ref[b]
    low = jnp.where(core == 1, other, mine)
    high = jnp.where(core == 1, mine, other)
    return jnp.concatenate([low, high], 0)


def chunk(z, m, width):
    return pl.ds(pl.multiple_of((z ^ m) * width, width), width)


def member(pos_ref):
    return pos_ref[0] % PLANE


def parts_kernel(pos_ref, x_ref, *refs):
    width = refs[0].shape[1]
    for m in range(PLANE):
        refs[m][...] = x_ref[:, chunk(member(pos_ref), m, width)]


def gram_kernel(pos_ref, *refs):
    parts, (rows_ref, mine_ref, theirs_ref) = refs[:PLANE], refs[PLANE:]
    core, _ = place(pos_ref)
    height = parts[0].shape[0]
    for m in range(PLANE):
        rows_ref[chunk(member(pos_ref), m, height), :] = parts[m][...]
    rows = rows_ref[...]
    gram = dot_low(rows, rows, 1, 1)
    split([gram[:RANK, :RANK], gram[RANK:, :RANK], gram[RANK:, RANK:]], core, mine_ref, theirs_ref)


def square(a, b, d):
    return jnp.concatenate([jnp.concatenate([a, b.T], 1), jnp.concatenate([b, d], 1)], 0)


def plane_gram(mine_ref, other_ref, core):
    return square(*[joined(mine_ref, other_ref, core, b) for b in range(3)])


def node_kernel(pos_ref, mine_ref, other_ref, rows_ref, *refs):
    nodes, low_ref, work = refs[:PLANES], refs[PLANES], refs[PLANES + 1 :]
    core, z = place(pos_ref)
    (low,) = leading_spaces([plane_gram(mine_ref, other_ref, core)], [work])
    low_ref[...] = low
    width = nodes[0].shape[1]
    for m in range(PLANES):
        nodes[m][...] = dot_low(low, rows_ref[:, chunk(z, m, width)], 0, 0).astype(bf16)


def reduced(gram, low):
    wide = low.astype(f32)
    return dot(wide, dot(gram, wide, 1, 0), 0, 0)


def diag_kernel(pos_ref, mine_ref, other_ref, low_ref, diag_ref):
    core, _ = place(pos_ref)
    diag = reduced(plane_gram(mine_ref, other_ref, core), low_ref[...])
    half = diag_ref.shape[1]
    diag_ref[0] = jnp.where(core == 1, diag[half:, :], diag[:half, :]).astype(diag_ref.dtype)


PAIRS = [(i, j) for i in range(PLANES) for j in range(i + 1, PLANES)]


def cross_kernel(pos_ref, *refs):
    nodes, (mine_ref, theirs_ref, all_ref) = refs[:PLANES], refs[PLANES:]
    core, z = place(pos_ref)
    for m in range(PLANES):
        all_ref[z ^ m] = nodes[m][...]
    split([dot_low(all_ref[j], all_ref[i], 1, 1) for i, j in PAIRS], core, mine_ref, theirs_ref)


def top_kernel(pos_ref, mine_ref, other_ref, *refs):
    nodes, (top_ref, gram_ref, low_ref), refs = refs[:PLANES], refs[PLANES : PLANES + 3], refs[PLANES + 3 :]
    all_ref, diag_ref, work = refs[0], refs[1], [refs[2:5], refs[5:8]]
    core, z = place(pos_ref)
    for m in range(PLANES):
        all_ref[z ^ m] = nodes[m][...]
        diag_ref[z ^ m] = joined(mine_ref, other_ref, core, len(PAIRS) + m)
    cross = {pair: joined(mine_ref, other_ref, core, b) for b, pair in enumerate(PAIRS)}
    gram_a = square(diag_ref[0], cross[0, 1], diag_ref[1])
    gram_b = square(diag_ref[2], cross[2, 3], diag_ref[3])
    low_a, low_b = leading_spaces([gram_a, gram_b], work)
    between = jnp.concatenate(
        [
            jnp.concatenate([cross[0, 2], cross[1, 2]], 1),
            jnp.concatenate([cross[0, 3], cross[1, 3]], 1),
        ],
        0,
    )
    gram = square(
        reduced(gram_a, low_a),
        dot(low_b.astype(f32), dot(between, low_a.astype(f32), 1, 0), 0, 0),
        reduced(gram_b, low_b),
    )
    gram_ref[...] = gram
    (low,) = leading_spaces([gram], work[:1])
    low_ref[...] = low
    node_a = dot_low(low_a, jnp.concatenate([all_ref[0], all_ref[1]], 0), 0, 0).astype(bf16)
    node_b = dot_low(low_b, jnp.concatenate([all_ref[2], all_ref[3]], 0), 0, 0).astype(bf16)
    top_ref[...] = dot_low(low, jnp.concatenate([node_a, node_b], 0), 0, 0).astype(bf16)


def factor_kernel(gram_ref, low_ref, factor_ref):
    factor_ref[...] = inverse_factors([reduced(gram_ref[...], low_ref[...])])[0][0]


def coeffs_kernel(pos_ref, rows_ref, factor_ref, *refs):
    tops, (mine_ref, theirs_ref) = refs[:PLANES], refs[PLANES:]
    core, z = place(pos_ref)
    width = tops[0].shape[1]
    total = None
    for m in range(PLANES):
        part = dot_low(rows_ref[:, chunk(z, m, width)], tops[m][...], 1, 1)
        total = part if total is None else total + part
    split([dot(total, factor_ref[...], 1, 1)], core, mine_ref, theirs_ref)


def project_kernel(pos_ref, mine_ref, other_ref, factor_ref, *refs):
    tops, outs, solved_ref = refs[:PLANES], refs[PLANES:-1], refs[-1]
    core, z = place(pos_ref)
    height, width = outs[0].shape[0], tops[0].shape[1]
    solved_ref[...] = dot(joined(mine_ref, other_ref, core, 0), factor_ref[...], 1, 0)
    solved = [solved_ref[chunk(member(pos_ref), m, height), :] for m in range(PLANE)]
    solved = jnp.concatenate(solved, 0).astype(bf16)
    for c in range(PLANES):
        made = dot_low(solved, tops[c][...], 1, 0).astype(bf16)
        for m in range(PLANE):
            outs[m][:, chunk(z, c, width)] = made[m * height : (m + 1) * height, :]


def whole_kernel(pos_ref, *refs):
    parts, out_ref = refs[:PLANE], refs[PLANE]
    width = parts[0].shape[1]
    for m in range(PLANE):
        out_ref[:, chunk(member(pos_ref), m, width)] = parts[m][...]


smem = pl.BlockSpec(memory_space=pltpu.SMEM)
vmem = pl.BlockSpec(memory_space=pltpu.VMEM)


def kernel(fn, outs, *args, scratch=(), scalar=True):
    single = not isinstance(outs, (list, tuple))
    shapes = [outs] if single else list(outs)
    res = pl.pallas_call(
        fn,
        out_shape=[jax.ShapeDtypeStruct(s, d) for s, d in shapes] if not single else None,
        in_specs=[smem if scalar and i == 0 else vmem for i in range(len(args))],
        out_specs=[vmem for _ in shapes],
        scratch_shapes=list(scratch),
        compiler_params=pltpu.CompilerParams(vmem_limit_bytes=40 * 2**20),
        name=fn.__name__,
    )(*args)
    return res


def body(mortality):
    count = lax.axis_size("cols")
    pos = lax.axis_index("cols").astype(jnp.int32).reshape(1)

    def swap(x, apart):
        return lax.ppermute(x, "cols", [(i, i ^ apart) for i in range(count)])

    def swap_all(parts, unit):
        return [parts[0]] + [swap(parts[m], unit * m) for m in range(1, len(parts))]

    def sum4(parts):
        parts = [p.astype(f32) for p in parts]
        return (parts[0] + parts[1]) + (parts[2] + parts[3])

    def plane_sum(mine, theirs):
        return sum4(swap_all([(mine + swap(theirs, 1)).astype(bf16)] * 4, 2))

    block, total = mortality.shape
    height, width = block * PLANE, total // PLANE
    part = width // PLANES
    half = RANK // 2

    parts = kernel(parts_kernel, [((block, width), bf16)] * PLANE, pos, mortality)
    parts = swap_all(parts, 1)
    rows, mine, theirs = kernel(
        gram_kernel, [((height, width), bf16)] + [((3, half, RANK), f32)] * 2, pos, *parts
    )
    mine = plane_sum(mine, theirs)
    other = swap(mine, 1)
    *nodes, low = kernel(
        node_kernel,
        [((RANK, part), bf16)] * PLANES + [((2 * RANK, RANK), bf16)],
        pos, mine, other, rows,
        scratch=work_shapes,
    )
    nodes = swap_all(nodes, PLANE)
    (diag,) = kernel(diag_kernel, [((1, half, RANK), bf16)], pos, mine, other, low)

    mine, theirs = kernel(
        cross_kernel,
        [((len(PAIRS), half, RANK), f32)] * 2,
        pos, *nodes,
        scratch=[pltpu.VMEM((PLANES, RANK, part), bf16)],
    )
    mine = plane_sum(mine, theirs)
    both = swap_all([jnp.concatenate([mine.astype(bf16), diag], 0)] * PLANES, PLANE)
    mine = jnp.concatenate([sum4([x[: len(PAIRS)] for x in both])] + [x[len(PAIRS) :].astype(f32) for x in both], 0)
    top, gram, low = kernel(
        top_kernel,
        [((RANK, part), bf16), ((2 * RANK, 2 * RANK), f32), ((2 * RANK, RANK), bf16)],
        pos, mine, swap(mine, 1), *nodes,
        scratch=[pltpu.VMEM((PLANES, RANK, part), bf16), pltpu.VMEM((PLANES, RANK, RANK), f32)] + work_shapes * 2,
    )
    tops = swap_all([top] * PLANES, PLANE)
    (factor,) = kernel(factor_kernel, [((RANK, RANK), f32)], gram, low, scalar=False)

    mine, theirs = kernel(coeffs_kernel, [((1, height // 2, RANK), f32)] * 2, pos, rows, factor, *tops)
    mine = plane_sum(mine, theirs)
    outs = kernel(
        project_kernel,
        [((block, width), bf16)] * PLANE,
        pos, mine, swap(mine, 1), factor, *tops,
        scratch=[pltpu.VMEM((height, RANK), f32)],
    )
    (result,) = kernel(whole_kernel, [((block, total), bf16)], pos, *swap_all(outs, 1))
    return result


def solution(mesh):
    in_specs = (P("cols", None),)
    out_specs = P("cols", None)
    return jax.shard_map(body, mesh=mesh, in_specs=in_specs, out_specs=out_specs, check_vma=False)
```

```python
import jax
import jax.numpy as jnp
from jax import lax
from jax.experimental import pallas as pl
from jax.experimental.pallas import tpu as pltpu
from jax.sharding import PartitionSpec as P

RANK = 128
LEVELS = 5
SWEEPS = 3
PLANE = 8
PLANES = 2**LEVELS // PLANE
TILE = 8
PANEL = 64
PIVOT_SHARE = 2e-5

precise = lax.Precision.HIGHEST
f32 = jnp.float32
bf16 = jnp.bfloat16


def iota2(shape, dim):
    return lax.broadcasted_iota(jnp.int32, shape, dim)


def dot(a, b, ca, cb, precision=precise):
    return lax.dot_general(a, b, (((ca,), (cb,)), ((), ())), precision=precision, preferred_element_type=f32)


def dot_low(a, b, ca, cb):
    return dot(a, b, ca, cb, None)


def lanes_of(x, k):
    return jnp.broadcast_to(x[:, k : k + 1], x.shape)


def rows_of(x, s):
    return jnp.broadcast_to(x[s : s + 1, :], x.shape)


def eliminate(sets, first, ahead):
    lane = iota2((TILE, RANK), 1)
    sub = iota2((TILE, RANK), 0)
    count = len(sets[0])
    early = [None] * len(sets)
    for t in range(count):
        g = TILE * (first + t)
        spread, coming = [], []
        for n, tiles in enumerate(sets):
            cols = {} if early[n] is None else {t: early[n]}
            for i in range(t + len(cols), count):
                cols[i] = [lanes_of(tiles[i], g + j) for j in range(TILE)]
            spread.append(cols)
            near = (t, t + 1) if ahead and t + 1 < count else ()
            coming.append({i: [lanes_of(tiles[i], g + TILE + j) for j in range(TILE)] for i in near})
        for k in range(TILE):
            here = lane == g + k
            for tiles, cols, look in zip(sets, spread, coming):
                pivot_row = [rows_of(cols[t][j], k) if j >= k else None for j in range(TILE)]
                inv = 1.0 / pivot_row[k]
                scaled = [pivot_row[j] * inv if j > k else None for j in range(TILE)]
                row = jnp.where(here, 1.0, rows_of(tiles[t], k)) * inv
                look_row = [rows_of(x, k) * inv for x in look[t]] if look else None
                for i in range(t, count):
                    col = cols[i][k]
                    if i == t:
                        col = jnp.where(sub > k, col, 0.0)
                        kept = jnp.where(here & (sub > k), 0.0, tiles[i])
                    else:
                        kept = jnp.where(here, 0.0, tiles[i])
                    for j in range(k + 1, TILE):
                        cols[i][j] = cols[i][j] - col * scaled[j]
                    tiles[i] = kept - col * row
                    if i in look:
                        look[i] = [x - col * y for x, y in zip(look[i], look_row)]
        early = [look.get(t + 1) for look in coming]
    return sets


def inverse_factors(matrices):
    alone = len(matrices) == 1
    size = PANEL if alone else PANEL // 2
    rests = list(matrices)
    done = [[] for _ in rests]
    for lo in range(0, RANK, size):
        hi = lo + size
        sets = [[rest[TILE * t : TILE * t + TILE, :] for t in range(size // TILE)] for rest in rests]
        for n, tiles in enumerate(eliminate(sets, lo // TILE, alone)):
            panel = jnp.concatenate(tiles, 0)
            done[n].append(panel)
            if hi == RANK:
                continue
            r = iota2((size, RANK), 0) + lo
            c = iota2((size, RANK), 1)
            pivots = jnp.sum(jnp.where(r == c, panel, 0.0), 1, keepdims=True)
            rows = jnp.where(r == c, 1.0, jnp.where((c > r) & (c < hi), 0.0, panel))
            tail = rests[n][size:, :]
            c = iota2(tail.shape, 1)
            tail = jnp.where((c >= lo) & (c < hi), 0.0, tail)
            rests[n] = tail - dot(panel * (1.0 / pivots), rows, 0, 0)[hi:, :]
    results = []
    for panels in done:
        x = jnp.concatenate(panels, 0)
        r = iota2((RANK, RANK), 0)
        c = iota2((RANK, RANK), 1)
        pivots = jnp.sum(jnp.where(r == c, x, 0.0), 1, keepdims=True)
        unit = jnp.where(r > c, x, jnp.where(r == c, 1.0, 0.0))
        results.append((unit * lax.rsqrt(pivots), pivots))
    return results


def diagonal_of(x):
    return jnp.sum(jnp.where(iota2(x.shape, 0) == iota2(x.shape, 1), x, 0.0), 1, keepdims=True)


def leading_spaces(grams, work):
    for gram, (gram_ref, imaged_ref, _) in zip(grams, work):
        largest = jnp.maximum(diagonal_of(gram[:RANK, :RANK]), diagonal_of(gram[RANK:, RANK:]))
        gram = gram * (1.0 / jnp.max(largest, keepdims=True))
        gram_ref[...] = gram
        imaged = gram[:, :RANK]
        for step in range(SWEEPS - 1):
            imaged = dot(gram, imaged, 1, 0)
        imaged_ref[...] = imaged

    def attempt(step):
        inners = [dot(imaged_ref[...], imaged_ref[...], 0, 0) for _, imaged_ref, _ in work]
        share = None
        for inner, (factor, pivots), (_, imaged_ref, frame_ref) in zip(inners, inverse_factors(inners), work):
            frame_ref[...] = dot(imaged_ref[...], factor, 1, 1)
            ratio = pivots / diagonal_of(inner)
            share = ratio if share is None else jnp.where(ratio < share, ratio, share)
        good = jnp.logical_and(step == 0, jnp.min(share) > PIVOT_SHARE)
        last = jnp.logical_or(good, step == SWEEPS)

        @pl.when(jnp.logical_not(last))
        def _():
            for gram_ref, imaged_ref, frame_ref in work:
                first = gram_ref[:, :RANK]
                imaged_ref[...] = jnp.where(step == 0, first, dot(gram_ref[...], frame_ref[...], 1, 0))

        return jnp.where(last, SWEEPS + 1, step + 1)

    lax.while_loop(lambda step: step <= SWEEPS, attempt, jnp.int32(0))
    return [frame_ref[...].astype(bf16) for _, _, frame_ref in work]


work_shapes = [pltpu.VMEM((2 * RANK, 2 * RANK), f32)] + [pltpu.VMEM((2 * RANK, RANK), f32)] * 2


def place(pos_ref):
    pos = pos_ref[0]
    return pos % 2, pos // PLANE % PLANES


def split(blocks, core, mine_ref, theirs_ref):
    half = mine_ref.shape[1]
    for b, block in enumerate(blocks):
        low, high = block[:half, :], block[half:, :]
        mine_ref[b] = jnp.where(core == 1, high, low)
        theirs_ref[b] = jnp.where(core == 1, low, high)


def joined(mine_ref, other_ref, core, b):
    mine, other = mine_ref[b], other_ref[b]
    low = jnp.where(core == 1, other, mine)
    high = jnp.where(core == 1, mine, other)
    return jnp.concatenate([low, high], 0)


def chunk(z, m, width):
    return pl.ds(pl.multiple_of((z ^ m) * width, width), width)


def member(pos_ref):
    return pos_ref[0] % PLANE


def copy_all(copies):
    for c in copies:
        c.start()
    for c in copies:
        c.wait()


def parts_kernel(pos_ref, x_ref, *refs):
    parts, sems = refs[:PLANE], refs[PLANE]
    where = [x_ref.at[:, chunk(member(pos_ref), m, parts[m].shape[1])] for m in range(PLANE)]
    copy_all([pltpu.make_async_copy(where[m], parts[m], sems.at[m]) for m in range(PLANE)])


def gram_kernel(pos_ref, *refs):
    parts, (rows_ref, mine_ref, theirs_ref) = refs[:PLANE], refs[PLANE:]
    core, _ = place(pos_ref)
    height = parts[0].shape[0]
    for m in range(PLANE):
        rows_ref[chunk(member(pos_ref), m, height), :] = parts[m][...]
    rows = rows_ref[...]
    gram = dot_low(rows, rows, 1, 1)
    split([gram[:RANK, :RANK], gram[RANK:, :RANK], gram[RANK:, RANK:]], core, mine_ref, theirs_ref)


def square(a, b, d):
    return jnp.concatenate([jnp.concatenate([a, b.T], 1), jnp.concatenate([b, d], 1)], 0)


def plane_gram(mine_ref, other_ref, core):
    return square(*[joined(mine_ref, other_ref, core, b) for b in range(3)])


def node_kernel(pos_ref, mine_ref, other_ref, rows_ref, *refs):
    nodes, low_ref, work = refs[:PLANES], refs[PLANES], refs[PLANES + 1 :]
    core, z = place(pos_ref)
    (low,) = leading_spaces([plane_gram(mine_ref, other_ref, core)], [work])
    low_ref[...] = low
    width = nodes[0].shape[1]
    for m in range(PLANES):
        nodes[m][...] = dot_low(low, rows_ref[:, chunk(z, m, width)], 0, 0).astype(bf16)


def reduced(gram, low):
    wide = low.astype(f32)
    return dot(wide, dot(gram, wide, 1, 0), 0, 0)


def diag_kernel(pos_ref, mine_ref, other_ref, low_ref, diag_ref):
    core, _ = place(pos_ref)
    diag = reduced(plane_gram(mine_ref, other_ref, core), low_ref[...])
    half = diag_ref.shape[1]
    diag_ref[0] = jnp.where(core == 1, diag[half:, :], diag[:half, :]).astype(diag_ref.dtype)


NEAR = [(0, 1), (2, 3)]
FAR = [(0, 2), (0, 3), (1, 2), (1, 3)]
PAIRS = NEAR + FAR


def cross_kernel(pos_ref, *refs):
    nodes, (mine_ref, theirs_ref, all_ref) = refs[:PLANES], refs[PLANES:]
    core, z = place(pos_ref)
    for m in range(PLANES):
        all_ref[z ^ m] = nodes[m][...]
    split([dot_low(all_ref[j], all_ref[i], 1, 1) for i, j in PAIRS], core, mine_ref, theirs_ref)


def pair_kernel(pos_ref, mine_ref, other_ref, *refs):
    nodes, outs, refs = refs[:PLANES], refs[PLANES : PLANES + 6], refs[PLANES + 6 :]
    all_ref, diag_ref, work = refs[0], refs[1], [refs[2:5], refs[5:8]]
    core, z = place(pos_ref)
    for m in range(PLANES):
        all_ref[z ^ m] = nodes[m][...]
        diag_ref[z ^ m] = joined(mine_ref, other_ref, core, len(NEAR) + m)
    grams = [square(diag_ref[i], joined(mine_ref, other_ref, core, b), diag_ref[j]) for b, (i, j) in enumerate(NEAR)]
    lows = leading_spaces(grams, work)
    for n, (gram, low, (i, j)) in enumerate(zip(grams, lows, NEAR)):
        low_ref, diag_out, node_ref = outs[3 * n : 3 * n + 3]
        low_ref[...] = low
        diag_out[...] = reduced(gram, low)
        node_ref[...] = dot_low(low, jnp.concatenate([all_ref[i], all_ref[j]], 0), 0, 0).astype(bf16)


def top_kernel(pos_ref, mine_ref, other_ref, low_a, diag_a, node_a, low_b, diag_b, node_b, *refs):
    (top_ref, gram_ref, low_ref), work = refs[:3], refs[3:]
    core, _ = place(pos_ref)
    cross = {pair: joined(mine_ref, other_ref, core, b) for b, pair in enumerate(FAR)}
    between = jnp.concatenate(
        [
            jnp.concatenate([cross[0, 2], cross[1, 2]], 1),
            jnp.concatenate([cross[0, 3], cross[1, 3]], 1),
        ],
        0,
    )
    between = dot(low_b[...].astype(f32), dot(between, low_a[...].astype(f32), 1, 0), 0, 0)
    gram = square(diag_a[...], between, diag_b[...])
    gram_ref[...] = gram
    (low,) = leading_spaces([gram], [work])
    low_ref[...] = low
    top_ref[...] = dot_low(low, jnp.concatenate([node_a[...], node_b[...]], 0), 0, 0).astype(bf16)


def factor_kernel(gram_ref, low_ref, factor_ref):
    factor_ref[...] = inverse_factors([reduced(gram_ref[...], low_ref[...])])[0][0]


def coeffs_kernel(pos_ref, rows_ref, factor_ref, *refs):
    tops, (mine_ref, theirs_ref) = refs[:PLANES], refs[PLANES:]
    core, z = place(pos_ref)
    width = tops[0].shape[1]
    total = None
    for m in range(PLANES):
        part = dot_low(rows_ref[:, chunk(z, m, width)], tops[m][...], 1, 1)
        total = part if total is None else total + part
    split([dot(total, factor_ref[...], 1, 1)], core, mine_ref, theirs_ref)


def project_kernel(pos_ref, mine_ref, other_ref, factor_ref, *refs):
    tops, outs, solved_ref = refs[:PLANES], refs[PLANES:-1], refs[-1]
    core, z = place(pos_ref)
    height, width = outs[0].shape[0], tops[0].shape[1]
    solved_ref[...] = dot(joined(mine_ref, other_ref, core, 0), factor_ref[...], 1, 0)
    solved = [solved_ref[chunk(member(pos_ref), m, height), :] for m in range(PLANE)]
    solved = jnp.concatenate(solved, 0).astype(bf16)
    for c in range(PLANES):
        made = dot_low(solved, tops[c][...], 1, 0).astype(bf16)
        for m in range(PLANE):
            outs[m][:, chunk(z, c, width)] = made[m * height : (m + 1) * height, :]


def whole_kernel(pos_ref, *refs):
    parts, out_ref, sems = refs[:PLANE], refs[PLANE], refs[PLANE + 1]
    where = [out_ref.at[:, chunk(member(pos_ref), m, parts[m].shape[1])] for m in range(PLANE)]
    copy_all([pltpu.make_async_copy(parts[m], where[m], sems.at[m]) for m in range(PLANE)])


smem = pl.BlockSpec(memory_space=pltpu.SMEM)
vmem = pl.BlockSpec(memory_space=pltpu.VMEM)
hbm = pl.BlockSpec(memory_space=pltpu.HBM)


def kernel(fn, outs, *args, scratch=(), scalar=True, far_in=False, far_out=False):
    single = not isinstance(outs, (list, tuple))
    shapes = [outs] if single else list(outs)
    res = pl.pallas_call(
        fn,
        out_shape=[jax.ShapeDtypeStruct(s, d) for s, d in shapes] if not single else None,
        in_specs=[smem if scalar and i == 0 else hbm if far_in else vmem for i in range(len(args))],
        out_specs=[hbm if far_out else vmem for _ in shapes],
        scratch_shapes=list(scratch),
        compiler_params=pltpu.CompilerParams(vmem_limit_bytes=40 * 2**20),
        name=fn.__name__,
    )(*args)
    return res


def body(mortality):
    count = lax.axis_size("cols")
    pos = lax.axis_index("cols").astype(jnp.int32).reshape(1)

    def swap(x, apart):
        return lax.ppermute(x, "cols", [(i, i ^ apart) for i in range(count)])

    def swap_all(parts, unit):
        return [parts[0]] + [swap(parts[m], unit * m) for m in range(1, len(parts))]

    def sum4(parts):
        parts = [p.astype(f32) for p in parts]
        return (parts[0] + parts[1]) + (parts[2] + parts[3])

    def plane_sum(mine, theirs):
        return sum4(swap_all([(mine + swap(theirs, 1)).astype(bf16)] * 4, 2))

    block, total = mortality.shape
    height, width = block * PLANE, total // PLANE
    part = width // PLANES
    half = RANK // 2

    sems = [pltpu.SemaphoreType.DMA((PLANE,))]
    parts = kernel(
        parts_kernel,
        [((block, width), bf16)] * PLANE,
        pos, pltpu.with_memory_space_constraint(mortality, pltpu.HBM),
        scratch=sems, far_in=True,
    )
    parts = swap_all(parts, 1)
    rows, mine, theirs = kernel(
        gram_kernel, [((height, width), bf16)] + [((3, half, RANK), f32)] * 2, pos, *parts
    )
    mine = plane_sum(mine, theirs)
    other = swap(mine, 1)
    *nodes, low = kernel(
        node_kernel,
        [((RANK, part), bf16)] * PLANES + [((2 * RANK, RANK), bf16)],
        pos, mine, other, rows,
        scratch=work_shapes,
    )
    nodes = swap_all(nodes, PLANE)
    (diag,) = kernel(diag_kernel, [((1, half, RANK), bf16)], pos, mine, other, low)

    mine, theirs = kernel(
        cross_kernel,
        [((len(PAIRS), half, RANK), f32)] * 2,
        pos, *nodes,
        scratch=[pltpu.VMEM((PLANES, RANK, part), bf16)],
    )
    mine = plane_sum(mine, theirs)
    low_sum = mine.astype(bf16)
    near = swap_all([jnp.concatenate([low_sum[: len(NEAR)], diag], 0)] * PLANES, PLANE)
    far = swap_all([low_sum[len(NEAR) :]] * PLANES, PLANE)
    mine = jnp.concatenate([sum4([x[: len(NEAR)] for x in near])] + [x[len(NEAR) :].astype(f32) for x in near], 0)
    pair_shapes = [((2 * RANK, RANK), bf16), ((RANK, RANK), f32), ((RANK, part), bf16)]
    pairs = kernel(
        pair_kernel,
        pair_shapes * 2,
        pos, mine, swap(mine, 1), *nodes,
        scratch=[pltpu.VMEM((PLANES, RANK, part), bf16), pltpu.VMEM((PLANES, RANK, RANK), f32)] + work_shapes * 2,
    )
    far, pairs = lax.optimization_barrier((far, pairs))
    mine = sum4(far)
    top, gram, low = kernel(
        top_kernel,
        [((RANK, part), bf16), ((2 * RANK, 2 * RANK), f32), ((2 * RANK, RANK), bf16)],
        pos, mine, swap(mine, 1), *pairs,
        scratch=work_shapes,
    )
    tops = swap_all([top] * PLANES, PLANE)
    (factor,) = kernel(factor_kernel, [((RANK, RANK), f32)], gram, low, scalar=False)

    mine, theirs = kernel(coeffs_kernel, [((1, height // 2, RANK), f32)] * 2, pos, rows, factor, *tops)
    mine = plane_sum(mine, theirs)
    outs = kernel(
        project_kernel,
        [((block, width), bf16)] * PLANE,
        pos, mine, swap(mine, 1), factor, *tops,
        scratch=[pltpu.VMEM((height, RANK), f32)],
    )
    (result,) = kernel(
        whole_kernel, [((block, total), bf16)], pos, *swap_all(outs, 1), scratch=sems, far_out=True
    )
    return result


def solution(mesh):
    in_specs = (P("cols", None),)
    out_specs = P("cols", None)
    return jax.shard_map(body, mesh=mesh, in_specs=in_specs, out_specs=out_specs, check_vma=False)
```

```python
import jax
import jax.numpy as jnp
from jax import lax
from jax.experimental import pallas as pl
from jax.experimental.pallas import tpu as pltpu
from jax.sharding import PartitionSpec as P

RANK = 128
LEVELS = 5
SWEEPS = 3
PLANE = 8
PLANES = 2**LEVELS // PLANE
TILE = 8
PANEL = 64
PLANE_ORDER = (0, 6, 7, 2, 4, 3, 5, 1)
TREE_ORDER = (0, 3, 2, 1)
PIVOT_SHARE = 2e-4

precise = lax.Precision.HIGHEST
f32 = jnp.float32
bf16 = jnp.bfloat16


def iota2(shape, dim):
    return lax.broadcasted_iota(jnp.int32, shape, dim)


def dot(a, b, ca, cb, precision=precise):
    return lax.dot_general(a, b, (((ca,), (cb,)), ((), ())), precision=precision, preferred_element_type=f32)


def dot_low(a, b, ca, cb):
    return dot(a, b, ca, cb, None)


def halves(x):
    high = x.astype(bf16)
    return high, (x - high.astype(f32)).astype(bf16)


def dot_split(a, b, ca, cb):
    ah, al = (a, None) if a.dtype == bf16 else halves(a)
    bh, bl = (b, None) if b.dtype == bf16 else halves(b)
    total = dot_low(ah, bh, ca, cb)
    if bl is not None:
        total = total + dot_low(ah, bl, ca, cb)
    return total if al is None else total + dot_low(al, bh, ca, cb)


def lanes_of(x, k):
    return jnp.broadcast_to(x[:, k : k + 1], x.shape)


def rows_of(x, s):
    return jnp.broadcast_to(x[s : s + 1, :], x.shape)


def eliminate(sets, first, ahead):
    lane = iota2((TILE, RANK), 1)
    sub = iota2((TILE, RANK), 0)
    count = len(sets[0])
    early = [None] * len(sets)
    for t in range(count):
        g = TILE * (first + t)
        spread, coming = [], []
        for n, tiles in enumerate(sets):
            cols = {} if early[n] is None else {t: early[n]}
            for i in range(t + len(cols), count):
                cols[i] = [lanes_of(tiles[i], g + j) for j in range(TILE)]
            spread.append(cols)
            near = (t, t + 1) if ahead and t + 1 < count else ()
            coming.append({i: [lanes_of(tiles[i], g + TILE + j) for j in range(TILE)] for i in near})
        for k in range(TILE):
            here = lane == g + k
            for tiles, cols, look in zip(sets, spread, coming):
                pivot_row = [rows_of(cols[t][j], k) if j >= k else None for j in range(TILE)]
                inv = 1.0 / pivot_row[k]
                scaled = [pivot_row[j] * inv if j > k else None for j in range(TILE)]
                row = jnp.where(here, 1.0, rows_of(tiles[t], k)) * inv
                look_row = [rows_of(x, k) * inv for x in look[t]] if look else None
                for i in range(t, count):
                    col = cols[i][k]
                    if i == t:
                        col = jnp.where(sub > k, col, 0.0)
                        kept = jnp.where(here & (sub > k), 0.0, tiles[i])
                    else:
                        kept = jnp.where(here, 0.0, tiles[i])
                    for j in range(k + 1, TILE):
                        cols[i][j] = cols[i][j] - col * scaled[j]
                    tiles[i] = kept - col * row
                    if i in look:
                        look[i] = [x - col * y for x, y in zip(look[i], look_row)]
        early = [look.get(t + 1) for look in coming]
    return sets


def inverse_factors(matrices):
    alone = len(matrices) == 1
    size = PANEL if alone else PANEL // 2
    rests = list(matrices)
    done = [[] for _ in rests]
    for lo in range(0, RANK, size):
        hi = lo + size
        sets = [[rest[TILE * t : TILE * t + TILE, :] for t in range(size // TILE)] for rest in rests]
        for n, tiles in enumerate(eliminate(sets, lo // TILE, alone)):
            panel = jnp.concatenate(tiles, 0)
            done[n].append(panel)
            if hi == RANK:
                continue
            r = iota2((size, RANK), 0) + lo
            c = iota2((size, RANK), 1)
            pivots = jnp.sum(jnp.where(r == c, panel, 0.0), 1, keepdims=True)
            rows = jnp.where(r == c, 1.0, jnp.where((c > r) & (c < hi), 0.0, panel))
            tail = rests[n][size:, :]
            c = iota2(tail.shape, 1)
            tail = jnp.where((c >= lo) & (c < hi), 0.0, tail)
            rests[n] = tail - dot(panel * (1.0 / pivots), rows, 0, 0)[hi:, :]
    results = []
    for panels in done:
        x = jnp.concatenate(panels, 0)
        r = iota2((RANK, RANK), 0)
        c = iota2((RANK, RANK), 1)
        pivots = jnp.sum(jnp.where(r == c, x, 0.0), 1, keepdims=True)
        unit = jnp.where(r > c, x, jnp.where(r == c, 1.0, 0.0))
        results.append((unit * lax.rsqrt(pivots), pivots))
    return results


def diagonal_of(x):
    return jnp.sum(jnp.where(iota2(x.shape, 0) == iota2(x.shape, 1), x, 0.0), 1, keepdims=True)


def leading_spaces(grams, work):
    for gram, (gram_ref, imaged_ref, _) in zip(grams, work):
        largest = jnp.maximum(diagonal_of(gram[:RANK, :RANK]), diagonal_of(gram[RANK:, RANK:]))
        gram = gram * (1.0 / jnp.max(largest, keepdims=True))
        gram_ref[...] = gram
        imaged = gram[:, :RANK]
        for step in range(SWEEPS - 1):
            imaged = dot_split(gram, imaged, 1, 0)
        imaged_ref[...] = imaged

    def attempt(step):
        inners = [dot(imaged_ref[...], imaged_ref[...], 0, 0) for _, imaged_ref, _ in work]
        share = None
        for inner, (factor, pivots), (_, imaged_ref, frame_ref) in zip(inners, inverse_factors(inners), work):
            frame_ref[...] = dot(imaged_ref[...], factor, 1, 1)
            ratio = pivots / diagonal_of(inner)
            share = ratio if share is None else jnp.where(ratio < share, ratio, share)
        good = jnp.logical_and(step == 0, jnp.min(share) > PIVOT_SHARE)
        last = jnp.logical_or(good, step == SWEEPS)

        @pl.when(jnp.logical_not(last))
        def _():
            for gram_ref, imaged_ref, frame_ref in work:
                first = gram_ref[:, :RANK]
                imaged_ref[...] = jnp.where(step == 0, first, dot(gram_ref[...], frame_ref[...], 1, 0))

        return jnp.where(last, SWEEPS + 1, step + 1)

    lax.while_loop(lambda step: step <= SWEEPS, attempt, jnp.int32(0))
    return [frame_ref[...].astype(bf16) for _, _, frame_ref in work]


work_shapes = [pltpu.VMEM((2 * RANK, 2 * RANK), f32)] + [pltpu.VMEM((2 * RANK, RANK), f32)] * 2


def place(pos_ref):
    pos = pos_ref[0]
    return pos % 2, pos // PLANE % PLANES


def split(blocks, core, mine_ref, theirs_ref):
    half = mine_ref.shape[1]
    for b, block in enumerate(blocks):
        low, high = block[:half, :], block[half:, :]
        mine_ref[b] = jnp.where(core == 1, high, low)
        theirs_ref[b] = jnp.where(core == 1, low, high)


def joined(mine_ref, other_ref, core, b):
    mine, other = mine_ref[b], other_ref[b]
    low = jnp.where(core == 1, other, mine)
    high = jnp.where(core == 1, mine, other)
    return jnp.concatenate([low, high], 0)


def chunk(z, m, width):
    return pl.ds(pl.multiple_of((z ^ m) * width, width), width)


def member(pos_ref):
    return pos_ref[0] % PLANE


def parts_kernel(pos_ref, x_ref, *refs):
    width = refs[0].shape[1]
    for ref, m in zip(refs, PLANE_ORDER):
        ref[...] = x_ref[:, chunk(member(pos_ref), m, width)]


def gram_kernel(pos_ref, *refs):
    parts, (rows_ref, mine_ref, theirs_ref) = refs[:PLANE], refs[PLANE:]
    core, _ = place(pos_ref)
    height = parts[0].shape[0]
    for ref, m in zip(parts, PLANE_ORDER):
        rows_ref[chunk(member(pos_ref), m, height), :] = ref[...]
    rows = rows_ref[...]
    gram = dot_low(rows, rows, 1, 1)
    split([gram[:RANK, :RANK], gram[RANK:, :RANK], gram[RANK:, RANK:]], core, mine_ref, theirs_ref)


def square(a, b, d):
    return jnp.concatenate([jnp.concatenate([a, b.T], 1), jnp.concatenate([b, d], 1)], 0)


def plane_gram(mine_ref, other_ref, core):
    return square(*[joined(mine_ref, other_ref, core, b) for b in range(3)])


def node_kernel(pos_ref, mine_ref, other_ref, rows_ref, *refs):
    nodes, low_ref, work = refs[:PLANES], refs[PLANES], refs[PLANES + 1 :]
    core, z = place(pos_ref)
    (low,) = leading_spaces([plane_gram(mine_ref, other_ref, core)], [work])
    low_ref[...] = low
    width = nodes[0].shape[1]
    for ref, m in zip(nodes, TREE_ORDER):
        ref[...] = dot_low(low, rows_ref[:, chunk(z, m, width)], 0, 0).astype(bf16)


def reduced(gram, low):
    return dot_split(low, dot_split(gram, low, 1, 0), 0, 0)


def diag_kernel(pos_ref, mine_ref, other_ref, low_ref, diag_ref):
    core, _ = place(pos_ref)
    diag = reduced(plane_gram(mine_ref, other_ref, core), low_ref[...])
    half = diag_ref.shape[1]
    diag_ref[0] = jnp.where(core == 1, diag[half:, :], diag[:half, :]).astype(diag_ref.dtype)


PAIRS = [(i, j) for i in range(PLANES) for j in range(i + 1, PLANES)]


def cross_kernel(pos_ref, *refs):
    nodes, (mine_ref, theirs_ref, all_ref) = refs[:PLANES], refs[PLANES:]
    core, z = place(pos_ref)
    for ref, m in zip(nodes, TREE_ORDER):
        all_ref[z ^ m] = ref[...]
    split([dot_low(all_ref[j], all_ref[i], 1, 1) for i, j in PAIRS], core, mine_ref, theirs_ref)


def top_kernel(pos_ref, mine_ref, other_ref, *refs):
    nodes, (top_ref, gram_ref, low_ref), refs = refs[:PLANES], refs[PLANES : PLANES + 3], refs[PLANES + 3 :]
    all_ref, diag_ref, work = refs[0], refs[1], [refs[2:5], refs[5:8]]
    core, z = place(pos_ref)
    for ref, m in zip(nodes, TREE_ORDER):
        all_ref[z ^ m] = ref[...]
        diag_ref[z ^ m] = joined(mine_ref, other_ref, core, len(PAIRS) + m)
    cross = {pair: joined(mine_ref, other_ref, core, b) for b, pair in enumerate(PAIRS)}
    gram_a = square(diag_ref[0], cross[0, 1], diag_ref[1])
    gram_b = square(diag_ref[2], cross[2, 3], diag_ref[3])
    low_a, low_b = leading_spaces([gram_a, gram_b], work)
    between = jnp.concatenate(
        [
            jnp.concatenate([cross[0, 2], cross[1, 2]], 1),
            jnp.concatenate([cross[0, 3], cross[1, 3]], 1),
        ],
        0,
    )
    gram = square(
        reduced(gram_a, low_a),
        dot_split(low_b, dot_split(between, low_a, 1, 0), 0, 0),
        reduced(gram_b, low_b),
    )
    gram_ref[...] = gram
    (low,) = leading_spaces([gram], work[:1])
    low_ref[...] = low
    node_a = dot_low(low_a, jnp.concatenate([all_ref[0], all_ref[1]], 0), 0, 0).astype(bf16)
    node_b = dot_low(low_b, jnp.concatenate([all_ref[2], all_ref[3]], 0), 0, 0).astype(bf16)
    top_ref[...] = dot_low(low, jnp.concatenate([node_a, node_b], 0), 0, 0).astype(bf16)


def factor_kernel(gram_ref, low_ref, factor_ref):
    factor_ref[...] = inverse_factors([reduced(gram_ref[...], low_ref[...])])[0][0]


def coeffs_kernel(pos_ref, rows_ref, factor_ref, *refs):
    tops, (mine_ref, theirs_ref) = refs[:PLANES], refs[PLANES:]
    core, z = place(pos_ref)
    width = tops[0].shape[1]
    total = None
    for m, ref in enumerate(tops):
        part = dot_low(rows_ref[:, chunk(z, m, width)], ref[...], 1, 1)
        total = part if total is None else total + part
    split([dot(total, factor_ref[...], 1, 1)], core, mine_ref, theirs_ref)


def project_kernel(pos_ref, mine_ref, other_ref, factor_ref, *refs):
    tops, outs, solved_ref = refs[:PLANES], refs[PLANES:-1], refs[-1]
    core, z = place(pos_ref)
    height, width = outs[0].shape[0], tops[0].shape[1]
    solved_ref[...] = dot(joined(mine_ref, other_ref, core, 0), factor_ref[...], 1, 0)
    solved = [solved_ref[chunk(member(pos_ref), m, height), :] for m in PLANE_ORDER]
    solved = jnp.concatenate(solved, 0).astype(bf16)
    for m, ref in enumerate(tops):
        made = dot_low(solved, ref[...], 1, 0).astype(bf16)
        for k in range(PLANE):
            outs[k][:, chunk(z, m, width)] = made[k * height : (k + 1) * height, :]


def whole_kernel(pos_ref, *refs):
    parts, out_ref = refs[:PLANE], refs[PLANE]
    width = parts[0].shape[1]
    for ref, m in zip(parts, PLANE_ORDER):
        out_ref[:, chunk(member(pos_ref), m, width)] = ref[...]


smem = pl.BlockSpec(memory_space=pltpu.SMEM)
vmem = pl.BlockSpec(memory_space=pltpu.VMEM)


def kernel(fn, outs, *args, scratch=(), scalar=True):
    single = not isinstance(outs, (list, tuple))
    shapes = [outs] if single else list(outs)
    res = pl.pallas_call(
        fn,
        out_shape=[jax.ShapeDtypeStruct(s, d) for s, d in shapes] if not single else None,
        in_specs=[smem if scalar and i == 0 else vmem for i in range(len(args))],
        out_specs=[vmem for _ in shapes],
        scratch_shapes=list(scratch),
        compiler_params=pltpu.CompilerParams(vmem_limit_bytes=40 * 2**20),
        name=fn.__name__,
    )(*args)
    return res


def body(mortality):
    count = lax.axis_size("cols")
    pos = lax.axis_index("cols").astype(jnp.int32).reshape(1)

    def swap(x, apart):
        return lax.ppermute(x, "cols", [(i, i ^ apart) for i in range(count)])

    def swap_all(parts, order, unit=1):
        return [x if m == 0 else swap(x, unit * m) for x, m in zip(parts, order)]

    def sum4(parts):
        parts = [p.astype(f32) for p in parts]
        return (parts[0] + parts[1]) + (parts[2] + parts[3])

    def plane_sum(mine, theirs):
        return sum4(swap_all([(mine + swap(theirs, 1)).astype(bf16)] * 4, range(4), 2))

    block, total = mortality.shape
    height, width = block * PLANE, total // PLANE
    part = width // PLANES
    half = RANK // 2

    parts = kernel(parts_kernel, [((block, width), bf16)] * PLANE, pos, mortality)
    parts = swap_all(parts, PLANE_ORDER)
    rows, mine, theirs = kernel(
        gram_kernel, [((height, width), bf16)] + [((3, half, RANK), f32)] * 2, pos, *parts
    )
    mine = plane_sum(mine, theirs)
    other = swap(mine, 1)
    *nodes, low = kernel(
        node_kernel,
        [((RANK, part), bf16)] * PLANES + [((2 * RANK, RANK), bf16)],
        pos, mine, other, rows,
        scratch=work_shapes,
    )
    nodes = swap_all(nodes, TREE_ORDER, PLANE)
    (diag,) = kernel(diag_kernel, [((1, half, RANK), bf16)], pos, mine, other, low)

    mine, theirs = kernel(
        cross_kernel,
        [((len(PAIRS), half, RANK), f32)] * 2,
        pos, *nodes,
        scratch=[pltpu.VMEM((PLANES, RANK, part), bf16)],
    )
    mine = plane_sum(mine, theirs)
    both = swap_all([jnp.concatenate([mine.astype(bf16), diag], 0)] * PLANES, range(PLANES), PLANE)
    mine = jnp.concatenate([sum4([x[: len(PAIRS)] for x in both])] + [x[len(PAIRS) :].astype(f32) for x in both], 0)
    top, gram, low = kernel(
        top_kernel,
        [((RANK, part), bf16), ((2 * RANK, 2 * RANK), f32), ((2 * RANK, RANK), bf16)],
        pos, mine, swap(mine, 1), *nodes,
        scratch=[pltpu.VMEM((PLANES, RANK, part), bf16), pltpu.VMEM((PLANES, RANK, RANK), f32)] + work_shapes * 2,
    )
    tops = swap_all([top] * PLANES, range(PLANES), PLANE)
    (factor,) = kernel(factor_kernel, [((RANK, RANK), f32)], gram, low, scalar=False)

    mine, theirs = kernel(coeffs_kernel, [((1, height // 2, RANK), f32)] * 2, pos, rows, factor, *tops)
    mine = plane_sum(mine, theirs)
    outs = kernel(
        project_kernel,
        [((block, width), bf16)] * PLANE,
        pos, mine, swap(mine, 1), factor, *tops,
        scratch=[pltpu.VMEM((height, RANK), f32)],
    )
    (result,) = kernel(whole_kernel, [((block, total), bf16)], pos, *swap_all(outs, PLANE_ORDER))
    return result


def solution(mesh):
    in_specs = (P("cols", None),)
    out_specs = P("cols", None)
    return jax.shard_map(body, mesh=mesh, in_specs=in_specs, out_specs=out_specs, check_vma=False)
```

```python
import jax
import jax.numpy as jnp
from jax import lax
from jax.experimental import pallas as pl
from jax.experimental.pallas import tpu as pltpu
from jax.sharding import PartitionSpec as P

RANK = 128
LEVELS = 5
SWEEPS = 3
PLANE = 8
PLANES = 2**LEVELS // PLANE
TILE = 8
PANEL = 64
PLANE_ORDER = (0, 6, 7, 2, 4, 3, 5, 1)
TREE_ORDER = (0, 3, 2, 1)
PIVOT_SHARE = 2e-4

precise = lax.Precision.HIGHEST
f32 = jnp.float32
bf16 = jnp.bfloat16


def iota2(shape, dim):
    return lax.broadcasted_iota(jnp.int32, shape, dim)


def dot(a, b, ca, cb, precision=precise):
    return lax.dot_general(a, b, (((ca,), (cb,)), ((), ())), precision=precision, preferred_element_type=f32)


def dot_low(a, b, ca, cb):
    return dot(a, b, ca, cb, None)


def halves(x):
    high = x.astype(bf16)
    return high, (x - high.astype(f32)).astype(bf16)


def dot_split(a, b, ca, cb):
    ah, al = (a, None) if a.dtype == bf16 else halves(a)
    bh, bl = (b, None) if b.dtype == bf16 else halves(b)
    total = dot_low(ah, bh, ca, cb)
    if bl is not None:
        total = total + dot_low(ah, bl, ca, cb)
    return total if al is None else total + dot_low(al, bh, ca, cb)


def lanes_of(x, k):
    return jnp.broadcast_to(x[:, k : k + 1], x.shape)


def rows_of(x, s):
    return jnp.broadcast_to(x[s : s + 1, :], x.shape)


def eliminate(sets, first, ahead):
    lane = iota2((TILE, RANK), 1)
    sub = iota2((TILE, RANK), 0)
    count = len(sets[0])
    early = [None] * len(sets)
    pivots = [[] for _ in sets]
    for t in range(count):
        g = TILE * (first + t)
        spread, coming = [], []
        for n, tiles in enumerate(sets):
            cols = {} if early[n] is None else {t: early[n]}
            for i in range(t + len(cols), count):
                cols[i] = [lanes_of(tiles[i], g + j) for j in range(TILE)]
            spread.append(cols)
            near = (t, t + 1) if ahead and t + 1 < count else ()
            coming.append({i: [lanes_of(tiles[i], g + TILE + j) for j in range(TILE)] for i in near})
            pivots[n].append(jnp.zeros((TILE, RANK), f32))
        for k in range(TILE):
            here = lane == g + k
            for tiles, cols, look, held in zip(sets, spread, coming, pivots):
                pivot_row = [rows_of(cols[t][j], k) if j >= k else None for j in range(TILE)]
                held[t] = jnp.where(sub == k, pivot_row[k], held[t])
                inv = 1.0 / pivot_row[k]
                scaled = [pivot_row[j] * inv if j > k else None for j in range(TILE)]
                row = jnp.where(here, 1.0, rows_of(tiles[t], k)) * inv
                look_row = [rows_of(x, k) * inv for x in look[t]] if look else None
                for i in range(t, count):
                    col = cols[i][k]
                    if i == t:
                        col = jnp.where(sub > k, col, 0.0)
                        kept = jnp.where(here & (sub > k), 0.0, tiles[i])
                    else:
                        kept = jnp.where(here, 0.0, tiles[i])
                    for j in range(k + 1, TILE):
                        cols[i][j] = cols[i][j] - col * scaled[j]
                    tiles[i] = kept - col * row
                    if i in look:
                        look[i] = [x - col * y for x, y in zip(look[i], look_row)]
        early = [look.get(t + 1) for look in coming]
    return list(zip(sets, pivots))


def inverse_factors(matrices):
    alone = len(matrices) == 1
    size = PANEL if alone else PANEL // 2
    rests = list(matrices)
    done = [[] for _ in rests]
    for lo in range(0, RANK, size):
        hi = lo + size
        sets = [[rest[TILE * t : TILE * t + TILE, :] for t in range(size // TILE)] for rest in rests]
        r = iota2((size, RANK), 0) + lo
        c = iota2((size, RANK), 1)
        for n, (tiles, pivots) in enumerate(eliminate(sets, lo // TILE, alone)):
            panel = jnp.concatenate(tiles, 0)
            pivots = jnp.concatenate(pivots, 0)
            unit = jnp.where(r > c, panel, jnp.where(r == c, 1.0, 0.0))
            done[n].append((unit * lax.rsqrt(pivots), pivots))
            if hi == RANK:
                continue
            rows = jnp.where(r == c, 1.0, jnp.where((c > r) & (c < hi), 0.0, panel))
            tail = rests[n][size:, :]
            at = iota2(tail.shape, 1)
            tail = jnp.where((at >= lo) & (at < hi), 0.0, tail)
            rests[n] = tail - dot(panel * (1.0 / pivots), rows, 0, 0)[hi:, :]
    return [tuple(jnp.concatenate(x, 0) for x in zip(*panels)) for panels in done]


def diagonal_of(x):
    return jnp.sum(jnp.where(iota2(x.shape, 0) == iota2(x.shape, 1), x, 0.0), 1, keepdims=True)


def unit_scale(blocks):
    largest = diagonal_of(blocks[0])
    for x in blocks[1:]:
        largest = jnp.maximum(largest, diagonal_of(x))
    return 1.0 / jnp.max(largest, keepdims=True)


def leading_spaces(grams, scale, work, careful, sound_ref):
    for gram, (gram_ref, imaged_ref, _) in zip(grams, work):
        gram_ref[...] = gram * scale
        imaged_ref[...] = gram_ref[:, :RANK]
    count = jnp.where(careful, SWEEPS, 1)

    def sweep(step, carry):
        @pl.when(jnp.logical_not(careful))
        def _():
            images = [imaged_ref[...] for _, imaged_ref, _ in work]
            for again in range(SWEEPS - 1):
                images = [dot_split(gram_ref[...], x, 1, 0) for x, (gram_ref, _, _) in zip(images, work)]
            for x, (_, imaged_ref, _) in zip(images, work):
                imaged_ref[...] = x

        inners = [dot(imaged_ref[...], imaged_ref[...], 0, 0) for _, imaged_ref, _ in work]
        for inner, (factor, pivots), (_, imaged_ref, frame_ref) in zip(inners, inverse_factors(inners), work):
            frame_ref[...] = dot(imaged_ref[...], factor, 1, 1)
            sound_ref[...] = jnp.where(pivots > PIVOT_SHARE * diagonal_of(inner), sound_ref[...], 0.0)

        @pl.when(step + 1 < count)
        def _():
            for gram_ref, imaged_ref, frame_ref in work:
                imaged_ref[...] = dot(gram_ref[...], frame_ref[...], 1, 0)

        return carry

    lax.fori_loop(0, count, sweep, 0)
    return [frame_ref[...].astype(bf16) for _, _, frame_ref in work]


def until_sound(sound_ref, attempt):
    def once(mode):
        sound_ref[...] = jnp.ones(sound_ref.shape, f32)
        attempt(mode == 1)
        sound = jnp.min(sound_ref[...]) > 0.5
        return jnp.where(jnp.logical_or(mode == 1, sound), 2, 1)

    lax.while_loop(lambda mode: mode < 2, once, jnp.int32(0))


sound_shape = [pltpu.VMEM((RANK, RANK), f32)]
work_shapes = [pltpu.VMEM((2 * RANK, 2 * RANK), f32)] + [pltpu.VMEM((2 * RANK, RANK), f32)] * 2


def place(pos_ref):
    pos = pos_ref[0]
    return pos % 2, pos // PLANE % PLANES


def split(blocks, core, mine_ref, theirs_ref):
    half = mine_ref.shape[1]
    for b, block in enumerate(blocks):
        low, high = block[:half, :], block[half:, :]
        mine_ref[b] = jnp.where(core == 1, high, low)
        theirs_ref[b] = jnp.where(core == 1, low, high)


def joined(mine_ref, other_ref, core, b):
    mine, other = mine_ref[b], other_ref[b]
    low = jnp.where(core == 1, other, mine)
    high = jnp.where(core == 1, mine, other)
    return jnp.concatenate([low, high], 0)


def chunk(z, m, width):
    return pl.ds(pl.multiple_of((z ^ m) * width, width), width)


def member(pos_ref):
    return pos_ref[0] % PLANE


def parts_kernel(pos_ref, x_ref, *refs):
    width = refs[0].shape[1]
    for ref, m in zip(refs, PLANE_ORDER):
        ref[...] = x_ref[:, chunk(member(pos_ref), m, width)]


def gram_kernel(pos_ref, *refs):
    parts, (rows_ref, mine_ref, theirs_ref) = refs[:PLANE], refs[PLANE:]
    core, _ = place(pos_ref)
    height = parts[0].shape[0]
    for ref, m in zip(parts, PLANE_ORDER):
        rows_ref[chunk(member(pos_ref), m, height), :] = ref[...]
    rows = rows_ref[...]
    gram = dot_low(rows, rows, 1, 1)
    split([gram[:RANK, :RANK], gram[RANK:, :RANK], gram[RANK:, RANK:]], core, mine_ref, theirs_ref)


def square(a, b, d):
    return jnp.concatenate([jnp.concatenate([a, b.T], 1), jnp.concatenate([b, d], 1)], 0)


def plane_gram(mine_ref, other_ref, core):
    return square(*[joined(mine_ref, other_ref, core, b) for b in range(3)])


def node_kernel(pos_ref, mine_ref, other_ref, rows_ref, *refs):
    nodes, low_ref, sound_ref, work = refs[:PLANES], refs[PLANES], refs[PLANES + 1], refs[PLANES + 2 :]
    core, z = place(pos_ref)
    width = nodes[0].shape[1]

    def attempt(careful):
        gram = plane_gram(mine_ref, other_ref, core)
        scale = unit_scale([gram[:RANK, :RANK], gram[RANK:, RANK:]])
        (low,) = leading_spaces([gram], scale, [work], careful, sound_ref)
        low_ref[...] = low
        for ref, m in zip(nodes, TREE_ORDER):
            ref[...] = dot_low(low, rows_ref[:, chunk(z, m, width)], 0, 0).astype(bf16)

    until_sound(sound_ref, attempt)


def reduced(gram, low):
    return dot_split(low, dot_split(gram, low, 1, 0), 0, 0)


def diag_kernel(pos_ref, mine_ref, other_ref, low_ref, diag_ref):
    core, _ = place(pos_ref)
    diag = reduced(plane_gram(mine_ref, other_ref, core), low_ref[...])
    half = diag_ref.shape[1]
    diag_ref[0] = jnp.where(core == 1, diag[half:, :], diag[:half, :]).astype(diag_ref.dtype)


PAIRS = [(i, j) for i in range(PLANES) for j in range(i + 1, PLANES)]


def cross_kernel(pos_ref, *refs):
    nodes, (mine_ref, theirs_ref, all_ref) = refs[:PLANES], refs[PLANES:]
    core, z = place(pos_ref)
    for ref, m in zip(nodes, TREE_ORDER):
        all_ref[z ^ m] = ref[...]
    split([dot_low(all_ref[j], all_ref[i], 1, 1) for i, j in PAIRS], core, mine_ref, theirs_ref)


def top_kernel(pos_ref, mine_ref, other_ref, *refs):
    nodes, (top_ref, gram_ref, low_ref), refs = refs[:PLANES], refs[PLANES : PLANES + 3], refs[PLANES + 3 :]
    all_ref, diag_ref, sound_ref, work = refs[0], refs[1], refs[2], [refs[3:6], refs[6:9]]
    core, z = place(pos_ref)
    for ref, m in zip(nodes, TREE_ORDER):
        all_ref[z ^ m] = ref[...]
        diag_ref[z ^ m] = joined(mine_ref, other_ref, core, len(PAIRS) + m)

    def attempt(careful):
        cross = {pair: joined(mine_ref, other_ref, core, b) for b, pair in enumerate(PAIRS)}
        scale = unit_scale([diag_ref[y] for y in range(PLANES)])
        grams = [square(diag_ref[i], cross[i, j], diag_ref[j]) for i, j in ((0, 1), (2, 3))]
        low_a, low_b = leading_spaces(grams, scale, work, careful, sound_ref)
        between = jnp.concatenate(
            [
                jnp.concatenate([cross[0, 2], cross[1, 2]], 1),
                jnp.concatenate([cross[0, 3], cross[1, 3]], 1),
            ],
            0,
        )
        gram = square(
            reduced(grams[0], low_a),
            dot_split(low_b, dot_split(between, low_a, 1, 0), 0, 0),
            reduced(grams[1], low_b),
        )
        gram_ref[...] = gram
        node_a = dot_low(low_a, jnp.concatenate([all_ref[0], all_ref[1]], 0), 0, 0).astype(bf16)
        node_b = dot_low(low_b, jnp.concatenate([all_ref[2], all_ref[3]], 0), 0, 0).astype(bf16)
        (low,) = leading_spaces([gram], scale, work[:1], careful, sound_ref)
        low_ref[...] = low
        top_ref[...] = dot_low(low, jnp.concatenate([node_a, node_b], 0), 0, 0).astype(bf16)

    until_sound(sound_ref, attempt)


def factor_kernel(gram_ref, low_ref, factor_ref):
    factor_ref[...] = inverse_factors([reduced(gram_ref[...], low_ref[...])])[0][0]


def coeffs_kernel(pos_ref, rows_ref, factor_ref, *refs):
    tops, (mine_ref, theirs_ref) = refs[:PLANES], refs[PLANES:]
    core, z = place(pos_ref)
    width = tops[0].shape[1]
    total = None
    for m, ref in enumerate(tops):
        part = dot_low(rows_ref[:, chunk(z, m, width)], ref[...], 1, 1)
        total = part if total is None else total + part
    split([dot(total, factor_ref[...], 1, 1)], core, mine_ref, theirs_ref)


def project_kernel(pos_ref, mine_ref, other_ref, factor_ref, *refs):
    tops, outs, solved_ref = refs[:PLANES], refs[PLANES:-1], refs[-1]
    core, z = place(pos_ref)
    height, width = outs[0].shape[0], tops[0].shape[1]
    solved_ref[...] = dot(joined(mine_ref, other_ref, core, 0), factor_ref[...], 1, 0)
    solved = [solved_ref[chunk(member(pos_ref), m, height), :] for m in PLANE_ORDER]
    solved = jnp.concatenate(solved, 0).astype(bf16)
    for m, ref in enumerate(tops):
        made = dot_low(solved, ref[...], 1, 0).astype(bf16)
        for k in range(PLANE):
            outs[k][:, chunk(z, m, width)] = made[k * height : (k + 1) * height, :]


def whole_kernel(pos_ref, *refs):
    parts, out_ref = refs[:PLANE], refs[PLANE]
    width = parts[0].shape[1]
    for ref, m in zip(parts, PLANE_ORDER):
        out_ref[:, chunk(member(pos_ref), m, width)] = ref[...]


smem = pl.BlockSpec(memory_space=pltpu.SMEM)
vmem = pl.BlockSpec(memory_space=pltpu.VMEM)


def kernel(fn, outs, *args, scratch=(), scalar=True):
    single = not isinstance(outs, (list, tuple))
    shapes = [outs] if single else list(outs)
    res = pl.pallas_call(
        fn,
        out_shape=[jax.ShapeDtypeStruct(s, d) for s, d in shapes] if not single else None,
        in_specs=[smem if scalar and i == 0 else vmem for i in range(len(args))],
        out_specs=[vmem for _ in shapes],
        scratch_shapes=list(scratch),
        compiler_params=pltpu.CompilerParams(vmem_limit_bytes=40 * 2**20),
        name=fn.__name__,
    )(*args)
    return res


def body(mortality):
    count = lax.axis_size("cols")
    pos = lax.axis_index("cols").astype(jnp.int32).reshape(1)

    def swap(x, apart):
        return lax.ppermute(x, "cols", [(i, i ^ apart) for i in range(count)])

    def swap_all(parts, order, unit=1):
        return [x if m == 0 else swap(x, unit * m) for x, m in zip(parts, order)]

    def sum4(parts):
        parts = [p.astype(f32) for p in parts]
        return (parts[0] + parts[1]) + (parts[2] + parts[3])

    def plane_sum(mine, theirs):
        return sum4(swap_all([(mine + swap(theirs, 1)).astype(bf16)] * 4, range(4), 2))

    block, total = mortality.shape
    height, width = block * PLANE, total // PLANE
    part = width // PLANES
    half = RANK // 2

    parts = kernel(parts_kernel, [((block, width), bf16)] * PLANE, pos, mortality)
    parts = swap_all(parts, PLANE_ORDER)
    rows, mine, theirs = kernel(
        gram_kernel, [((height, width), bf16)] + [((3, half, RANK), f32)] * 2, pos, *parts
    )
    mine = plane_sum(mine, theirs)
    other = swap(mine, 1)
    *nodes, low = kernel(
        node_kernel,
        [((RANK, part), bf16)] * PLANES + [((2 * RANK, RANK), bf16)],
        pos, mine, other, rows,
        scratch=sound_shape + work_shapes,
    )
    nodes = swap_all(nodes, TREE_ORDER, PLANE)
    (diag,) = kernel(diag_kernel, [((1, half, RANK), bf16)], pos, mine, other, low)

    mine, theirs = kernel(
        cross_kernel,
        [((len(PAIRS), half, RANK), f32)] * 2,
        pos, *nodes,
        scratch=[pltpu.VMEM((PLANES, RANK, part), bf16)],
    )
    mine = plane_sum(mine, theirs)
    both = swap_all([jnp.concatenate([mine.astype(bf16), diag], 0)] * PLANES, range(PLANES), PLANE)
    mine = jnp.concatenate([sum4([x[: len(PAIRS)] for x in both])] + [x[len(PAIRS) :].astype(f32) for x in both], 0)
    top, gram, low = kernel(
        top_kernel,
        [((RANK, part), bf16), ((2 * RANK, 2 * RANK), f32), ((2 * RANK, RANK), bf16)],
        pos, mine, swap(mine, 1), *nodes,
        scratch=[pltpu.VMEM((PLANES, RANK, part), bf16), pltpu.VMEM((PLANES, RANK, RANK), f32)]
        + sound_shape
        + work_shapes * 2,
    )
    tops = swap_all([top] * PLANES, range(PLANES), PLANE)
    (factor,) = kernel(factor_kernel, [((RANK, RANK), f32)], gram, low, scalar=False)

    mine, theirs = kernel(coeffs_kernel, [((1, height // 2, RANK), f32)] * 2, pos, rows, factor, *tops)
    mine = plane_sum(mine, theirs)
    outs = kernel(
        project_kernel,
        [((block, width), bf16)] * PLANE,
        pos, mine, swap(mine, 1), factor, *tops,
        scratch=[pltpu.VMEM((height, RANK), f32)],
    )
    (result,) = kernel(whole_kernel, [((block, total), bf16)], pos, *swap_all(outs, PLANE_ORDER))
    return result


def solution(mesh):
    in_specs = (P("cols", None),)
    out_specs = P("cols", None)
    return jax.shard_map(body, mesh=mesh, in_specs=in_specs, out_specs=out_specs, check_vma=False)
```

```python
import jax
import jax.numpy as jnp
from jax import lax
from jax.experimental import pallas as pl
from jax.experimental.pallas import tpu as pltpu
from jax.sharding import PartitionSpec as P

RANK = 128
LEVELS = 5
SWEEPS = 3
PLANE = 8
PLANES = 2**LEVELS // PLANE
TILE = 8
PANEL = 64
PLANE_ORDER = (0, 6, 7, 2, 4, 3, 5, 1)
MIDDLE = (1, 2)
PIVOT_SHARE = 2e-4

precise = lax.Precision.HIGHEST
f32 = jnp.float32
bf16 = jnp.bfloat16


def iota2(shape, dim):
    return lax.broadcasted_iota(jnp.int32, shape, dim)


def dot(a, b, ca, cb, precision=precise):
    return lax.dot_general(a, b, (((ca,), (cb,)), ((), ())), precision=precision, preferred_element_type=f32)


def dot_low(a, b, ca, cb):
    return dot(a, b, ca, cb, None)


def halves(x):
    high = x.astype(bf16)
    return high, (x - high.astype(f32)).astype(bf16)


def dot_split(a, b, ca, cb):
    ah, al = (a, None) if a.dtype == bf16 else halves(a)
    bh, bl = (b, None) if b.dtype == bf16 else halves(b)
    total = dot_low(ah, bh, ca, cb)
    if bl is not None:
        total = total + dot_low(ah, bl, ca, cb)
    return total if al is None else total + dot_low(al, bh, ca, cb)


def lanes_of(x, k):
    return jnp.broadcast_to(x[:, k : k + 1], x.shape)


def rows_of(x, s):
    return jnp.broadcast_to(x[s : s + 1, :], x.shape)


def eliminate(sets, first, ahead):
    lane = iota2((TILE, RANK), 1)
    sub = iota2((TILE, RANK), 0)
    count = len(sets[0])
    early = [None] * len(sets)
    pivots = [[] for _ in sets]
    for t in range(count):
        g = TILE * (first + t)
        spread, coming = [], []
        for n, tiles in enumerate(sets):
            cols = {} if early[n] is None else {t: early[n]}
            for i in range(t + len(cols), count):
                cols[i] = [lanes_of(tiles[i], g + j) for j in range(TILE)]
            spread.append(cols)
            near = (t, t + 1) if ahead and t + 1 < count else ()
            coming.append({i: [lanes_of(tiles[i], g + TILE + j) for j in range(TILE)] for i in near})
            pivots[n].append(jnp.zeros((TILE, RANK), f32))
        for k in range(TILE):
            here = lane == g + k
            for tiles, cols, look, held in zip(sets, spread, coming, pivots):
                pivot_row = [rows_of(cols[t][j], k) if j >= k else None for j in range(TILE)]
                held[t] = jnp.where(sub == k, pivot_row[k], held[t])
                inv = 1.0 / pivot_row[k]
                scaled = [pivot_row[j] * inv if j > k else None for j in range(TILE)]
                row = jnp.where(here, 1.0, rows_of(tiles[t], k)) * inv
                look_row = [rows_of(x, k) * inv for x in look[t]] if look else None
                for i in range(t, count):
                    col = cols[i][k]
                    if i == t:
                        col = jnp.where(sub > k, col, 0.0)
                        kept = jnp.where(here & (sub > k), 0.0, tiles[i])
                    else:
                        kept = jnp.where(here, 0.0, tiles[i])
                    for j in range(k + 1, TILE):
                        cols[i][j] = cols[i][j] - col * scaled[j]
                    tiles[i] = kept - col * row
                    if i in look:
                        look[i] = [x - col * y for x, y in zip(look[i], look_row)]
        early = [look.get(t + 1) for look in coming]
    return list(zip(sets, pivots))


def inverse_factors(matrices):
    alone = len(matrices) == 1
    size = PANEL if alone else PANEL // 2
    rests = list(matrices)
    done = [[] for _ in rests]
    for lo in range(0, RANK, size):
        hi = lo + size
        sets = [[rest[TILE * t : TILE * t + TILE, :] for t in range(size // TILE)] for rest in rests]
        r = iota2((size, RANK), 0) + lo
        c = iota2((size, RANK), 1)
        for n, (tiles, pivots) in enumerate(eliminate(sets, lo // TILE, alone)):
            panel = jnp.concatenate(tiles, 0)
            pivots = jnp.concatenate(pivots, 0)
            unit = jnp.where(r > c, panel, jnp.where(r == c, 1.0, 0.0))
            done[n].append((unit * lax.rsqrt(pivots), pivots))
            if hi == RANK:
                continue
            rows = jnp.where(r == c, 1.0, jnp.where((c > r) & (c < hi), 0.0, panel))
            tail = rests[n][size:, :]
            at = iota2(tail.shape, 1)
            tail = jnp.where((at >= lo) & (at < hi), 0.0, tail)
            rests[n] = tail - dot(panel * (1.0 / pivots), rows, 0, 0)[hi:, :]
    return [tuple(jnp.concatenate(x, 0) for x in zip(*panels)) for panels in done]


def diagonal_of(x):
    return jnp.sum(jnp.where(iota2(x.shape, 0) == iota2(x.shape, 1), x, 0.0), 1, keepdims=True)


def unit_scale(blocks):
    largest = diagonal_of(blocks[0])
    for x in blocks[1:]:
        largest = jnp.maximum(largest, diagonal_of(x))
    return 1.0 / jnp.max(largest, keepdims=True)


def leading_spaces(grams, scale, work, careful, sound_ref):
    for gram, (gram_ref, imaged_ref, _) in zip(grams, work):
        gram_ref[...] = gram * scale
        imaged_ref[...] = gram_ref[:, :RANK]
    count = jnp.where(careful, SWEEPS, 1)

    def sweep(step, carry):
        @pl.when(jnp.logical_not(careful))
        def _():
            images = [imaged_ref[...] for _, imaged_ref, _ in work]
            for again in range(SWEEPS - 1):
                images = [dot_split(gram_ref[...], x, 1, 0) for x, (gram_ref, _, _) in zip(images, work)]
            for x, (_, imaged_ref, _) in zip(images, work):
                imaged_ref[...] = x

        inners = [dot(imaged_ref[...], imaged_ref[...], 0, 0) for _, imaged_ref, _ in work]
        for inner, (factor, pivots), (_, imaged_ref, frame_ref) in zip(inners, inverse_factors(inners), work):
            frame_ref[...] = dot(imaged_ref[...], factor, 1, 1)
            sound_ref[...] = jnp.where(pivots > PIVOT_SHARE * diagonal_of(inner), sound_ref[...], 0.0)

        @pl.when(step + 1 < count)
        def _():
            for gram_ref, imaged_ref, frame_ref in work:
                imaged_ref[...] = dot(gram_ref[...], frame_ref[...], 1, 0)

        return carry

    lax.fori_loop(0, count, sweep, 0)
    return [frame_ref[...].astype(bf16) for _, _, frame_ref in work]


def until_sound(sound_ref, attempt, idle=False):
    def once(mode):
        sound_ref[...] = jnp.ones(sound_ref.shape, f32)
        attempt(mode == 1)
        sound = jnp.min(sound_ref[...]) > 0.5
        return jnp.where(jnp.logical_or(jnp.logical_or(mode == 1, idle), sound), 2, 1)

    lax.while_loop(lambda mode: mode < 2, once, jnp.int32(0))


sound_shape = [pltpu.VMEM((RANK, RANK), f32)]
work_shapes = [pltpu.VMEM((2 * RANK, 2 * RANK), f32)] + [pltpu.VMEM((2 * RANK, RANK), f32)] * 2


def place(pos_ref):
    pos = pos_ref[0]
    return pos % 2, pos // PLANE % PLANES


def split(blocks, core, mine_ref, theirs_ref):
    half = mine_ref.shape[1]
    for b, block in enumerate(blocks):
        low, high = block[:half, :], block[half:, :]
        mine_ref[b] = jnp.where(core == 1, high, low)
        theirs_ref[b] = jnp.where(core == 1, low, high)


def joined(mine_ref, other_ref, core, b):
    mine, other = mine_ref[b], other_ref[b]
    low = jnp.where(core == 1, other, mine)
    high = jnp.where(core == 1, mine, other)
    return jnp.concatenate([low, high], 0)


def chunk(z, m, width):
    return pl.ds(pl.multiple_of((z ^ m) * width, width), width)


def in_middle(z):
    return jnp.logical_or(z == MIDDLE[0], z == MIDDLE[1])


def side(z, far, width):
    return pl.ds(pl.multiple_of(((z // 2) ^ far) * width, width), width)


def member(pos_ref):
    return pos_ref[0] % PLANE


def parts_kernel(pos_ref, x_ref, *refs):
    width = refs[0].shape[1]
    for ref, m in zip(refs, PLANE_ORDER):
        ref[...] = x_ref[:, chunk(member(pos_ref), m, width)]


def gram_kernel(pos_ref, *refs):
    parts, (rows_ref, mine_ref, theirs_ref) = refs[:PLANE], refs[PLANE:]
    core, _ = place(pos_ref)
    height = parts[0].shape[0]
    for ref, m in zip(parts, PLANE_ORDER):
        rows_ref[chunk(member(pos_ref), m, height), :] = ref[...]
    rows = rows_ref[...]
    gram = dot_low(rows, rows, 1, 1)
    split([gram[:RANK, :RANK], gram[RANK:, :RANK], gram[RANK:, RANK:]], core, mine_ref, theirs_ref)


def square(a, b, d):
    return jnp.concatenate([jnp.concatenate([a, b.T], 1), jnp.concatenate([b, d], 1)], 0)


def plane_gram(mine_ref, other_ref, core):
    return square(*[joined(mine_ref, other_ref, core, b) for b in range(3)])


def node_kernel(pos_ref, mine_ref, other_ref, rows_ref, *refs):
    sides, low_ref, sound_ref, work = refs[:2], refs[2], refs[3], refs[4:]
    core, z = place(pos_ref)
    width = sides[0].shape[1]

    def attempt(careful):
        gram = plane_gram(mine_ref, other_ref, core)
        scale = unit_scale([gram[:RANK, :RANK], gram[RANK:, RANK:]])
        (low,) = leading_spaces([gram], scale, [work], careful, sound_ref)
        low_ref[...] = low
        for far, ref in enumerate(sides):
            ref[...] = dot_low(low, rows_ref[:, side(z, far, width)], 0, 0).astype(bf16)

    until_sound(sound_ref, attempt)


def reduced(gram, low):
    return dot_split(low, dot_split(gram, low, 1, 0), 0, 0)


def diag_kernel(pos_ref, mine_ref, other_ref, low_ref, diag_ref):
    core, _ = place(pos_ref)
    diag = reduced(plane_gram(mine_ref, other_ref, core), low_ref[...])
    half = diag_ref.shape[1]
    diag_ref[0] = jnp.where(core == 1, diag[half:, :], diag[:half, :]).astype(diag_ref.dtype)


PAIRS = [(i, j) for i in range(PLANES) for j in range(i + 1, PLANES)]


def cross_kernel(pos_ref, *refs):
    nodes, (mine_ref, theirs_ref, all_ref) = refs[:PLANES], refs[PLANES:]
    core, z = place(pos_ref)
    for m, ref in enumerate(nodes):
        all_ref[z ^ m] = ref[...]
    split([dot_low(all_ref[j], all_ref[i], 1, 1) for i, j in PAIRS], core, mine_ref, theirs_ref)


def top_kernel(pos_ref, mine_ref, other_ref, *refs):
    nodes, (top_ref, gram_ref, low_ref), refs = refs[:PLANES], refs[PLANES : PLANES + 3], refs[PLANES + 3 :]
    all_ref, diag_ref, sound_ref, work = refs[0], refs[1], refs[2], [refs[3:6], refs[6:9]]
    core, z = place(pos_ref)
    for m, ref in enumerate(nodes):
        all_ref[z ^ m] = ref[...]
        diag_ref[z ^ m] = joined(mine_ref, other_ref, core, len(PAIRS) + m)

    def attempt(careful):
        cross = {pair: joined(mine_ref, other_ref, core, b) for b, pair in enumerate(PAIRS)}
        scale = unit_scale([diag_ref[y] for y in range(PLANES)])
        grams = [square(diag_ref[i], cross[i, j], diag_ref[j]) for i, j in ((0, 1), (2, 3))]
        low_a, low_b = leading_spaces(grams, scale, work, careful, sound_ref)
        between = jnp.concatenate(
            [
                jnp.concatenate([cross[0, 2], cross[1, 2]], 1),
                jnp.concatenate([cross[0, 3], cross[1, 3]], 1),
            ],
            0,
        )
        gram = square(
            reduced(grams[0], low_a),
            dot_split(low_b, dot_split(between, low_a, 1, 0), 0, 0),
            reduced(grams[1], low_b),
        )
        gram_ref[...] = gram
        node_a = dot_low(low_a, jnp.concatenate([all_ref[0], all_ref[1]], 0), 0, 0).astype(bf16)
        node_b = dot_low(low_b, jnp.concatenate([all_ref[2], all_ref[3]], 0), 0, 0).astype(bf16)
        (low,) = leading_spaces([gram], scale, work[:1], careful, sound_ref)
        low_ref[...] = low
        top_ref[...] = dot_low(low, jnp.concatenate([node_a, node_b], 0), 0, 0).astype(bf16)

    until_sound(sound_ref, attempt, jnp.logical_not(in_middle(z)))


def factor_kernel(gram_ref, low_ref, factor_ref):
    factor_ref[...] = inverse_factors([reduced(gram_ref[...], low_ref[...])])[0][0]


def halves_of_top(z, own_ref, near_ref, far_outer_ref, far_ref):
    middle = in_middle(z)
    return jnp.where(middle, own_ref[...], near_ref[...]), jnp.where(middle, far_ref[...], far_outer_ref[...])


def coeffs_kernel(pos_ref, rows_ref, *refs):
    tops, (mine_ref, theirs_ref) = refs[:PLANES], refs[PLANES:]
    core, z = place(pos_ref)
    near, far = halves_of_top(z, *tops)
    width = near.shape[1]
    total = dot_low(rows_ref[:, side(z, 0, width)], near, 1, 1)
    total = total + dot_low(rows_ref[:, side(z, 1, width)], far, 1, 1)
    split([total], core, mine_ref, theirs_ref)


def project_kernel(pos_ref, mine_ref, other_ref, own_factor_ref, factor_ref, *refs):
    tops, outs, solved_ref = refs[:PLANES], refs[PLANES:-1], refs[-1]
    core, z = place(pos_ref)
    factor = jnp.where(in_middle(z), own_factor_ref[...], factor_ref[...])
    height = outs[0].shape[0]
    solved_ref[...] = dot(dot(joined(mine_ref, other_ref, core, 0), factor, 1, 1), factor, 1, 0)
    solved = [solved_ref[chunk(member(pos_ref), m, height), :] for m in PLANE_ORDER]
    solved = jnp.concatenate(solved, 0).astype(bf16)
    for far, top in enumerate(halves_of_top(z, *tops)):
        made = dot_low(solved, top, 1, 0).astype(bf16)
        for k in range(PLANE):
            outs[k][:, side(z, far, top.shape[1])] = made[k * height : (k + 1) * height, :]


def whole_kernel(pos_ref, *refs):
    parts, out_ref = refs[:PLANE], refs[PLANE]
    width = parts[0].shape[1]
    for ref, m in zip(parts, PLANE_ORDER):
        out_ref[:, chunk(member(pos_ref), m, width)] = ref[...]


smem = pl.BlockSpec(memory_space=pltpu.SMEM)
vmem = pl.BlockSpec(memory_space=pltpu.VMEM)


def kernel(fn, outs, *args, scratch=(), scalar=True):
    single = not isinstance(outs, (list, tuple))
    shapes = [outs] if single else list(outs)
    res = pl.pallas_call(
        fn,
        out_shape=[jax.ShapeDtypeStruct(s, d) for s, d in shapes] if not single else None,
        in_specs=[smem if scalar and i == 0 else vmem for i in range(len(args))],
        out_specs=[vmem for _ in shapes],
        scratch_shapes=list(scratch),
        compiler_params=pltpu.CompilerParams(vmem_limit_bytes=40 * 2**20),
        name=fn.__name__,
    )(*args)
    return res


def body(mortality):
    count = lax.axis_size("cols")
    pos = lax.axis_index("cols").astype(jnp.int32).reshape(1)

    def swap(x, apart):
        return lax.ppermute(x, "cols", [(i, i ^ apart) for i in range(count)])

    def swap_all(parts, order, unit=1):
        return [x if m == 0 else swap(x, unit * m) for x, m in zip(parts, order)]

    def send(x, apart, from_middle):
        starts = [i for i in range(count) if (i // PLANE % PLANES in MIDDLE) == from_middle]
        return lax.ppermute(x, "cols", [(i, i ^ apart * PLANE) for i in starts])

    def sum4(parts):
        parts = [p.astype(f32) for p in parts]
        return (parts[0] + parts[1]) + (parts[2] + parts[3])

    def plane_sum(mine, theirs):
        return sum4(swap_all([(mine + swap(theirs, 1)).astype(bf16)] * 4, range(4), 2))

    block, total = mortality.shape
    height, width = block * PLANE, total // PLANE
    part = width // len(MIDDLE)
    half = RANK // 2

    parts = kernel(parts_kernel, [((block, width), bf16)] * PLANE, pos, mortality)
    parts = swap_all(parts, PLANE_ORDER)
    rows, mine, theirs = kernel(
        gram_kernel, [((height, width), bf16)] + [((3, half, RANK), f32)] * 2, pos, *parts
    )
    mine = plane_sum(mine, theirs)
    other = swap(mine, 1)
    near, far, low = kernel(
        node_kernel,
        [((RANK, part), bf16)] * 2 + [((2 * RANK, RANK), bf16)],
        pos, mine, other, rows,
        scratch=sound_shape + work_shapes,
    )
    nodes = [near, send(near, 1, False), send(far, 2, False), send(far, 3, True)]
    (diag,) = kernel(diag_kernel, [((1, half, RANK), bf16)], pos, mine, other, low)

    mine, theirs = kernel(
        cross_kernel,
        [((len(PAIRS), half, RANK), f32)] * 2,
        pos, *nodes,
        scratch=[pltpu.VMEM((PLANES, RANK, part), bf16)],
    )
    mine = plane_sum(mine, theirs)
    diags = [diag, send(diag, 1, False), send(diag, 2, False)]
    mine, diags = lax.optimization_barrier((mine, diags))
    both = jnp.concatenate([mine.astype(bf16), diags[0]], 0)
    beyond = send(both, 3, True)
    mine = both[: len(PAIRS)].astype(f32) + beyond[: len(PAIRS)].astype(f32)
    mine = jnp.concatenate([mine] + [x.astype(f32) for x in diags + [beyond[len(PAIRS) :]]], 0)
    top, gram, low = kernel(
        top_kernel,
        [((RANK, part), bf16), ((2 * RANK, 2 * RANK), f32), ((2 * RANK, RANK), bf16)],
        pos, mine, swap(mine, 1), *nodes,
        scratch=[pltpu.VMEM((PLANES, RANK, part), bf16), pltpu.VMEM((PLANES, RANK, RANK), f32)]
        + sound_shape
        + work_shapes * 2,
    )
    tops = [top, send(top, 1, True), send(top, 2, True), send(top, 3, True)]
    (factor,) = kernel(factor_kernel, [((RANK, RANK), f32)], gram, low, scalar=False)

    near_factor = send(factor, 1, True)
    factor, tops = lax.optimization_barrier((factor, tops))

    mine, theirs = kernel(coeffs_kernel, [((1, height // 2, RANK), f32)] * 2, pos, rows, *tops)
    mine = plane_sum(mine, theirs)
    outs = kernel(
        project_kernel,
        [((block, width), bf16)] * PLANE,
        pos, mine, swap(mine, 1), factor, near_factor, *tops,
        scratch=[pltpu.VMEM((height, RANK), f32)],
    )
    (result,) = kernel(whole_kernel, [((block, total), bf16)], pos, *swap_all(outs, PLANE_ORDER))
    return result


def solution(mesh):
    in_specs = (P("cols", None),)
    out_specs = P("cols", None)
    return jax.shard_map(body, mesh=mesh, in_specs=in_specs, out_specs=out_specs, check_vma=False)
```

```python
import functools

import jax
import jax.numpy as jnp
from jax import lax
from jax.experimental import pallas as pl
from jax.experimental.pallas import tpu as pltpu
from jax.sharding import PartitionSpec as P

RANK = 128
LEVELS = 5
SWEEPS = 3
PLANE = 8
PLANES = 2**LEVELS // PLANE
TILE = 8
PANEL = 64
PLANE_ORDER = (6, 7, 2, 4, 3, 5, 1, 0)
TREE_ORDER = (0, 3, 2, 1)
PIVOT_SHARE = 2e-4

precise = lax.Precision.HIGHEST
f32 = jnp.float32
bf16 = jnp.bfloat16


def iota2(shape, dim):
    return lax.broadcasted_iota(jnp.int32, shape, dim)


def dot(a, b, ca, cb, precision=precise):
    return lax.dot_general(a, b, (((ca,), (cb,)), ((), ())), precision=precision, preferred_element_type=f32)


def dot_low(a, b, ca, cb):
    return dot(a, b, ca, cb, None)


def halves(x):
    high = x.astype(bf16)
    return high, (x - high.astype(f32)).astype(bf16)


def dot_split(a, b, ca, cb):
    ah, al = (a, None) if a.dtype == bf16 else halves(a)
    bh, bl = (b, None) if b.dtype == bf16 else halves(b)
    total = dot_low(ah, bh, ca, cb)
    if bl is not None:
        total = total + dot_low(ah, bl, ca, cb)
    return total if al is None else total + dot_low(al, bh, ca, cb)


def lanes_of(x, k):
    return jnp.broadcast_to(x[:, k : k + 1], x.shape)


def rows_of(x, s):
    return jnp.broadcast_to(x[s : s + 1, :], x.shape)


def eliminate(sets, first, ahead):
    lane = iota2((TILE, RANK), 1)
    sub = iota2((TILE, RANK), 0)
    count = len(sets[0])
    early = [None] * len(sets)
    pivots = [[] for _ in sets]
    for t in range(count):
        g = TILE * (first + t)
        spread, coming = [], []
        for n, tiles in enumerate(sets):
            cols = {} if early[n] is None else {t: early[n]}
            for i in range(t + len(cols), count):
                cols[i] = [lanes_of(tiles[i], g + j) for j in range(TILE)]
            spread.append(cols)
            near = (t, t + 1) if ahead and t + 1 < count else ()
            coming.append({i: [lanes_of(tiles[i], g + TILE + j) for j in range(TILE)] for i in near})
            pivots[n].append(jnp.zeros((TILE, RANK), f32))
        for k in range(TILE):
            here = lane == g + k
            for tiles, cols, look, held in zip(sets, spread, coming, pivots):
                pivot_row = [rows_of(cols[t][j], k) if j >= k else None for j in range(TILE)]
                held[t] = jnp.where(sub == k, pivot_row[k], held[t])
                inv = 1.0 / pivot_row[k]
                scaled = [pivot_row[j] * inv if j > k else None for j in range(TILE)]
                row = jnp.where(here, 1.0, rows_of(tiles[t], k)) * inv
                look_row = [rows_of(x, k) * inv for x in look[t]] if look else None
                for i in range(t, count):
                    col = cols[i][k]
                    if i == t:
                        col = jnp.where(sub > k, col, 0.0)
                        kept = jnp.where(here & (sub > k), 0.0, tiles[i])
                    else:
                        kept = jnp.where(here, 0.0, tiles[i])
                    for j in range(k + 1, TILE):
                        cols[i][j] = cols[i][j] - col * scaled[j]
                    tiles[i] = kept - col * row
                    if i in look:
                        look[i] = [x - col * y for x, y in zip(look[i], look_row)]
        early = [look.get(t + 1) for look in coming]
    return list(zip(sets, pivots))


def inverse_factors(matrices):
    alone = len(matrices) == 1
    size = PANEL if alone else PANEL // 2
    rests = list(matrices)
    done = [[] for _ in rests]
    for lo in range(0, RANK, size):
        hi = lo + size
        sets = [[rest[TILE * t : TILE * t + TILE, :] for t in range(size // TILE)] for rest in rests]
        r = iota2((size, RANK), 0) + lo
        c = iota2((size, RANK), 1)
        for n, (tiles, pivots) in enumerate(eliminate(sets, lo // TILE, alone)):
            panel = jnp.concatenate(tiles, 0)
            pivots = jnp.concatenate(pivots, 0)
            unit = jnp.where(r > c, panel, jnp.where(r == c, 1.0, 0.0))
            done[n].append((unit * lax.rsqrt(pivots), pivots))
            if hi == RANK:
                continue
            rows = jnp.where(r == c, 1.0, jnp.where((c > r) & (c < hi), 0.0, panel))
            tail = rests[n][size:, :]
            at = iota2(tail.shape, 1)
            tail = jnp.where((at >= lo) & (at < hi), 0.0, tail)
            rests[n] = tail - dot(panel * (1.0 / pivots), rows, 0, 0)[hi:, :]
    return [tuple(jnp.concatenate(x, 0) for x in zip(*panels)) for panels in done]


def diagonal_of(x):
    return jnp.sum(jnp.where(iota2(x.shape, 0) == iota2(x.shape, 1), x, 0.0), 1, keepdims=True)


def unit_scale(blocks):
    largest = diagonal_of(blocks[0])
    for x in blocks[1:]:
        largest = jnp.maximum(largest, diagonal_of(x))
    return 1.0 / jnp.max(largest, keepdims=True)


def leading_spaces(grams, scale, work, careful, sound_ref):
    for gram, (gram_ref, imaged_ref, _) in zip(grams, work):
        gram_ref[...] = gram * scale
        imaged_ref[...] = gram_ref[:, :RANK]
    count = jnp.where(careful, SWEEPS, 1)

    def sweep(step, carry):
        @pl.when(jnp.logical_not(careful))
        def _():
            images = [imaged_ref[...] for _, imaged_ref, _ in work]
            for again in range(SWEEPS - 1):
                images = [dot_split(gram_ref[...], x, 1, 0) for x, (gram_ref, _, _) in zip(images, work)]
            for x, (_, imaged_ref, _) in zip(images, work):
                imaged_ref[...] = x

        inners = [dot(imaged_ref[...], imaged_ref[...], 0, 0) for _, imaged_ref, _ in work]
        for inner, (factor, pivots), (_, imaged_ref, frame_ref) in zip(inners, inverse_factors(inners), work):
            frame_ref[...] = dot(imaged_ref[...], factor, 1, 1)
            sound_ref[...] = jnp.where(pivots > PIVOT_SHARE * diagonal_of(inner), sound_ref[...], 0.0)

        @pl.when(step + 1 < count)
        def _():
            for gram_ref, imaged_ref, frame_ref in work:
                imaged_ref[...] = dot(gram_ref[...], frame_ref[...], 1, 0)

        return carry

    lax.fori_loop(0, count, sweep, 0)
    return [frame_ref[...].astype(bf16) for _, _, frame_ref in work]


def until_sound(sound_ref, attempt):
    def once(mode):
        sound_ref[...] = jnp.ones(sound_ref.shape, f32)
        attempt(mode == 1)
        sound = jnp.min(sound_ref[...]) > 0.5
        return jnp.where(jnp.logical_or(mode == 1, sound), 2, 1)

    lax.while_loop(lambda mode: mode < 2, once, jnp.int32(0))


sound_shape = [pltpu.VMEM((RANK, RANK), f32)]
work_shapes = [pltpu.VMEM((2 * RANK, 2 * RANK), f32)] + [pltpu.VMEM((2 * RANK, RANK), f32)] * 2


def place(pos_ref):
    pos = pos_ref[0]
    return pos % 2, pos // PLANE % PLANES


def split(blocks, core, mine_ref, theirs_ref):
    half = mine_ref.shape[1]
    for b, block in enumerate(blocks):
        low, high = block[:half, :], block[half:, :]
        mine_ref[b] = jnp.where(core == 1, high, low)
        theirs_ref[b] = jnp.where(core == 1, low, high)


def joined(mine_ref, other_ref, core, b):
    mine, other = mine_ref[b].astype(f32), other_ref[b].astype(f32)
    low = jnp.where(core == 1, other, mine)
    high = jnp.where(core == 1, mine, other)
    return jnp.concatenate([low, high], 0)


def chunk(z, m, width):
    return pl.ds(pl.multiple_of((z ^ m) * width, width), width)


def member(pos_ref):
    return pos_ref[0] % PLANE


def copy_all(copies):
    for c in copies:
        c.start()
    for c in copies:
        c.wait()


def parts_kernel(order, pos_ref, x_ref, *refs):
    parts, sems = refs[:-1], refs[-1]
    where = [x_ref.at[:, chunk(member(pos_ref), m, parts[0].shape[1])] for m in order]
    copy_all([pltpu.make_async_copy(w, part, sems.at[k]) for k, (w, part) in enumerate(zip(where, parts))])


def gram_kernel(pos_ref, *refs):
    parts, (rows_ref, mine_ref, theirs_ref) = refs[:PLANE], refs[PLANE:]
    core, _ = place(pos_ref)
    height = parts[0].shape[0]
    for ref, m in zip(parts, PLANE_ORDER):
        rows_ref[chunk(member(pos_ref), m, height), :] = ref[...]
    rows = rows_ref[...]
    gram = dot_low(rows, rows, 1, 1)
    split([gram[:RANK, :RANK], gram[RANK:, :RANK], gram[RANK:, RANK:]], core, mine_ref, theirs_ref)


def square(a, b, d):
    return jnp.concatenate([jnp.concatenate([a, b.T], 1), jnp.concatenate([b, d], 1)], 0)


def plane_gram(mine_ref, other_ref, core):
    return square(*[joined(mine_ref, other_ref, core, b) for b in range(3)])


def node_kernel(pos_ref, mine_ref, other_ref, rows_ref, *refs):
    nodes, low_ref, sound_ref, work = refs[:PLANES], refs[PLANES], refs[PLANES + 1], refs[PLANES + 2 :]
    core, z = place(pos_ref)
    width = nodes[0].shape[1]

    def attempt(careful):
        gram = plane_gram(mine_ref, other_ref, core)
        scale = unit_scale([gram[:RANK, :RANK], gram[RANK:, RANK:]])
        (low,) = leading_spaces([gram], scale, [work], careful, sound_ref)
        low_ref[...] = low
        for ref, m in zip(nodes, TREE_ORDER):
            ref[...] = dot_low(low, rows_ref[:, chunk(z, m, width)], 0, 0).astype(bf16)

    until_sound(sound_ref, attempt)


def reduced(gram, low):
    return dot_split(low, dot_split(gram, low, 1, 0), 0, 0)


def diag_kernel(pos_ref, mine_ref, other_ref, low_ref, diag_ref):
    core, _ = place(pos_ref)
    diag = reduced(plane_gram(mine_ref, other_ref, core), low_ref[...])
    half = diag_ref.shape[1]
    diag_ref[0] = jnp.where(core == 1, diag[half:, :], diag[:half, :]).astype(diag_ref.dtype)


PAIRS = [(i, j) for i in range(PLANES) for j in range(i + 1, PLANES)]


def cross_kernel(pos_ref, *refs):
    nodes, (mine_ref, theirs_ref, all_ref) = refs[:PLANES], refs[PLANES:]
    core, z = place(pos_ref)
    for ref, m in zip(nodes, TREE_ORDER):
        all_ref[z ^ m] = ref[...]
    split([dot_low(all_ref[j], all_ref[i], 1, 1) for i, j in PAIRS], core, mine_ref, theirs_ref)


def top_kernel(pos_ref, mine_ref, other_ref, *refs):
    nodes, (top_ref, gram_ref, low_ref), refs = refs[:PLANES], refs[PLANES : PLANES + 3], refs[PLANES + 3 :]
    all_ref, diag_ref, sound_ref, work = refs[0], refs[1], refs[2], [refs[3:6], refs[6:9]]
    core, z = place(pos_ref)
    for ref, m in zip(nodes, TREE_ORDER):
        all_ref[z ^ m] = ref[...]
        diag_ref[z ^ m] = joined(mine_ref, other_ref, core, len(PAIRS) + m)

    def attempt(careful):
        cross = {pair: joined(mine_ref, other_ref, core, b) for b, pair in enumerate(PAIRS)}
        scale = unit_scale([diag_ref[y] for y in range(PLANES)])
        grams = [square(diag_ref[i], cross[i, j], diag_ref[j]) for i, j in ((0, 1), (2, 3))]
        low_a, low_b = leading_spaces(grams, scale, work, careful, sound_ref)
        between = jnp.concatenate(
            [
                jnp.concatenate([cross[0, 2], cross[1, 2]], 1),
                jnp.concatenate([cross[0, 3], cross[1, 3]], 1),
            ],
            0,
        )
        gram = square(
            reduced(grams[0], low_a),
            dot_split(low_b, dot_split(between, low_a, 1, 0), 0, 0),
            reduced(grams[1], low_b),
        )
        gram_ref[...] = gram
        node_a = dot_low(low_a, jnp.concatenate([all_ref[0], all_ref[1]], 0), 0, 0).astype(bf16)
        node_b = dot_low(low_b, jnp.concatenate([all_ref[2], all_ref[3]], 0), 0, 0).astype(bf16)
        (low,) = leading_spaces([gram], scale, work[:1], careful, sound_ref)
        low_ref[...] = low
        top_ref[...] = dot_low(low, jnp.concatenate([node_a, node_b], 0), 0, 0).astype(bf16)

    until_sound(sound_ref, attempt)


def factor_kernel(gram_ref, low_ref, factor_ref):
    factor_ref[...] = inverse_factors([reduced(gram_ref[...], low_ref[...])])[0][0]


def coeffs_kernel(pos_ref, rows_ref, factor_ref, *refs):
    tops, (mine_ref, theirs_ref) = refs[:PLANES], refs[PLANES:]
    core, z = place(pos_ref)
    width = tops[0].shape[1]
    total = None
    for m, ref in enumerate(tops):
        part = dot_low(rows_ref[:, chunk(z, m, width)], ref[...], 1, 1)
        total = part if total is None else total + part
    split([dot(total, factor_ref[...], 1, 1)], core, mine_ref, theirs_ref)


def project_kernel(pos_ref, mine_ref, other_ref, factor_ref, *refs):
    tops, outs, solved_ref = refs[:PLANES], refs[PLANES:-1], refs[-1]
    core, z = place(pos_ref)
    height, width = outs[0].shape[0], tops[0].shape[1]
    solved_ref[...] = dot(joined(mine_ref, other_ref, core, 0), factor_ref[...], 1, 0)
    solved = [solved_ref[chunk(member(pos_ref), m, height), :] for m in PLANE_ORDER]
    solved = jnp.concatenate(solved, 0).astype(bf16)
    for m, ref in enumerate(tops):
        made = dot_low(solved, ref[...], 1, 0).astype(bf16)
        for k in range(PLANE):
            outs[k][:, chunk(z, m, width)] = made[k * height : (k + 1) * height, :]


def whole_kernel(order, pos_ref, *refs):
    parts, out_ref, sems = refs[: len(order)], refs[-2], refs[-1]
    where = [out_ref.at[:, chunk(member(pos_ref), m, parts[0].shape[1])] for m in order]
    copy_all([pltpu.make_async_copy(part, w, sems.at[k]) for k, (w, part) in enumerate(zip(where, parts))])


smem = pl.BlockSpec(memory_space=pltpu.SMEM)
vmem = pl.BlockSpec(memory_space=pltpu.VMEM)
hbm = pl.BlockSpec(memory_space=pltpu.HBM)


def kernel(fn, outs, *args, scratch=(), scalar=True):
    return pl.pallas_call(
        fn,
        out_shape=[jax.ShapeDtypeStruct(s, d) for s, d in outs],
        in_specs=[smem if scalar and i == 0 else vmem for i in range(len(args))],
        out_specs=[vmem for _ in outs],
        scratch_shapes=list(scratch),
        compiler_params=pltpu.CompilerParams(vmem_limit_bytes=40 * 2**20),
        name=fn.__name__,
    )(*args)


def read_parts(order, pos, x, width):
    return pl.pallas_call(
        functools.partial(parts_kernel, order),
        out_shape=[jax.ShapeDtypeStruct((x.shape[0], width), x.dtype) for _ in order],
        in_specs=[smem, hbm],
        out_specs=[vmem for _ in order],
        scratch_shapes=[pltpu.SemaphoreType.DMA((len(order),))],
        compiler_params=pltpu.CompilerParams(vmem_limit_bytes=40 * 2**20),
        name="parts_kernel",
    )(pos, pltpu.with_memory_space_constraint(x, pltpu.HBM))


def write_parts(order, pos, parts, shape, before=None):
    earlier = [] if before is None else [before]
    return pl.pallas_call(
        functools.partial(whole_kernel, order),
        out_shape=jax.ShapeDtypeStruct(shape, parts[0].dtype),
        in_specs=[smem] + [vmem] * len(parts) + [hbm] * len(earlier),
        out_specs=hbm,
        scratch_shapes=[pltpu.SemaphoreType.DMA((len(order),))],
        input_output_aliases={} if before is None else {len(parts) + 1: 0},
        compiler_params=pltpu.CompilerParams(vmem_limit_bytes=40 * 2**20),
        name="whole_kernel",
    )(pos, *parts, *earlier)


def body(mortality):
    count = lax.axis_size("cols")
    pos = lax.axis_index("cols").astype(jnp.int32).reshape(1)

    def swap(x, apart):
        return lax.ppermute(x, "cols", [(i, i ^ apart) for i in range(count)])

    def swap_all(parts, order, unit=1):
        return [x if m == 0 else swap(x, unit * m) for x, m in zip(parts, order)]

    def sum4(parts):
        parts = [p.astype(f32) for p in parts]
        return (parts[0] + parts[1]) + (parts[2] + parts[3])

    def plane_sum(mine, theirs):
        return sum4(swap_all([(mine + swap(theirs, 1)).astype(bf16)] * 4, range(4), 2)).astype(bf16)

    block, total = mortality.shape
    height, width = block * PLANE, total // PLANE
    part = width // PLANES
    half = RANK // 2

    early, late = PLANE_ORDER[:4], PLANE_ORDER[4:]
    parts = read_parts(early, pos, mortality, width)
    parts, after = lax.optimization_barrier((parts, pos))
    parts = parts + read_parts(late, after, mortality, width)
    parts = swap_all(parts, PLANE_ORDER)
    rows, mine, theirs = kernel(
        gram_kernel, [((height, width), bf16)] + [((3, half, RANK), f32)] * 2, pos, *parts
    )
    mine = plane_sum(mine, theirs)
    other = swap(mine, 1)
    *nodes, low = kernel(
        node_kernel,
        [((RANK, part), bf16)] * PLANES + [((2 * RANK, RANK), bf16)],
        pos, mine, other, rows,
        scratch=sound_shape + work_shapes,
    )
    nodes = swap_all(nodes, TREE_ORDER, PLANE)
    (diag,) = kernel(diag_kernel, [((1, half, RANK), bf16)], pos, mine, other, low)

    mine, theirs = kernel(
        cross_kernel,
        [((len(PAIRS), half, RANK), f32)] * 2,
        pos, *nodes,
        scratch=[pltpu.VMEM((PLANES, RANK, part), bf16)],
    )
    mine = plane_sum(mine, theirs)
    both = swap_all([jnp.concatenate([mine, diag], 0)] * PLANES, range(PLANES), PLANE)
    total_cross = sum4([x[: len(PAIRS)] for x in both]).astype(bf16)
    mine = jnp.concatenate([total_cross] + [x[len(PAIRS) :] for x in both], 0)
    top, gram, low = kernel(
        top_kernel,
        [((RANK, part), bf16), ((2 * RANK, 2 * RANK), f32), ((2 * RANK, RANK), bf16)],
        pos, mine, swap(mine, 1), *nodes,
        scratch=[pltpu.VMEM((PLANES, RANK, part), bf16), pltpu.VMEM((PLANES, RANK, RANK), f32)]
        + sound_shape
        + work_shapes * 2,
    )
    tops = swap_all([top] * PLANES, range(PLANES), PLANE)
    (factor,) = kernel(factor_kernel, [((RANK, RANK), f32)], gram, low, scalar=False)

    mine, theirs = kernel(coeffs_kernel, [((1, height // 2, RANK), f32)] * 2, pos, rows, factor, *tops)
    mine = plane_sum(mine, theirs)
    outs = kernel(
        project_kernel,
        [((block, width), bf16)] * PLANE,
        pos, mine, swap(mine, 1), factor, *tops,
        scratch=[pltpu.VMEM((height, RANK), f32)],
    )
    outs = swap_all(outs, PLANE_ORDER)
    early, late = PLANE_ORDER[:3] + PLANE_ORDER[-1:], PLANE_ORDER[3:-1]
    result = write_parts(early, pos, outs[:3] + outs[-1:], (block, total))
    return write_parts(late, pos, outs[3:-1], (block, total), result)


def solution(mesh):
    in_specs = (P("cols", None),)
    out_specs = P("cols", None)
    return jax.shard_map(body, mesh=mesh, in_specs=in_specs, out_specs=out_specs, check_vma=False)
```

```python
import jax
import jax.numpy as jnp
from jax import lax
from jax.experimental import pallas as pl
from jax.experimental.pallas import tpu as pltpu
from jax.sharding import PartitionSpec as P

RANK = 128
LEVELS = 5
SWEEPS = 3
PLANE = 8
PLANES = 2**LEVELS // PLANE
TILE = 8
PANEL = 64
PLANE_ORDER = (0, 6, 7, 2, 4, 3, 5, 1)
TREE_ORDER = (0, 2, 3, 1)
SUM_ORDER = (0, 1, 3, 2)
PIVOT_SHARE = 2e-4

precise = lax.Precision.HIGHEST
f32 = jnp.float32
bf16 = jnp.bfloat16


def iota2(shape, dim):
    return lax.broadcasted_iota(jnp.int32, shape, dim)


def dot(a, b, ca, cb, precision=precise):
    return lax.dot_general(a, b, (((ca,), (cb,)), ((), ())), precision=precision, preferred_element_type=f32)


def dot_low(a, b, ca, cb):
    return dot(a, b, ca, cb, None)


def halves(x):
    high = x.astype(bf16)
    return high, (x - high.astype(f32)).astype(bf16)


def dot_split(a, b, ca, cb):
    ah, al = (a, None) if a.dtype == bf16 else halves(a)
    bh, bl = (b, None) if b.dtype == bf16 else halves(b)
    total = dot_low(ah, bh, ca, cb)
    if bl is not None:
        total = total + dot_low(ah, bl, ca, cb)
    return total if al is None else total + dot_low(al, bh, ca, cb)


def lanes_of(x, k):
    return jnp.broadcast_to(x[:, k : k + 1], x.shape)


def rows_of(x, s):
    return jnp.broadcast_to(x[s : s + 1, :], x.shape)


def eliminate(sets, first, ahead):
    lane = iota2((TILE, RANK), 1)
    sub = iota2((TILE, RANK), 0)
    count = len(sets[0])
    early = [None] * len(sets)
    pivots = [[] for _ in sets]
    for t in range(count):
        g = TILE * (first + t)
        spread, coming = [], []
        for n, tiles in enumerate(sets):
            cols = {} if early[n] is None else {t: early[n]}
            for i in range(t + len(cols), count):
                cols[i] = [lanes_of(tiles[i], g + j) for j in range(TILE)]
            spread.append(cols)
            near = (t, t + 1) if ahead and t + 1 < count else ()
            coming.append({i: [lanes_of(tiles[i], g + TILE + j) for j in range(TILE)] for i in near})
            pivots[n].append(jnp.zeros((TILE, RANK), f32))
        for k in range(TILE):
            here = lane == g + k
            for tiles, cols, look, held in zip(sets, spread, coming, pivots):
                pivot_row = [rows_of(cols[t][j], k) if j >= k else None for j in range(TILE)]
                held[t] = jnp.where(sub == k, pivot_row[k], held[t])
                inv = 1.0 / pivot_row[k]
                scaled = [pivot_row[j] * inv if j > k else None for j in range(TILE)]
                row = jnp.where(here, 1.0, rows_of(tiles[t], k)) * inv
                look_row = [rows_of(x, k) * inv for x in look[t]] if look else None
                for i in range(t, count):
                    col = cols[i][k]
                    if i == t:
                        col = jnp.where(sub > k, col, 0.0)
                        kept = jnp.where(here & (sub > k), 0.0, tiles[i])
                    else:
                        kept = jnp.where(here, 0.0, tiles[i])
                    for j in range(k + 1, TILE):
                        cols[i][j] = cols[i][j] - col * scaled[j]
                    tiles[i] = kept - col * row
                    if i in look:
                        look[i] = [x - col * y for x, y in zip(look[i], look_row)]
        early = [look.get(t + 1) for look in coming]
    return list(zip(sets, pivots))


def inverse_factors(matrices):
    alone = len(matrices) == 1
    size = PANEL if alone else PANEL // 2
    rests = list(matrices)
    done = [[] for _ in rests]
    for lo in range(0, RANK, size):
        hi = lo + size
        sets = [[rest[TILE * t : TILE * t + TILE, :] for t in range(size // TILE)] for rest in rests]
        r = iota2((size, RANK), 0) + lo
        c = iota2((size, RANK), 1)
        for n, (tiles, pivots) in enumerate(eliminate(sets, lo // TILE, alone)):
            panel = jnp.concatenate(tiles, 0)
            pivots = jnp.concatenate(pivots, 0)
            unit = jnp.where(r > c, panel, jnp.where(r == c, 1.0, 0.0))
            done[n].append((unit * lax.rsqrt(pivots), pivots))
            if hi == RANK:
                continue
            rows = jnp.where(r == c, 1.0, jnp.where((c > r) & (c < hi), 0.0, panel))
            tail = rests[n][size:, :]
            at = iota2(tail.shape, 1)
            tail = jnp.where((at >= lo) & (at < hi), 0.0, tail)
            rests[n] = tail - dot(panel * (1.0 / pivots), rows, 0, 0)[hi:, :]
    return [tuple(jnp.concatenate(x, 0) for x in zip(*panels)) for panels in done]


def diagonal_of(x):
    return jnp.sum(jnp.where(iota2(x.shape, 0) == iota2(x.shape, 1), x, 0.0), 1, keepdims=True)


def unit_scale(blocks):
    largest = diagonal_of(blocks[0])
    for x in blocks[1:]:
        largest = jnp.maximum(largest, diagonal_of(x))
    return 1.0 / jnp.max(largest, keepdims=True)


def leading_spaces(grams, scale, work, careful, sound_ref):
    for gram, (gram_ref, imaged_ref, _) in zip(grams, work):
        gram_ref[...] = gram * scale
        imaged_ref[...] = gram_ref[:, :RANK]
    count = jnp.where(careful, SWEEPS, 1)

    def sweep(step, carry):
        @pl.when(jnp.logical_not(careful))
        def _():
            images = [imaged_ref[...] for _, imaged_ref, _ in work]
            for again in range(SWEEPS - 1):
                images = [dot_split(gram_ref[...], x, 1, 0) for x, (gram_ref, _, _) in zip(images, work)]
            for x, (_, imaged_ref, _) in zip(images, work):
                imaged_ref[...] = x

        inners = [dot(imaged_ref[...], imaged_ref[...], 0, 0) for _, imaged_ref, _ in work]
        for inner, (factor, pivots), (_, imaged_ref, frame_ref) in zip(inners, inverse_factors(inners), work):
            frame_ref[...] = dot(imaged_ref[...], factor, 1, 1)
            sound_ref[...] = jnp.where(pivots > PIVOT_SHARE * diagonal_of(inner), sound_ref[...], 0.0)

        @pl.when(step + 1 < count)
        def _():
            for gram_ref, imaged_ref, frame_ref in work:
                imaged_ref[...] = dot(gram_ref[...], frame_ref[...], 1, 0)

        return carry

    lax.fori_loop(0, count, sweep, 0)
    return [frame_ref[...].astype(bf16) for _, _, frame_ref in work]


def until_sound(sound_ref, attempt):
    def once(mode):
        sound_ref[...] = jnp.ones(sound_ref.shape, f32)
        attempt(mode == 1)
        sound = jnp.min(sound_ref[...]) > 0.5
        return jnp.where(jnp.logical_or(mode == 1, sound), 2, 1)

    lax.while_loop(lambda mode: mode < 2, once, jnp.int32(0))


sound_shape = [pltpu.VMEM((RANK, RANK), f32)]
work_shapes = [pltpu.VMEM((2 * RANK, 2 * RANK), f32)] + [pltpu.VMEM((2 * RANK, RANK), f32)] * 2


def place(pos_ref):
    pos = pos_ref[0]
    return pos % 2, pos // PLANE % PLANES


def split(blocks, core, mine_ref, theirs_ref):
    half = mine_ref.shape[1]
    for b, block in enumerate(blocks):
        low, high = block[:half, :], block[half:, :]
        mine_ref[b] = jnp.where(core == 1, high, low)
        theirs_ref[b] = jnp.where(core == 1, low, high)


def joined(mine_ref, other_ref, core, b):
    mine, other = mine_ref[b], other_ref[b]
    low = jnp.where(core == 1, other, mine)
    high = jnp.where(core == 1, mine, other)
    return jnp.concatenate([low, high], 0)


def chunk(z, m, width):
    return pl.ds(pl.multiple_of((z ^ m) * width, width), width)


def member(pos_ref):
    return pos_ref[0] % PLANE


def parts_kernel(pos_ref, x_ref, *refs):
    width = refs[0].shape[1]
    for ref, m in zip(refs, PLANE_ORDER):
        ref[...] = x_ref[:, chunk(member(pos_ref), m, width)]


def gram_kernel(pos_ref, *refs):
    parts, (rows_ref, mine_ref, theirs_ref) = refs[:PLANE], refs[PLANE:]
    core, _ = place(pos_ref)
    height = parts[0].shape[0]
    for ref, m in zip(parts, PLANE_ORDER):
        rows_ref[chunk(member(pos_ref), m, height), :] = ref[...]
    rows = rows_ref[...]
    gram = dot_low(rows, rows, 1, 1)
    split([gram[:RANK, :RANK], gram[RANK:, :RANK], gram[RANK:, RANK:]], core, mine_ref, theirs_ref)


def square(a, b, d):
    return jnp.concatenate([jnp.concatenate([a, b.T], 1), jnp.concatenate([b, d], 1)], 0)


def plane_gram(mine_ref, other_ref, core):
    return square(*[joined(mine_ref, other_ref, core, b) for b in range(3)])


def node_kernel(pos_ref, mine_ref, other_ref, rows_ref, *refs):
    nodes, low_ref, sound_ref, work = refs[:PLANES], refs[PLANES], refs[PLANES + 1], refs[PLANES + 2 :]
    core, z = place(pos_ref)
    width = nodes[0].shape[1]

    def attempt(careful):
        gram = plane_gram(mine_ref, other_ref, core)
        scale = unit_scale([gram[:RANK, :RANK], gram[RANK:, RANK:]])
        (low,) = leading_spaces([gram], scale, [work], careful, sound_ref)
        low_ref[...] = low
        for ref, m in zip(nodes, TREE_ORDER):
            ref[...] = dot_low(low, rows_ref[:, chunk(z, m, width)], 0, 0).astype(bf16)

    until_sound(sound_ref, attempt)


def reduced(gram, low):
    return dot_split(low, dot_split(gram, low, 1, 0), 0, 0)


def diag_kernel(pos_ref, mine_ref, other_ref, low_ref, diag_ref):
    core, _ = place(pos_ref)
    diag = reduced(plane_gram(mine_ref, other_ref, core), low_ref[...])
    half = diag_ref.shape[1]
    diag_ref[0] = jnp.where(core == 1, diag[half:, :], diag[:half, :]).astype(diag_ref.dtype)


PAIRS = [(i, j) for i in range(PLANES) for j in range(i + 1, PLANES)]


def cross_kernel(pos_ref, *refs):
    nodes, (mine_ref, theirs_ref, all_ref) = refs[:PLANES], refs[PLANES:]
    core, z = place(pos_ref)
    for ref, m in zip(nodes, TREE_ORDER):
        all_ref[z ^ m] = ref[...]
    split([dot_low(all_ref[j], all_ref[i], 1, 1) for i, j in PAIRS], core, mine_ref, theirs_ref)


def top_kernel(pos_ref, mine_ref, other_ref, *refs):
    nodes, (top_ref, gram_ref, low_ref), refs = refs[:PLANES], refs[PLANES : PLANES + 3], refs[PLANES + 3 :]
    all_ref, diag_ref, sound_ref, work = refs[0], refs[1], refs[2], [refs[3:6], refs[6:9]]
    core, z = place(pos_ref)
    for ref, m in zip(nodes, TREE_ORDER):
        all_ref[z ^ m] = ref[...]
        diag_ref[z ^ m] = joined(mine_ref, other_ref, core, len(PAIRS) + SUM_ORDER.index(m))

    def attempt(careful):
        cross = {pair: joined(mine_ref, other_ref, core, b) for b, pair in enumerate(PAIRS)}
        scale = unit_scale([diag_ref[y] for y in range(PLANES)])
        grams = [square(diag_ref[i], cross[i, j], diag_ref[j]) for i, j in ((0, 1), (2, 3))]
        low_a, low_b = leading_spaces(grams, scale, work, careful, sound_ref)
        between = jnp.concatenate(
            [
                jnp.concatenate([cross[0, 2], cross[1, 2]], 1),
                jnp.concatenate([cross[0, 3], cross[1, 3]], 1),
            ],
            0,
        )
        gram = square(
            reduced(grams[0], low_a),
            dot_split(low_b, dot_split(between, low_a, 1, 0), 0, 0),
            reduced(grams[1], low_b),
        )
        gram_ref[...] = gram
        node_a = dot_low(low_a, jnp.concatenate([all_ref[0], all_ref[1]], 0), 0, 0).astype(bf16)
        node_b = dot_low(low_b, jnp.concatenate([all_ref[2], all_ref[3]], 0), 0, 0).astype(bf16)
        (low,) = leading_spaces([gram], scale, work[:1], careful, sound_ref)
        low_ref[...] = low
        top_ref[...] = dot_low(low, jnp.concatenate([node_a, node_b], 0), 0, 0).astype(bf16)

    until_sound(sound_ref, attempt)


def factor_kernel(gram_ref, low_ref, factor_ref):
    factor_ref[...] = inverse_factors([reduced(gram_ref[...], low_ref[...])])[0][0]


def coeffs_kernel(pos_ref, rows_ref, factor_ref, *refs):
    tops, (mine_ref, theirs_ref) = refs[:PLANES], refs[PLANES:]
    core, z = place(pos_ref)
    width = tops[0].shape[1]
    total = None
    for m, ref in zip(SUM_ORDER, tops):
        part = dot_low(rows_ref[:, chunk(z, m, width)], ref[...], 1, 1)
        total = part if total is None else total + part
    split([dot(total, factor_ref[...], 1, 1)], core, mine_ref, theirs_ref)


def project_kernel(pos_ref, mine_ref, other_ref, factor_ref, *refs):
    tops, outs, solved_ref = refs[:PLANES], refs[PLANES:-1], refs[-1]
    core, z = place(pos_ref)
    height, width = outs[0].shape[0], tops[0].shape[1]
    solved_ref[...] = dot(joined(mine_ref, other_ref, core, 0), factor_ref[...], 1, 0)
    solved = [solved_ref[chunk(member(pos_ref), m, height), :] for m in PLANE_ORDER]
    solved = jnp.concatenate(solved, 0).astype(bf16)
    for m, ref in zip(SUM_ORDER, tops):
        made = dot_low(solved, ref[...], 1, 0).astype(bf16)
        for k in range(PLANE):
            outs[k][:, chunk(z, m, width)] = made[k * height : (k + 1) * height, :]


def whole_kernel(pos_ref, *refs):
    parts, out_ref = refs[:PLANE], refs[PLANE]
    width = parts[0].shape[1]
    for ref, m in zip(parts, PLANE_ORDER):
        out_ref[:, chunk(member(pos_ref), m, width)] = ref[...]


smem = pl.BlockSpec(memory_space=pltpu.SMEM)
vmem = pl.BlockSpec(memory_space=pltpu.VMEM)


def kernel(fn, outs, *args, scratch=(), scalar=True):
    single = not isinstance(outs, (list, tuple))
    shapes = [outs] if single else list(outs)
    res = pl.pallas_call(
        fn,
        out_shape=[jax.ShapeDtypeStruct(s, d) for s, d in shapes] if not single else None,
        in_specs=[smem if scalar and i == 0 else vmem for i in range(len(args))],
        out_specs=[vmem for _ in shapes],
        scratch_shapes=list(scratch),
        compiler_params=pltpu.CompilerParams(vmem_limit_bytes=40 * 2**20),
        name=fn.__name__,
    )(*args)
    return res


def body(mortality):
    count = lax.axis_size("cols")
    pos = lax.axis_index("cols").astype(jnp.int32).reshape(1)

    def swap(x, apart):
        return lax.ppermute(x, "cols", [(i, i ^ apart) for i in range(count)])

    def swap_all(parts, order, unit=1):
        return [x if m == 0 else swap(x, unit * m) for x, m in zip(parts, order)]

    def sum4(parts):
        parts = [p.astype(f32) for p in parts]
        return (parts[0] + parts[1]) + (parts[2] + parts[3])

    def plane_sum(mine, theirs):
        return sum4(swap_all([(mine + swap(theirs, 1)).astype(bf16)] * 4, range(4), 2))

    block, total = mortality.shape
    height, width = block * PLANE, total // PLANE
    part = width // PLANES
    half = RANK // 2

    parts = kernel(parts_kernel, [((block, width), bf16)] * PLANE, pos, mortality)
    parts = swap_all(parts, PLANE_ORDER)
    rows, mine, theirs = kernel(
        gram_kernel, [((height, width), bf16)] + [((3, half, RANK), f32)] * 2, pos, *parts
    )
    mine = plane_sum(mine, theirs)
    other = swap(mine, 1)
    *nodes, low = kernel(
        node_kernel,
        [((RANK, part), bf16)] * PLANES + [((2 * RANK, RANK), bf16)],
        pos, mine, other, rows,
        scratch=sound_shape + work_shapes,
    )
    nodes = swap_all(nodes, TREE_ORDER, PLANE)
    (diag,) = kernel(diag_kernel, [((1, half, RANK), bf16)], pos, mine, other, low)

    mine, theirs = kernel(
        cross_kernel,
        [((len(PAIRS), half, RANK), f32)] * 2,
        pos, *nodes,
        scratch=[pltpu.VMEM((PLANES, RANK, part), bf16)],
    )
    mine = plane_sum(mine, theirs)
    both = swap_all([jnp.concatenate([mine.astype(bf16), diag], 0)] * PLANES, SUM_ORDER, PLANE)
    mine = jnp.concatenate([sum4([x[: len(PAIRS)] for x in both])] + [x[len(PAIRS) :].astype(f32) for x in both], 0)
    top, gram, low = kernel(
        top_kernel,
        [((RANK, part), bf16), ((2 * RANK, 2 * RANK), f32), ((2 * RANK, RANK), bf16)],
        pos, mine, swap(mine, 1), *nodes,
        scratch=[pltpu.VMEM((PLANES, RANK, part), bf16), pltpu.VMEM((PLANES, RANK, RANK), f32)]
        + sound_shape
        + work_shapes * 2,
    )
    tops = swap_all([top] * PLANES, SUM_ORDER, PLANE)
    (factor,) = kernel(factor_kernel, [((RANK, RANK), f32)], gram, low, scalar=False)

    mine, theirs = kernel(coeffs_kernel, [((1, height // 2, RANK), f32)] * 2, pos, rows, factor, *tops)
    mine = plane_sum(mine, theirs)
    outs = kernel(
        project_kernel,
        [((block, width), bf16)] * PLANE,
        pos, mine, swap(mine, 1), factor, *tops,
        scratch=[pltpu.VMEM((height, RANK), f32)],
    )
    (result,) = kernel(whole_kernel, [((block, total), bf16)], pos, *swap_all(outs, PLANE_ORDER))
    return result


def solution(mesh):
    in_specs = (P("cols", None),)
    out_specs = P("cols", None)
    return jax.shard_map(body, mesh=mesh, in_specs=in_specs, out_specs=out_specs, check_vma=False)
```

```python
import jax
import jax.numpy as jnp
from jax import lax
from jax.experimental import pallas as pl
from jax.experimental.pallas import tpu as pltpu
from jax.sharding import PartitionSpec as P

RANK = 128
LEVELS = 5
SWEEPS = 3
PLANE = 8
PLANES = 2**LEVELS // PLANE
TILE = 8
PANEL = 64
PLANE_ORDER = (0, 6, 7, 2, 4, 3, 5, 1)
TREE_ORDER = (0, 2, 3, 1)
TOP_ORDER = (0, 1, 3, 2)
PIVOT_SHARE = 2e-4

precise = lax.Precision.HIGHEST
f32 = jnp.float32
bf16 = jnp.bfloat16


def iota2(shape, dim):
    return lax.broadcasted_iota(jnp.int32, shape, dim)


def dot(a, b, ca, cb, precision=precise):
    return lax.dot_general(a, b, (((ca,), (cb,)), ((), ())), precision=precision, preferred_element_type=f32)


def dot_low(a, b, ca, cb):
    return dot(a, b, ca, cb, None)


def halves(x):
    high = x.astype(bf16)
    return high, (x - high.astype(f32)).astype(bf16)


def dot_split(a, b, ca, cb):
    ah, al = (a, None) if a.dtype == bf16 else halves(a)
    bh, bl = (b, None) if b.dtype == bf16 else halves(b)
    total = dot_low(ah, bh, ca, cb)
    if bl is not None:
        total = total + dot_low(ah, bl, ca, cb)
    return total if al is None else total + dot_low(al, bh, ca, cb)


def lanes_of(x, k):
    return jnp.broadcast_to(x[:, k : k + 1], x.shape)


def rows_of(x, s):
    return jnp.broadcast_to(x[s : s + 1, :], x.shape)


def eliminate(sets, first, ahead):
    lane = iota2((TILE, RANK), 1)
    sub = iota2((TILE, RANK), 0)
    count = len(sets[0])
    early = [None] * len(sets)
    pivots = [[] for _ in sets]
    for t in range(count):
        g = TILE * (first + t)
        spread, coming = [], []
        for n, tiles in enumerate(sets):
            cols = {} if early[n] is None else {t: early[n]}
            for i in range(t + len(cols), count):
                cols[i] = [lanes_of(tiles[i], g + j) for j in range(TILE)]
            spread.append(cols)
            near = (t, t + 1) if ahead and t + 1 < count else ()
            coming.append({i: [lanes_of(tiles[i], g + TILE + j) for j in range(TILE)] for i in near})
            pivots[n].append(jnp.zeros((TILE, RANK), f32))
        for k in range(TILE):
            here = lane == g + k
            for tiles, cols, look, held in zip(sets, spread, coming, pivots):
                pivot_row = [rows_of(cols[t][j], k) if j >= k else None for j in range(TILE)]
                held[t] = jnp.where(sub == k, pivot_row[k], held[t])
                inv = 1.0 / pivot_row[k]
                scaled = [pivot_row[j] * inv if j > k else None for j in range(TILE)]
                row = jnp.where(here, 1.0, rows_of(tiles[t], k)) * inv
                look_row = [rows_of(x, k) * inv for x in look[t]] if look else None
                for i in range(t, count):
                    col = cols[i][k]
                    if i == t:
                        col = jnp.where(sub > k, col, 0.0)
                        kept = jnp.where(here & (sub > k), 0.0, tiles[i])
                    else:
                        kept = jnp.where(here, 0.0, tiles[i])
                    for j in range(k + 1, TILE):
                        cols[i][j] = cols[i][j] - col * scaled[j]
                    tiles[i] = kept - col * row
                    if i in look:
                        look[i] = [x - col * y for x, y in zip(look[i], look_row)]
        early = [look.get(t + 1) for look in coming]
    return list(zip(sets, pivots))


def inverse_factors(matrices):
    alone = len(matrices) == 1
    size = PANEL if alone else PANEL // 2
    rests = list(matrices)
    done = [[] for _ in rests]
    for lo in range(0, RANK, size):
        hi = lo + size
        sets = [[rest[TILE * t : TILE * t + TILE, :] for t in range(size // TILE)] for rest in rests]
        r = iota2((size, RANK), 0) + lo
        c = iota2((size, RANK), 1)
        for n, (tiles, pivots) in enumerate(eliminate(sets, lo // TILE, alone)):
            panel = jnp.concatenate(tiles, 0)
            pivots = jnp.concatenate(pivots, 0)
            unit = jnp.where(r > c, panel, jnp.where(r == c, 1.0, 0.0))
            done[n].append((unit * lax.rsqrt(pivots), pivots))
            if hi == RANK:
                continue
            rows = jnp.where(r == c, 1.0, jnp.where((c > r) & (c < hi), 0.0, panel))
            tail = rests[n][size:, :]
            at = iota2(tail.shape, 1)
            tail = jnp.where((at >= lo) & (at < hi), 0.0, tail)
            rests[n] = tail - dot(panel * (1.0 / pivots), rows, 0, 0)[hi:, :]
    return [tuple(jnp.concatenate(x, 0) for x in zip(*panels)) for panels in done]


def diagonal_of(x):
    return jnp.sum(jnp.where(iota2(x.shape, 0) == iota2(x.shape, 1), x, 0.0), 1, keepdims=True)


def unit_scale(blocks):
    largest = diagonal_of(blocks[0])
    for x in blocks[1:]:
        largest = jnp.maximum(largest, diagonal_of(x))
    return 1.0 / jnp.max(largest, keepdims=True)


def leading_spaces(grams, scale, work, careful, sound_ref):
    for gram, (gram_ref, imaged_ref, _) in zip(grams, work):
        gram_ref[...] = gram * scale
        imaged_ref[...] = gram_ref[:, :RANK]
    count = jnp.where(careful, SWEEPS, 1)

    def sweep(step, carry):
        @pl.when(jnp.logical_not(careful))
        def _():
            images = [imaged_ref[...] for _, imaged_ref, _ in work]
            for again in range(SWEEPS - 1):
                images = [dot_split(gram_ref[...], x, 1, 0) for x, (gram_ref, _, _) in zip(images, work)]
            for x, (_, imaged_ref, _) in zip(images, work):
                imaged_ref[...] = x

        inners = [dot(imaged_ref[...], imaged_ref[...], 0, 0) for _, imaged_ref, _ in work]
        for inner, (factor, pivots), (_, imaged_ref, frame_ref) in zip(inners, inverse_factors(inners), work):
            frame_ref[...] = dot(imaged_ref[...], factor, 1, 1)
            sound_ref[...] = jnp.where(pivots > PIVOT_SHARE * diagonal_of(inner), sound_ref[...], 0.0)

        @pl.when(step + 1 < count)
        def _():
            for gram_ref, imaged_ref, frame_ref in work:
                imaged_ref[...] = dot(gram_ref[...], frame_ref[...], 1, 0)

        return carry

    lax.fori_loop(0, count, sweep, 0)
    return [frame_ref[...].astype(bf16) for _, _, frame_ref in work]


def until_sound(sound_ref, attempt):
    def once(mode):
        sound_ref[...] = jnp.ones(sound_ref.shape, f32)
        attempt(mode == 1)
        sound = jnp.min(sound_ref[...]) > 0.5
        return jnp.where(jnp.logical_or(mode == 1, sound), 2, 1)

    lax.while_loop(lambda mode: mode < 2, once, jnp.int32(0))


sound_shape = [pltpu.VMEM((RANK, RANK), f32)]
work_shapes = [pltpu.VMEM((2 * RANK, 2 * RANK), f32)] + [pltpu.VMEM((2 * RANK, RANK), f32)] * 2


def place(pos_ref):
    pos = pos_ref[0]
    return pos % 2, pos // PLANE % PLANES


def split(blocks, core, mine_ref, theirs_ref):
    half = mine_ref.shape[1]
    for b, block in enumerate(blocks):
        low, high = block[:half, :], block[half:, :]
        mine_ref[b] = jnp.where(core == 1, high, low)
        theirs_ref[b] = jnp.where(core == 1, low, high)


def joined(mine_ref, other_ref, core, b):
    mine, other = mine_ref[b], other_ref[b]
    low = jnp.where(core == 1, other, mine)
    high = jnp.where(core == 1, mine, other)
    return jnp.concatenate([low, high], 0)


def chunk(z, m, width):
    return pl.ds(pl.multiple_of((z ^ m) * width, width), width)


def member(pos_ref):
    return pos_ref[0] % PLANE


def parts_kernel(pos_ref, x_ref, *refs):
    width = refs[0].shape[1]
    for ref, m in zip(refs, PLANE_ORDER):
        ref[...] = x_ref[:, chunk(member(pos_ref), m, width)]


def gram_kernel(pos_ref, *refs):
    parts, (rows_ref, mine_ref, theirs_ref) = refs[:PLANE], refs[PLANE:]
    core, _ = place(pos_ref)
    height = parts[0].shape[0]
    for ref, m in zip(parts, PLANE_ORDER):
        rows_ref[chunk(member(pos_ref), m, height), :] = ref[...]
    rows = rows_ref[...]
    gram = dot_low(rows, rows, 1, 1)
    split([gram[:RANK, :RANK], gram[RANK:, :RANK], gram[RANK:, RANK:]], core, mine_ref, theirs_ref)


def square(a, b, d):
    return jnp.concatenate([jnp.concatenate([a, b.T], 1), jnp.concatenate([b, d], 1)], 0)


def plane_gram(mine_ref, other_ref, core):
    return square(*[joined(mine_ref, other_ref, core, b) for b in range(3)])


def node_kernel(pos_ref, mine_ref, other_ref, rows_ref, *refs):
    nodes, low_ref, sound_ref, work = refs[:PLANES], refs[PLANES], refs[PLANES + 1], refs[PLANES + 2 :]
    core, z = place(pos_ref)
    width = nodes[0].shape[1]

    def attempt(careful):
        gram = plane_gram(mine_ref, other_ref, core)
        scale = unit_scale([gram[:RANK, :RANK], gram[RANK:, RANK:]])
        (low,) = leading_spaces([gram], scale, [work], careful, sound_ref)
        low_ref[...] = low
        for ref, m in zip(nodes, TREE_ORDER):
            ref[...] = dot_low(low, rows_ref[:, chunk(z, m, width)], 0, 0).astype(bf16)

    until_sound(sound_ref, attempt)


def reduced(gram, low):
    return dot_split(low, dot_split(gram, low, 1, 0), 0, 0)


def diag_kernel(pos_ref, mine_ref, other_ref, low_ref, diag_ref):
    core, _ = place(pos_ref)
    diag = reduced(plane_gram(mine_ref, other_ref, core), low_ref[...])
    half = diag_ref.shape[1]
    diag_ref[0] = jnp.where(core == 1, diag[half:, :], diag[:half, :]).astype(diag_ref.dtype)


PAIRS = [(i, j) for i in range(PLANES) for j in range(i + 1, PLANES)]


def cross_kernel(pos_ref, *refs):
    nodes, (mine_ref, theirs_ref, all_ref) = refs[:PLANES], refs[PLANES:]
    core, z = place(pos_ref)
    for ref, m in zip(nodes, TREE_ORDER):
        all_ref[z ^ m] = ref[...]
    split([dot_low(all_ref[j], all_ref[i], 1, 1) for i, j in PAIRS], core, mine_ref, theirs_ref)


def top_kernel(pos_ref, mine_ref, other_ref, *refs):
    nodes, (top_ref, gram_ref, low_ref), refs = refs[:PLANES], refs[PLANES : PLANES + 3], refs[PLANES + 3 :]
    all_ref, diag_ref, sound_ref, work = refs[0], refs[1], refs[2], [refs[3:6], refs[6:9]]
    core, z = place(pos_ref)
    for ref, m in zip(nodes, TREE_ORDER):
        all_ref[z ^ m] = ref[...]
        diag_ref[z ^ m] = joined(mine_ref, other_ref, core, len(PAIRS) + m)

    def attempt(careful):
        cross = {pair: joined(mine_ref, other_ref, core, b) for b, pair in enumerate(PAIRS)}
        scale = unit_scale([diag_ref[y] for y in range(PLANES)])
        grams = [square(diag_ref[i], cross[i, j], diag_ref[j]) for i, j in ((0, 1), (2, 3))]
        low_a, low_b = leading_spaces(grams, scale, work, careful, sound_ref)
        between = jnp.concatenate(
            [
                jnp.concatenate([cross[0, 2], cross[1, 2]], 1),
                jnp.concatenate([cross[0, 3], cross[1, 3]], 1),
            ],
            0,
        )
        gram = square(
            reduced(grams[0], low_a),
            dot_split(low_b, dot_split(between, low_a, 1, 0), 0, 0),
            reduced(grams[1], low_b),
        )
        gram_ref[...] = gram
        node_a = dot_low(low_a, jnp.concatenate([all_ref[0], all_ref[1]], 0), 0, 0).astype(bf16)
        node_b = dot_low(low_b, jnp.concatenate([all_ref[2], all_ref[3]], 0), 0, 0).astype(bf16)
        (low,) = leading_spaces([gram], scale, work[:1], careful, sound_ref)
        low_ref[...] = low
        top_ref[...] = dot_low(low, jnp.concatenate([node_a, node_b], 0), 0, 0).astype(bf16)

    until_sound(sound_ref, attempt)


def factor_kernel(gram_ref, low_ref, factor_ref):
    factor_ref[...] = inverse_factors([reduced(gram_ref[...], low_ref[...])])[0][0]


def coeffs_kernel(pos_ref, rows_ref, factor_ref, *refs):
    tops, (mine_ref, theirs_ref) = refs[:PLANES], refs[PLANES:]
    core, z = place(pos_ref)
    width = tops[0].shape[1]
    total = None
    for m, ref in zip(TOP_ORDER, tops):
        part = dot_low(rows_ref[:, chunk(z, m, width)], ref[...], 1, 1)
        total = part if total is None else total + part
    split([dot(total, factor_ref[...], 1, 1)], core, mine_ref, theirs_ref)


def project_kernel(pos_ref, mine_ref, other_ref, factor_ref, *refs):
    tops, outs, solved_ref = refs[:PLANES], refs[PLANES:-1], refs[-1]
    core, z = place(pos_ref)
    height, width = outs[0].shape[0], tops[0].shape[1]
    solved_ref[...] = dot(joined(mine_ref, other_ref, core, 0), factor_ref[...], 1, 0)
    solved = [solved_ref[chunk(member(pos_ref), m, height), :] for m in PLANE_ORDER]
    solved = jnp.concatenate(solved, 0).astype(bf16)
    for m, ref in zip(TOP_ORDER, tops):
        made = dot_low(solved, ref[...], 1, 0).astype(bf16)
        for k in range(PLANE):
            outs[k][:, chunk(z, m, width)] = made[k * height : (k + 1) * height, :]


def whole_kernel(pos_ref, *refs):
    parts, out_ref = refs[:PLANE], refs[PLANE]
    width = parts[0].shape[1]
    for ref, m in zip(parts, PLANE_ORDER):
        out_ref[:, chunk(member(pos_ref), m, width)] = ref[...]


smem = pl.BlockSpec(memory_space=pltpu.SMEM)
vmem = pl.BlockSpec(memory_space=pltpu.VMEM)


def kernel(fn, outs, *args, scratch=(), scalar=True):
    single = not isinstance(outs, (list, tuple))
    shapes = [outs] if single else list(outs)
    res = pl.pallas_call(
        fn,
        out_shape=[jax.ShapeDtypeStruct(s, d) for s, d in shapes] if not single else None,
        in_specs=[smem if scalar and i == 0 else vmem for i in range(len(args))],
        out_specs=[vmem for _ in shapes],
        scratch_shapes=list(scratch),
        compiler_params=pltpu.CompilerParams(vmem_limit_bytes=40 * 2**20),
        name=fn.__name__,
    )(*args)
    return res


def body(mortality):
    count = lax.axis_size("cols")
    pos = lax.axis_index("cols").astype(jnp.int32).reshape(1)

    def swap(x, apart):
        return lax.ppermute(x, "cols", [(i, i ^ apart) for i in range(count)])

    def swap_all(parts, order, unit=1):
        return [x if m == 0 else swap(x, unit * m) for x, m in zip(parts, order)]

    def sum4(parts):
        parts = [p.astype(f32) for p in parts]
        return (parts[0] + parts[1]) + (parts[2] + parts[3])

    def plane_sum(mine, theirs):
        return sum4(swap_all([(mine + swap(theirs, 1)).astype(bf16)] * 4, range(4), 2))

    block, total = mortality.shape
    height, width = block * PLANE, total // PLANE
    part = width // PLANES
    half = RANK // 2

    parts = kernel(parts_kernel, [((block, width), bf16)] * PLANE, pos, mortality)
    parts = swap_all(parts, PLANE_ORDER)
    rows, mine, theirs = kernel(
        gram_kernel, [((height, width), bf16)] + [((3, half, RANK), f32)] * 2, pos, *parts
    )
    mine = plane_sum(mine, theirs)
    other = swap(mine, 1)
    *nodes, low = kernel(
        node_kernel,
        [((RANK, part), bf16)] * PLANES + [((2 * RANK, RANK), bf16)],
        pos, mine, other, rows,
        scratch=sound_shape + work_shapes,
    )
    nodes = swap_all(nodes, TREE_ORDER, PLANE)
    (diag,) = kernel(diag_kernel, [((1, half, RANK), bf16)], pos, mine, other, low)

    mine, theirs = kernel(
        cross_kernel,
        [((len(PAIRS), half, RANK), f32)] * 2,
        pos, *nodes,
        scratch=[pltpu.VMEM((PLANES, RANK, part), bf16)],
    )
    mine = plane_sum(mine, theirs)
    both = swap_all([jnp.concatenate([mine.astype(bf16), diag], 0)] * PLANES, range(PLANES), PLANE)
    mine = jnp.concatenate([sum4([x[: len(PAIRS)] for x in both])] + [x[len(PAIRS) :].astype(f32) for x in both], 0)
    top, gram, low = kernel(
        top_kernel,
        [((RANK, part), bf16), ((2 * RANK, 2 * RANK), f32), ((2 * RANK, RANK), bf16)],
        pos, mine, swap(mine, 1), *nodes,
        scratch=[pltpu.VMEM((PLANES, RANK, part), bf16), pltpu.VMEM((PLANES, RANK, RANK), f32)]
        + sound_shape
        + work_shapes * 2,
    )
    tops = swap_all([top] * PLANES, TOP_ORDER, PLANE)
    (factor,) = kernel(factor_kernel, [((RANK, RANK), f32)], gram, low, scalar=False)

    mine, theirs = kernel(coeffs_kernel, [((1, height // 2, RANK), f32)] * 2, pos, rows, factor, *tops)
    mine = plane_sum(mine, theirs)
    outs = kernel(
        project_kernel,
        [((block, width), bf16)] * PLANE,
        pos, mine, swap(mine, 1), factor, *tops,
        scratch=[pltpu.VMEM((height, RANK), f32)],
    )
    (result,) = kernel(whole_kernel, [((block, total), bf16)], pos, *swap_all(outs, PLANE_ORDER))
    return result


def solution(mesh):
    in_specs = (P("cols", None),)
    out_specs = P("cols", None)
    return jax.shard_map(body, mesh=mesh, in_specs=in_specs, out_specs=out_specs, check_vma=False)
```

```python
import jax
import jax.numpy as jnp
from jax import lax
from jax.experimental import pallas as pl
from jax.experimental.pallas import tpu as pltpu
from jax.sharding import PartitionSpec as P

RANK = 128
LEVELS = 5
SWEEPS = 3
PLANE = 8
PLANES = 2**LEVELS // PLANE
TILE = 8
PANEL = 64
PLANE_ORDER = (0, 2, 4, 6, 7, 3, 5, 1)
TREE_ORDER = (0, 2, 3, 1)
SUM_ORDER = (0, 1, 3, 2)
PIVOT_SHARE = 2e-4

precise = lax.Precision.HIGHEST
f32 = jnp.float32
bf16 = jnp.bfloat16


def iota2(shape, dim):
    return lax.broadcasted_iota(jnp.int32, shape, dim)


def dot(a, b, ca, cb, precision=precise):
    return lax.dot_general(a, b, (((ca,), (cb,)), ((), ())), precision=precision, preferred_element_type=f32)


def dot_low(a, b, ca, cb):
    return dot(a, b, ca, cb, None)


def halves(x):
    high = x.astype(bf16)
    return high, (x - high.astype(f32)).astype(bf16)


def dot_split(a, b, ca, cb):
    ah, al = (a, None) if a.dtype == bf16 else halves(a)
    bh, bl = (b, None) if b.dtype == bf16 else halves(b)
    total = dot_low(ah, bh, ca, cb)
    if bl is not None:
        total = total + dot_low(ah, bl, ca, cb)
    return total if al is None else total + dot_low(al, bh, ca, cb)


def lanes_of(x, k):
    return jnp.broadcast_to(x[:, k : k + 1], x.shape)


def rows_of(x, s):
    return jnp.broadcast_to(x[s : s + 1, :], x.shape)


def eliminate(sets, first, ahead):
    lane = iota2((TILE, RANK), 1)
    sub = iota2((TILE, RANK), 0)
    count = len(sets[0])
    early = [None] * len(sets)
    pivots = [[] for _ in sets]
    for t in range(count):
        g = TILE * (first + t)
        spread, coming = [], []
        for n, tiles in enumerate(sets):
            cols = {} if early[n] is None else {t: early[n]}
            for i in range(t + len(cols), count):
                cols[i] = [lanes_of(tiles[i], g + j) for j in range(TILE)]
            spread.append(cols)
            near = (t, t + 1) if ahead and t + 1 < count else ()
            coming.append({i: [lanes_of(tiles[i], g + TILE + j) for j in range(TILE)] for i in near})
            pivots[n].append(jnp.zeros((TILE, RANK), f32))
        for k in range(TILE):
            here = lane == g + k
            for tiles, cols, look, held in zip(sets, spread, coming, pivots):
                pivot_row = [rows_of(cols[t][j], k) if j >= k else None for j in range(TILE)]
                held[t] = jnp.where(sub == k, pivot_row[k], held[t])
                inv = 1.0 / pivot_row[k]
                scaled = [pivot_row[j] * inv if j > k else None for j in range(TILE)]
                row = jnp.where(here, 1.0, rows_of(tiles[t], k)) * inv
                look_row = [rows_of(x, k) * inv for x in look[t]] if look else None
                for i in range(t, count):
                    col = cols[i][k]
                    if i == t:
                        col = jnp.where(sub > k, col, 0.0)
                        kept = jnp.where(here & (sub > k), 0.0, tiles[i])
                    else:
                        kept = jnp.where(here, 0.0, tiles[i])
                    for j in range(k + 1, TILE):
                        cols[i][j] = cols[i][j] - col * scaled[j]
                    tiles[i] = kept - col * row
                    if i in look:
                        look[i] = [x - col * y for x, y in zip(look[i], look_row)]
        early = [look.get(t + 1) for look in coming]
    return list(zip(sets, pivots))


def inverse_factors(matrices):
    alone = len(matrices) == 1
    size = PANEL if alone else PANEL // 2
    rests = list(matrices)
    done = [[] for _ in rests]
    for lo in range(0, RANK, size):
        hi = lo + size
        sets = [[rest[TILE * t : TILE * t + TILE, :] for t in range(size // TILE)] for rest in rests]
        r = iota2((size, RANK), 0) + lo
        c = iota2((size, RANK), 1)
        for n, (tiles, pivots) in enumerate(eliminate(sets, lo // TILE, alone)):
            panel = jnp.concatenate(tiles, 0)
            pivots = jnp.concatenate(pivots, 0)
            unit = jnp.where(r > c, panel, jnp.where(r == c, 1.0, 0.0))
            done[n].append((unit * lax.rsqrt(pivots), pivots))
            if hi == RANK:
                continue
            rows = jnp.where(r == c, 1.0, jnp.where((c > r) & (c < hi), 0.0, panel))
            tail = rests[n][size:, :]
            at = iota2(tail.shape, 1)
            tail = jnp.where((at >= lo) & (at < hi), 0.0, tail)
            rests[n] = tail - dot(panel * (1.0 / pivots), rows, 0, 0)[hi:, :]
    return [tuple(jnp.concatenate(x, 0) for x in zip(*panels)) for panels in done]


def diagonal_of(x):
    return jnp.sum(jnp.where(iota2(x.shape, 0) == iota2(x.shape, 1), x, 0.0), 1, keepdims=True)


def unit_scale(blocks):
    largest = diagonal_of(blocks[0])
    for x in blocks[1:]:
        largest = jnp.maximum(largest, diagonal_of(x))
    return 1.0 / jnp.max(largest, keepdims=True)


def leading_spaces(grams, scale, work, careful, sound_ref):
    for gram, (gram_ref, imaged_ref, _) in zip(grams, work):
        gram_ref[...] = gram * scale
        imaged_ref[...] = gram_ref[:, :RANK]
    count = jnp.where(careful, SWEEPS, 1)

    def sweep(step, carry):
        @pl.when(jnp.logical_not(careful))
        def _():
            images = [imaged_ref[...] for _, imaged_ref, _ in work]
            for again in range(SWEEPS - 1):
                images = [dot_split(gram_ref[...], x, 1, 0) for x, (gram_ref, _, _) in zip(images, work)]
            for x, (_, imaged_ref, _) in zip(images, work):
                imaged_ref[...] = x

        inners = [dot(imaged_ref[...], imaged_ref[...], 0, 0) for _, imaged_ref, _ in work]
        for inner, (factor, pivots), (_, imaged_ref, frame_ref) in zip(inners, inverse_factors(inners), work):
            frame_ref[...] = dot(imaged_ref[...], factor, 1, 1)
            sound_ref[...] = jnp.where(pivots > PIVOT_SHARE * diagonal_of(inner), sound_ref[...], 0.0)

        @pl.when(step + 1 < count)
        def _():
            for gram_ref, imaged_ref, frame_ref in work:
                imaged_ref[...] = dot(gram_ref[...], frame_ref[...], 1, 0)

        return carry

    lax.fori_loop(0, count, sweep, 0)
    return [frame_ref[...].astype(bf16) for _, _, frame_ref in work]


def until_sound(sound_ref, attempt):
    def once(mode):
        sound_ref[...] = jnp.ones(sound_ref.shape, f32)
        attempt(mode == 1)
        sound = jnp.min(sound_ref[...]) > 0.5
        return jnp.where(jnp.logical_or(mode == 1, sound), 2, 1)

    lax.while_loop(lambda mode: mode < 2, once, jnp.int32(0))


sound_shape = [pltpu.VMEM((RANK, RANK), f32)]
work_shapes = [pltpu.VMEM((2 * RANK, 2 * RANK), f32)] + [pltpu.VMEM((2 * RANK, RANK), f32)] * 2


def place(pos_ref):
    pos = pos_ref[0]
    return pos % 2, pos // PLANE % PLANES


def split(blocks, core, mine_ref, theirs_ref):
    half = mine_ref.shape[1]
    for b, block in enumerate(blocks):
        low, high = block[:half, :], block[half:, :]
        mine_ref[b] = jnp.where(core == 1, high, low)
        theirs_ref[b] = jnp.where(core == 1, low, high)


def joined(mine_ref, other_ref, core, b):
    mine, other = mine_ref[b], other_ref[b]
    low = jnp.where(core == 1, other, mine)
    high = jnp.where(core == 1, mine, other)
    return jnp.concatenate([low, high], 0)


def chunk(z, m, width):
    return pl.ds(pl.multiple_of((z ^ m) * width, width), width)


def member(pos_ref):
    return pos_ref[0] % PLANE


def parts_kernel(pos_ref, x_ref, *refs):
    width = refs[0].shape[1]
    for ref, m in zip(refs, PLANE_ORDER):
        ref[...] = x_ref[:, chunk(member(pos_ref), m, width)]


def gram_kernel(pos_ref, *refs):
    parts, (rows_ref, mine_ref, theirs_ref) = refs[:PLANE], refs[PLANE:]
    core, _ = place(pos_ref)
    height = parts[0].shape[0]
    for ref, m in zip(parts, PLANE_ORDER):
        rows_ref[chunk(member(pos_ref), m, height), :] = ref[...]
    rows = rows_ref[...]
    gram = dot_low(rows, rows, 1, 1)
    split([gram[:RANK, :RANK], gram[RANK:, :RANK], gram[RANK:, RANK:]], core, mine_ref, theirs_ref)


def square(a, b, d):
    return jnp.concatenate([jnp.concatenate([a, b.T], 1), jnp.concatenate([b, d], 1)], 0)


def plane_gram(mine_ref, other_ref, core):
    return square(*[joined(mine_ref, other_ref, core, b) for b in range(3)])


def node_kernel(pos_ref, mine_ref, other_ref, rows_ref, *refs):
    nodes, low_ref, sound_ref, work = refs[:PLANES], refs[PLANES], refs[PLANES + 1], refs[PLANES + 2 :]
    core, z = place(pos_ref)
    width = nodes[0].shape[1]

    def attempt(careful):
        gram = plane_gram(mine_ref, other_ref, core)
        scale = unit_scale([gram[:RANK, :RANK], gram[RANK:, RANK:]])
        (low,) = leading_spaces([gram], scale, [work], careful, sound_ref)
        low_ref[...] = low
        for ref, m in zip(nodes, TREE_ORDER):
            ref[...] = dot_low(low, rows_ref[:, chunk(z, m, width)], 0, 0).astype(bf16)

    until_sound(sound_ref, attempt)


def reduced(gram, low):
    return dot_split(low, dot_split(gram, low, 1, 0), 0, 0)


def diag_kernel(pos_ref, mine_ref, other_ref, low_ref, diag_ref):
    core, _ = place(pos_ref)
    diag = reduced(plane_gram(mine_ref, other_ref, core), low_ref[...])
    half = diag_ref.shape[1]
    diag_ref[0] = jnp.where(core == 1, diag[half:, :], diag[:half, :]).astype(diag_ref.dtype)


PAIRS = [(i, j) for i in range(PLANES) for j in range(i + 1, PLANES)]


def cross_kernel(pos_ref, *refs):
    nodes, (mine_ref, theirs_ref, all_ref) = refs[:PLANES], refs[PLANES:]
    core, z = place(pos_ref)
    for ref, m in zip(nodes, TREE_ORDER):
        all_ref[z ^ m] = ref[...]
    split([dot_low(all_ref[j], all_ref[i], 1, 1) for i, j in PAIRS], core, mine_ref, theirs_ref)


def top_kernel(pos_ref, mine_ref, other_ref, *refs):
    nodes, (top_ref, gram_ref, low_ref), refs = refs[:PLANES], refs[PLANES : PLANES + 3], refs[PLANES + 3 :]
    all_ref, diag_ref, sound_ref, work = refs[0], refs[1], refs[2], [refs[3:6], refs[6:9]]
    core, z = place(pos_ref)
    for ref, m in zip(nodes, TREE_ORDER):
        all_ref[z ^ m] = ref[...]
        diag_ref[z ^ m] = joined(mine_ref, other_ref, core, len(PAIRS) + SUM_ORDER.index(m))

    def attempt(careful):
        cross = {pair: joined(mine_ref, other_ref, core, b) for b, pair in enumerate(PAIRS)}
        scale = unit_scale([diag_ref[y] for y in range(PLANES)])
        grams = [square(diag_ref[i], cross[i, j], diag_ref[j]) for i, j in ((0, 1), (2, 3))]
        low_a, low_b = leading_spaces(grams, scale, work, careful, sound_ref)
        between = jnp.concatenate(
            [
                jnp.concatenate([cross[0, 2], cross[1, 2]], 1),
                jnp.concatenate([cross[0, 3], cross[1, 3]], 1),
            ],
            0,
        )
        gram = square(
            reduced(grams[0], low_a),
            dot_split(low_b, dot_split(between, low_a, 1, 0), 0, 0),
            reduced(grams[1], low_b),
        )
        gram_ref[...] = gram
        node_a = dot_low(low_a, jnp.concatenate([all_ref[0], all_ref[1]], 0), 0, 0).astype(bf16)
        node_b = dot_low(low_b, jnp.concatenate([all_ref[2], all_ref[3]], 0), 0, 0).astype(bf16)
        (low,) = leading_spaces([gram], scale, work[:1], careful, sound_ref)
        low_ref[...] = low
        top_ref[...] = dot_low(low, jnp.concatenate([node_a, node_b], 0), 0, 0).astype(bf16)

    until_sound(sound_ref, attempt)


def factor_kernel(gram_ref, low_ref, factor_ref):
    factor_ref[...] = inverse_factors([reduced(gram_ref[...], low_ref[...])])[0][0]


def coeffs_kernel(pos_ref, rows_ref, factor_ref, *refs):
    tops, (mine_ref, theirs_ref) = refs[:PLANES], refs[PLANES:]
    core, z = place(pos_ref)
    width = tops[0].shape[1]
    total = None
    for m, ref in zip(SUM_ORDER, tops):
        part = dot_low(rows_ref[:, chunk(z, m, width)], ref[...], 1, 1)
        total = part if total is None else total + part
    split([dot(total, factor_ref[...], 1, 1)], core, mine_ref, theirs_ref)


def project_kernel(pos_ref, mine_ref, other_ref, factor_ref, *refs):
    tops, outs, solved_ref = refs[:PLANES], refs[PLANES:-1], refs[-1]
    core, z = place(pos_ref)
    height, width = outs[0].shape[0], tops[0].shape[1]
    solved_ref[...] = dot(joined(mine_ref, other_ref, core, 0), factor_ref[...], 1, 0)
    solved = [solved_ref[chunk(member(pos_ref), m, height), :] for m in PLANE_ORDER]
    solved = jnp.concatenate(solved, 0).astype(bf16)
    for m, ref in zip(SUM_ORDER, tops):
        made = dot_low(solved, ref[...], 1, 0).astype(bf16)
        for k in range(PLANE):
            outs[k][:, chunk(z, m, width)] = made[k * height : (k + 1) * height, :]


def whole_kernel(pos_ref, *refs):
    parts, out_ref = refs[:PLANE], refs[PLANE]
    width = parts[0].shape[1]
    for ref, m in zip(parts, PLANE_ORDER):
        out_ref[:, chunk(member(pos_ref), m, width)] = ref[...]


smem = pl.BlockSpec(memory_space=pltpu.SMEM)
vmem = pl.BlockSpec(memory_space=pltpu.VMEM)


def kernel(fn, outs, *args, scratch=(), scalar=True):
    single = not isinstance(outs, (list, tuple))
    shapes = [outs] if single else list(outs)
    res = pl.pallas_call(
        fn,
        out_shape=[jax.ShapeDtypeStruct(s, d) for s, d in shapes] if not single else None,
        in_specs=[smem if scalar and i == 0 else vmem for i in range(len(args))],
        out_specs=[vmem for _ in shapes],
        scratch_shapes=list(scratch),
        compiler_params=pltpu.CompilerParams(vmem_limit_bytes=40 * 2**20),
        name=fn.__name__,
    )(*args)
    return res


def body(mortality):
    count = lax.axis_size("cols")
    pos = lax.axis_index("cols").astype(jnp.int32).reshape(1)

    def swap(x, apart):
        return lax.ppermute(x, "cols", [(i, i ^ apart) for i in range(count)])

    def swap_all(parts, order, unit=1):
        return [x if m == 0 else swap(x, unit * m) for x, m in zip(parts, order)]

    def sum4(parts):
        parts = [p.astype(f32) for p in parts]
        return (parts[0] + parts[1]) + (parts[2] + parts[3])

    def plane_sum(mine, theirs):
        return sum4(swap_all([(mine + swap(theirs, 1)).astype(bf16)] * 4, range(4), 2))

    block, total = mortality.shape
    height, width = block * PLANE, total // PLANE
    part = width // PLANES
    half = RANK // 2

    parts = kernel(parts_kernel, [((block, width), bf16)] * PLANE, pos, mortality)
    parts = swap_all(parts, PLANE_ORDER)
    rows, mine, theirs = kernel(
        gram_kernel, [((height, width), bf16)] + [((3, half, RANK), f32)] * 2, pos, *parts
    )
    mine = plane_sum(mine, theirs)
    other = swap(mine, 1)
    *nodes, low = kernel(
        node_kernel,
        [((RANK, part), bf16)] * PLANES + [((2 * RANK, RANK), bf16)],
        pos, mine, other, rows,
        scratch=sound_shape + work_shapes,
    )
    nodes = swap_all(nodes, TREE_ORDER, PLANE)
    (diag,) = kernel(diag_kernel, [((1, half, RANK), bf16)], pos, mine, other, low)

    mine, theirs = kernel(
        cross_kernel,
        [((len(PAIRS), half, RANK), f32)] * 2,
        pos, *nodes,
        scratch=[pltpu.VMEM((PLANES, RANK, part), bf16)],
    )
    mine = plane_sum(mine, theirs)
    both = swap_all([jnp.concatenate([mine.astype(bf16), diag], 0)] * PLANES, SUM_ORDER, PLANE)
    mine = jnp.concatenate([sum4([x[: len(PAIRS)] for x in both])] + [x[len(PAIRS) :].astype(f32) for x in both], 0)
    top, gram, low = kernel(
        top_kernel,
        [((RANK, part), bf16), ((2 * RANK, 2 * RANK), f32), ((2 * RANK, RANK), bf16)],
        pos, mine, swap(mine, 1), *nodes,
        scratch=[pltpu.VMEM((PLANES, RANK, part), bf16), pltpu.VMEM((PLANES, RANK, RANK), f32)]
        + sound_shape
        + work_shapes * 2,
    )
    tops = swap_all([top] * PLANES, SUM_ORDER, PLANE)
    (factor,) = kernel(factor_kernel, [((RANK, RANK), f32)], gram, low, scalar=False)

    mine, theirs = kernel(coeffs_kernel, [((1, height // 2, RANK), f32)] * 2, pos, rows, factor, *tops)
    mine = plane_sum(mine, theirs)
    outs = kernel(
        project_kernel,
        [((block, width), bf16)] * PLANE,
        pos, mine, swap(mine, 1), factor, *tops,
        scratch=[pltpu.VMEM((height, RANK), f32)],
    )
    (result,) = kernel(whole_kernel, [((block, total), bf16)], pos, *swap_all(outs, PLANE_ORDER))
    return result


def solution(mesh):
    in_specs = (P("cols", None),)
    out_specs = P("cols", None)
    return jax.shard_map(body, mesh=mesh, in_specs=in_specs, out_specs=out_specs, check_vma=False)
```

```python
import jax
import jax.numpy as jnp
from jax import lax
from jax.experimental import pallas as pl
from jax.experimental.pallas import tpu as pltpu
from jax.sharding import PartitionSpec as P

RANK = 128
LEVELS = 5
SWEEPS = 3
PLANE = 8
PLANES = 2**LEVELS // PLANE
TILE = 8
PANEL = 64
PLANE_ORDER = (0, 6, 7, 2, 4, 3, 5, 1)
TREE_ORDER = (0, 2, 3, 1)
SUM_ORDER = (0, 1, 3, 2)
PIVOT_SHARE = 2e-4

precise = lax.Precision.HIGHEST
f32 = jnp.float32
bf16 = jnp.bfloat16


def iota2(shape, dim):
    return lax.broadcasted_iota(jnp.int32, shape, dim)


def dot(a, b, ca, cb, precision=precise):
    return lax.dot_general(a, b, (((ca,), (cb,)), ((), ())), precision=precision, preferred_element_type=f32)


def dot_low(a, b, ca, cb):
    return dot(a, b, ca, cb, None)


def halves(x):
    high = x.astype(bf16)
    return high, (x - high.astype(f32)).astype(bf16)


def dot_split(a, b, ca, cb):
    ah, al = (a, None) if a.dtype == bf16 else halves(a)
    bh, bl = (b, None) if b.dtype == bf16 else halves(b)
    total = dot_low(ah, bh, ca, cb)
    if bl is not None:
        total = total + dot_low(ah, bl, ca, cb)
    return total if al is None else total + dot_low(al, bh, ca, cb)


def lanes_of(x, k):
    return jnp.broadcast_to(x[:, k : k + 1], x.shape)


def rows_of(x, s):
    return jnp.broadcast_to(x[s : s + 1, :], x.shape)


def eliminate(sets, first, ahead):
    lane = iota2((TILE, RANK), 1)
    sub = iota2((TILE, RANK), 0)
    count = len(sets[0])
    early = [None] * len(sets)
    pivots = [[] for _ in sets]
    for t in range(count):
        g = TILE * (first + t)
        spread, coming = [], []
        for n, tiles in enumerate(sets):
            cols = {} if early[n] is None else {t: early[n]}
            for i in range(t + len(cols), count):
                cols[i] = [lanes_of(tiles[i], g + j) for j in range(TILE)]
            spread.append(cols)
            near = (t, t + 1) if ahead and t + 1 < count else ()
            coming.append({i: [lanes_of(tiles[i], g + TILE + j) for j in range(TILE)] for i in near})
            pivots[n].append(jnp.zeros((TILE, RANK), f32))
        for k in range(TILE):
            here = lane == g + k
            for tiles, cols, look, held in zip(sets, spread, coming, pivots):
                pivot_row = [rows_of(cols[t][j], k) if j >= k else None for j in range(TILE)]
                held[t] = jnp.where(sub == k, pivot_row[k], held[t])
                inv = 1.0 / pivot_row[k]
                scaled = [pivot_row[j] * inv if j > k else None for j in range(TILE)]
                row = jnp.where(here, 1.0, rows_of(tiles[t], k)) * inv
                look_row = [rows_of(x, k) * inv for x in look[t]] if look else None
                for i in range(t, count):
                    col = cols[i][k]
                    if i == t:
                        col = jnp.where(sub > k, col, 0.0)
                        kept = jnp.where(here & (sub > k), 0.0, tiles[i])
                    else:
                        kept = jnp.where(here, 0.0, tiles[i])
                    for j in range(k + 1, TILE):
                        cols[i][j] = cols[i][j] - col * scaled[j]
                    tiles[i] = kept - col * row
                    if i in look:
                        look[i] = [x - col * y for x, y in zip(look[i], look_row)]
        early = [look.get(t + 1) for look in coming]
    return list(zip(sets, pivots))


def inverse_factors(matrices):
    alone = len(matrices) == 1
    size = PANEL if alone else PANEL // 2
    rests = list(matrices)
    done = [[] for _ in rests]
    for lo in range(0, RANK, size):
        hi = lo + size
        sets = [[rest[TILE * t : TILE * t + TILE, :] for t in range(size // TILE)] for rest in rests]
        r = iota2((size, RANK), 0) + lo
        c = iota2((size, RANK), 1)
        for n, (tiles, pivots) in enumerate(eliminate(sets, lo // TILE, alone)):
            panel = jnp.concatenate(tiles, 0)
            pivots = jnp.concatenate(pivots, 0)
            unit = jnp.where(r > c, panel, jnp.where(r == c, 1.0, 0.0))
            done[n].append((unit * lax.rsqrt(pivots), pivots))
            if hi == RANK:
                continue
            rows = jnp.where(r == c, 1.0, jnp.where((c > r) & (c < hi), 0.0, panel))
            tail = rests[n][size:, :]
            at = iota2(tail.shape, 1)
            tail = jnp.where((at >= lo) & (at < hi), 0.0, tail)
            rests[n] = tail - dot(panel * (1.0 / pivots), rows, 0, 0)[hi:, :]
    return [tuple(jnp.concatenate(x, 0) for x in zip(*panels)) for panels in done]


def diagonal_of(x):
    return jnp.sum(jnp.where(iota2(x.shape, 0) == iota2(x.shape, 1), x, 0.0), 1, keepdims=True)


def unit_scale(blocks):
    largest = diagonal_of(blocks[0])
    for x in blocks[1:]:
        largest = jnp.maximum(largest, diagonal_of(x))
    return 1.0 / jnp.max(largest, keepdims=True)


def leading_spaces(grams, scale, work, careful, sound_ref):
    for gram, (gram_ref, imaged_ref, _) in zip(grams, work):
        gram_ref[...] = gram * scale
        imaged_ref[...] = gram_ref[:, :RANK]
    count = jnp.where(careful, SWEEPS, 1)

    def sweep(step, carry):
        @pl.when(jnp.logical_not(careful))
        def _():
            images = [imaged_ref[...] for _, imaged_ref, _ in work]
            for again in range(SWEEPS - 1):
                images = [dot_split(gram_ref[...], x, 1, 0) for x, (gram_ref, _, _) in zip(images, work)]
            for x, (_, imaged_ref, _) in zip(images, work):
                imaged_ref[...] = x

        inners = [dot(imaged_ref[...], imaged_ref[...], 0, 0) for _, imaged_ref, _ in work]
        for inner, (factor, pivots), (_, imaged_ref, frame_ref) in zip(inners, inverse_factors(inners), work):
            frame_ref[...] = dot(imaged_ref[...], factor, 1, 1)
            sound_ref[...] = jnp.where(pivots > PIVOT_SHARE * diagonal_of(inner), sound_ref[...], 0.0)

        @pl.when(step + 1 < count)
        def _():
            for gram_ref, imaged_ref, frame_ref in work:
                imaged_ref[...] = dot(gram_ref[...], frame_ref[...], 1, 0)

        return carry

    lax.fori_loop(0, count, sweep, 0)
    return [frame_ref[...].astype(bf16) for _, _, frame_ref in work]


def until_sound(sound_ref, attempt):
    def once(mode):
        sound_ref[...] = jnp.ones(sound_ref.shape, f32)
        attempt(mode == 1)
        sound = jnp.min(sound_ref[...]) > 0.5
        return jnp.where(jnp.logical_or(mode == 1, sound), 2, 1)

    lax.while_loop(lambda mode: mode < 2, once, jnp.int32(0))


sound_shape = [pltpu.VMEM((RANK, RANK), f32)]
work_shapes = [pltpu.VMEM((2 * RANK, 2 * RANK), f32)] + [pltpu.VMEM((2 * RANK, RANK), f32)] * 2


def place(pos_ref):
    pos = pos_ref[0]
    return pos % 2, pos // PLANE % PLANES


def split(blocks, core, mine_ref, theirs_ref):
    half = mine_ref.shape[1]
    for b, block in enumerate(blocks):
        low, high = block[:half, :], block[half:, :]
        mine_ref[b] = jnp.where(core == 1, high, low)
        theirs_ref[b] = jnp.where(core == 1, low, high)


def joined(mine_ref, other_ref, core, b):
    mine, other = mine_ref[b], other_ref[b]
    low = jnp.where(core == 1, other, mine)
    high = jnp.where(core == 1, mine, other)
    return jnp.concatenate([low, high], 0)


def chunk(z, m, width):
    return pl.ds(pl.multiple_of((z ^ m) * width, width), width)


def member(pos_ref):
    return pos_ref[0] % PLANE


def parts_kernel(pos_ref, x_ref, *refs):
    width = refs[0].shape[1]
    for ref, m in zip(refs, PLANE_ORDER):
        ref[...] = x_ref[:, chunk(member(pos_ref), m, width)]


def gram_kernel(pos_ref, *refs):
    parts, (rows_ref, mine_ref, theirs_ref) = refs[:PLANE], refs[PLANE:]
    core, _ = place(pos_ref)
    height = parts[0].shape[0]
    for ref, m in zip(parts, PLANE_ORDER):
        rows_ref[chunk(member(pos_ref), m, height), :] = ref[...]
    rows = rows_ref[...]
    gram = dot_low(rows, rows, 1, 1)
    split([gram[:RANK, :RANK], gram[RANK:, :RANK], gram[RANK:, RANK:]], core, mine_ref, theirs_ref)


def square(a, b, d):
    return jnp.concatenate([jnp.concatenate([a, b.T], 1), jnp.concatenate([b, d], 1)], 0)


def plane_gram(mine_ref, other_ref, core):
    return square(*[joined(mine_ref, other_ref, core, b) for b in range(3)])


def node_kernel(pos_ref, mine_ref, other_ref, rows_ref, *refs):
    nodes, low_ref, sound_ref, work = refs[:PLANES], refs[PLANES], refs[PLANES + 1], refs[PLANES + 2 :]
    core, z = place(pos_ref)
    width = nodes[0].shape[1]

    def attempt(careful):
        gram = plane_gram(mine_ref, other_ref, core)
        scale = unit_scale([gram[:RANK, :RANK], gram[RANK:, RANK:]])
        (low,) = leading_spaces([gram], scale, [work], careful, sound_ref)
        low_ref[...] = low
        for ref, m in zip(nodes, TREE_ORDER):
            ref[...] = dot_low(low, rows_ref[:, chunk(z, m, width)], 0, 0).astype(bf16)

    until_sound(sound_ref, attempt)


def reduced(gram, low):
    return dot_split(low, dot_split(gram, low, 1, 0), 0, 0)


def diag_kernel(pos_ref, mine_ref, other_ref, low_ref, diag_ref):
    core, _ = place(pos_ref)
    diag = reduced(plane_gram(mine_ref, other_ref, core), low_ref[...])
    half = diag_ref.shape[1]
    diag_ref[0] = jnp.where(core == 1, diag[half:, :], diag[:half, :]).astype(diag_ref.dtype)


PAIRS = [(i, j) for i in range(PLANES) for j in range(i + 1, PLANES)]


def cross_kernel(pos_ref, *refs):
    nodes, (mine_ref, theirs_ref, all_ref) = refs[:PLANES], refs[PLANES:]
    core, z = place(pos_ref)
    for ref, m in zip(nodes, TREE_ORDER):
        all_ref[z ^ m] = ref[...]
    split([dot_low(all_ref[j], all_ref[i], 1, 1) for i, j in PAIRS], core, mine_ref, theirs_ref)


def top_kernel(pos_ref, mine_ref, other_ref, *refs):
    nodes, (top_ref, gram_ref, low_ref), refs = refs[:PLANES], refs[PLANES : PLANES + 3], refs[PLANES + 3 :]
    all_ref, diag_ref, sound_ref, work = refs[0], refs[1], refs[2], [refs[3:6], refs[6:9]]
    core, z = place(pos_ref)
    for ref, m in zip(nodes, TREE_ORDER):
        all_ref[z ^ m] = ref[...]
        diag_ref[z ^ m] = joined(mine_ref, other_ref, core, len(PAIRS) + SUM_ORDER.index(m))

    def attempt(careful):
        cross = {pair: joined(mine_ref, other_ref, core, b) for b, pair in enumerate(PAIRS)}
        scale = unit_scale([diag_ref[y] for y in range(PLANES)])
        grams = [square(diag_ref[i], cross[i, j], diag_ref[j]) for i, j in ((0, 1), (2, 3))]
        low_a, low_b = leading_spaces(grams, scale, work, careful, sound_ref)
        between = jnp.concatenate(
            [
                jnp.concatenate([cross[0, 2], cross[1, 2]], 1),
                jnp.concatenate([cross[0, 3], cross[1, 3]], 1),
            ],
            0,
        )
        gram = square(
            reduced(grams[0], low_a),
            dot_split(low_b, dot_split(between, low_a, 1, 0), 0, 0),
            reduced(grams[1], low_b),
        )
        gram_ref[...] = gram
        node_a = dot_low(low_a, jnp.concatenate([all_ref[0], all_ref[1]], 0), 0, 0).astype(bf16)
        node_b = dot_low(low_b, jnp.concatenate([all_ref[2], all_ref[3]], 0), 0, 0).astype(bf16)
        (low,) = leading_spaces([gram], scale, work[:1], careful, sound_ref)
        low_ref[...] = low
        top_ref[...] = dot_low(low, jnp.concatenate([node_a, node_b], 0), 0, 0).astype(bf16)

    until_sound(sound_ref, attempt)


def factor_kernel(gram_ref, low_ref, factor_ref):
    factor_ref[...] = inverse_factors([reduced(gram_ref[...], low_ref[...])])[0][0]


def coeffs_kernel(pos_ref, rows_ref, factor_ref, *refs):
    tops, (mine_ref, theirs_ref) = refs[:PLANES], refs[PLANES:]
    core, z = place(pos_ref)
    width = tops[0].shape[1]
    total = None
    for m, ref in zip(SUM_ORDER, tops):
        part = dot_low(rows_ref[:, chunk(z, m, width)], ref[...], 1, 1)
        total = part if total is None else total + part
    split([dot(total, factor_ref[...], 1, 1)], core, mine_ref, theirs_ref)


def project_kernel(pos_ref, mine_ref, other_ref, factor_ref, *refs):
    tops, outs, solved_ref = refs[:PLANES], refs[PLANES:-1], refs[-1]
    core, z = place(pos_ref)
    height, width = outs[0].shape[0], tops[0].shape[1]
    solved_ref[...] = dot(joined(mine_ref, other_ref, core, 0), factor_ref[...], 1, 0)
    solved = [solved_ref[chunk(member(pos_ref), m, height), :] for m in PLANE_ORDER]
    solved = jnp.concatenate(solved, 0).astype(bf16)
    for m, ref in zip(SUM_ORDER, tops):
        made = dot_low(solved, ref[...], 1, 0).astype(bf16)
        for k in range(PLANE):
            outs[k][:, chunk(z, m, width)] = made[k * height : (k + 1) * height, :]


def whole_kernel(pos_ref, *refs):
    parts, out_ref = refs[:PLANE], refs[PLANE]
    width = parts[0].shape[1]
    for ref, m in zip(parts, PLANE_ORDER):
        out_ref[:, chunk(member(pos_ref), m, width)] = ref[...]


smem = pl.BlockSpec(memory_space=pltpu.SMEM)
vmem = pl.BlockSpec(memory_space=pltpu.VMEM)


def kernel(fn, outs, *args, scratch=(), scalar=True):
    single = not isinstance(outs, (list, tuple))
    shapes = [outs] if single else list(outs)
    res = pl.pallas_call(
        fn,
        out_shape=[jax.ShapeDtypeStruct(s, d) for s, d in shapes] if not single else None,
        in_specs=[smem if scalar and i == 0 else vmem for i in range(len(args))],
        out_specs=[vmem for _ in shapes],
        scratch_shapes=list(scratch),
        compiler_params=pltpu.CompilerParams(vmem_limit_bytes=40 * 2**20),
        name=fn.__name__,
    )(*args)
    return res


def body(mortality):
    count = lax.axis_size("cols")
    pos = lax.axis_index("cols").astype(jnp.int32).reshape(1)

    def swap(x, apart):
        return lax.ppermute(x, "cols", [(i, i ^ apart) for i in range(count)])

    def swap_all(parts, order, unit=1):
        return [x if m == 0 else swap(x, unit * m) for x, m in zip(parts, order)]

    def sum4(parts):
        parts = [p.astype(f32) for p in parts]
        return (parts[0] + parts[1]) + (parts[2] + parts[3])

    def plane_sum(mine, theirs):
        return sum4(swap_all([(mine + swap(theirs, 1)).astype(bf16)] * 4, (0, 3, 2, 1), 2))

    block, total = mortality.shape
    height, width = block * PLANE, total // PLANE
    part = width // PLANES
    half = RANK // 2

    parts = kernel(parts_kernel, [((block, width), bf16)] * PLANE, pos, mortality)
    parts = swap_all(parts, PLANE_ORDER)
    rows, mine, theirs = kernel(
        gram_kernel, [((height, width), bf16)] + [((3, half, RANK), f32)] * 2, pos, *parts
    )
    mine = plane_sum(mine, theirs)
    other = swap(mine, 1)
    *nodes, low = kernel(
        node_kernel,
        [((RANK, part), bf16)] * PLANES + [((2 * RANK, RANK), bf16)],
        pos, mine, other, rows,
        scratch=sound_shape + work_shapes,
    )
    nodes = swap_all(nodes, TREE_ORDER, PLANE)
    (diag,) = kernel(diag_kernel, [((1, half, RANK), bf16)], pos, mine, other, low)

    mine, theirs = kernel(
        cross_kernel,
        [((len(PAIRS), half, RANK), f32)] * 2,
        pos, *nodes,
        scratch=[pltpu.VMEM((PLANES, RANK, part), bf16)],
    )
    mine = plane_sum(mine, theirs)
    both = swap_all([jnp.concatenate([mine.astype(bf16), diag], 0)] * PLANES, SUM_ORDER, PLANE)
    mine = jnp.concatenate([sum4([x[: len(PAIRS)] for x in both])] + [x[len(PAIRS) :].astype(f32) for x in both], 0)
    top, gram, low = kernel(
        top_kernel,
        [((RANK, part), bf16), ((2 * RANK, 2 * RANK), f32), ((2 * RANK, RANK), bf16)],
        pos, mine, swap(mine, 1), *nodes,
        scratch=[pltpu.VMEM((PLANES, RANK, part), bf16), pltpu.VMEM((PLANES, RANK, RANK), f32)]
        + sound_shape
        + work_shapes * 2,
    )
    tops = swap_all([top] * PLANES, SUM_ORDER, PLANE)
    (factor,) = kernel(factor_kernel, [((RANK, RANK), f32)], gram, low, scalar=False)

    mine, theirs = kernel(coeffs_kernel, [((1, height // 2, RANK), f32)] * 2, pos, rows, factor, *tops)
    mine = plane_sum(mine, theirs)
    outs = kernel(
        project_kernel,
        [((block, width), bf16)] * PLANE,
        pos, mine, swap(mine, 1), factor, *tops,
        scratch=[pltpu.VMEM((height, RANK), f32)],
    )
    (result,) = kernel(whole_kernel, [((block, total), bf16)], pos, *swap_all(outs, PLANE_ORDER))
    return result


def solution(mesh):
    in_specs = (P("cols", None),)
    out_specs = P("cols", None)
    return jax.shard_map(body, mesh=mesh, in_specs=in_specs, out_specs=out_specs, check_vma=False)
```
